32 devices in a mesh: tm: 4 (over x, core), space: 8 (over z, y).
Axes of the slice: x: 2, y: 2, z: 4, core: 2. Of those that a mesh axis runs over, the one named last changes fastest.
Arguments:
- state: bfloat16 [24, 16, 8, 8, 128], P('tm', None, 'space'), may hold values from -6 to 6
- noise: bfloat16 [24, 16, 8, 8, 128], P('tm', None, 'space'), may hold values from -6 to 6
- conv_one: bfloat16 [64, 16, 3, 3, 3], replicated, may hold values from -0.3125 to 0.3125
- bias_one: float32 [64], replicated, may hold values from -3 to 3
- conv_two: bfloat16 [64, 64, 3, 3, 3], replicated, may hold values from -0.15625 to 0.15625
- bias_two: float32 [64], replicated, may hold values from -3 to 3
- conv_three: bfloat16 [16, 64, 3, 3, 3], replicated, may hold values from -0.15625 to 0.15625
- bias_three: float32 [16], replicated, may hold values from -3 to 3
- day_of_frame: int32 [24], P('tm'), may hold values from 0 to 1, never falling along the last dimension, each value on 1 to 23 neighbouring positions
- observed: float32 [2, 8, 8, 128], P(None, 'space'), may hold values from -18 to 18
- obs_mask: int32 [8, 8, 128], P('space'), may hold values 0 or 1
Outputs:
- updated: bfloat16 [24, 16, 8, 8, 128], P('tm', None, 'space')
The draws below stay inside these ranges and needn't reach their ends.
Inputs may be any that keep to these rules, and one draw needn't show every extreme that they name: `day_of_frame`: frames of one observation period are consecutive and periods never go back; every period has 1 to 23 frames and one has exactly 23.
All inputs are finite; a program needn't handle non-finite values. No bound on the sum of `obs_mask` on one device may be relied on, other than what follows from the above.
Results may differ from the reference program's by a relative error of at most 0.0028.
Values may be sent and summed in bfloat16 or wider, within the bound.
No kernel may reach another device: no remote copies, remote signals or barrier semaphores. Data moves between devices by JAX's collectives and lax.ppermute only.
A program may use at most 64 MiB of HBM per device.

```python
import math
import jax
import jax.numpy as jnp
import numpy as np
from jax import lax

FIELDS = 16
HID = 64
TY = 8
TX = 128
GX = 8
GY = 1
FRAMES = 24
TILES = 8
DAYS = 2
MOST = 23


def place_ends(values, stream_key, low, high):
    longest = values.shape.index(max(values.shape))
    spots = []
    for shift in (0, 1):
        where = [jax.random.randint(jax.random.fold_in(stream_key, axis), (), 0, length) for axis, length in enumerate(values.shape)]
        where[longest] = (where[longest] + shift) % values.shape[longest]
        spots.append(tuple(where))
    return values.at[spots[0]].set(low).at[spots[1]].set(high)


def block_scale(stream_key, dims, split, smallest, high):
    def one(position, shards_of):
        heights = jax.random.uniform(jax.random.fold_in(jax.random.fold_in(stream_key, 6), position), (shards_of,), jnp.float32, smallest / len(split), high / len(split))
        return jnp.repeat(jnp.exp(heights), dims[position] // shards_of).reshape((-1,) + (1,) * (len(dims) - position - 1))

    factor_of = one(*split[0])
    for cut in split[1:]:
        factor_of = factor_of * one(*cut)
    return factor_of


def profile(amount, total, bound, skew):
    loads = [(1 << 20) // math.isqrt(grade ** skew) + 1 for grade in range(2, amount + 1)]
    rest, counts = total - bound - (amount - 1), [1] * (amount - 1)
    while rest > 0:
        free = [i for i in range(amount - 1) if counts[i] < bound]
        mass, remaining = sum([loads[i] for i in free]), rest
        for i in free:
            more = min(bound - counts[i], max(1, remaining * loads[i] // mass), rest)
            counts[i] = counts[i] + more
            rest = rest - more
    return np.array([bound] + counts)


def ragged_sizes(stream_key, count, total, most, lean):
    if count == 2:
        one = jax.random.randint(stream_key, (), max(1, total - most), min(most, total - 1) + 1)
        return jnp.stack([one, total - one])
    sizes = jnp.asarray(profile(count, total, most, lean), jnp.int32)
    couples = (count - 1) // 2
    donor, taker = sizes[1:1 + 2 * couples:2], sizes[2:2 + 2 * couples:2]
    room = jnp.minimum(donor - 1, most - taker)
    shifted = jax.random.randint(jax.random.fold_in(stream_key, 1), (couples,), 0, 1 << 20) % (room + 1)
    sizes = sizes.at[1:1 + 2 * couples:2].set(donor - shifted).at[2:2 + 2 * couples:2].set(taker + shifted)
    return sizes[jax.random.permutation(jax.random.fold_in(stream_key, 2), count)]


def centred(stream_key, shape, spread, bound, pieces=(), kind=jnp.bfloat16):
    values = spread * jax.random.normal(stream_key, shape, jnp.float32)
    if pieces:
        values = values * block_scale(stream_key, shape, pieces, -0.22, 0.18)
    return jnp.clip(values, -bound, bound).astype(kind)


def setup_inputs(seed: int = 0) -> dict:
    arg_keys = jax.random.split(jax.random.key(seed), 12)
    return {
        "state": centred(arg_keys[0], (FRAMES, FIELDS, TILES, TY, TX), 1.0, 6.0, ((0, 4), (2, 8))),
        "noise": centred(arg_keys[1], (FRAMES, FIELDS, TILES, TY, TX), 1.0, 6.0, ((0, 4), (2, 8))),
        "conv_one": centred(arg_keys[2], (HID, FIELDS, 3, 3, 3), (27 * FIELDS) ** -0.5, 0.3125),
        "bias_one": centred(arg_keys[3], (HID,), 0.5, 3.0, (), jnp.float32),
        "conv_two": centred(arg_keys[4], (HID, HID, 3, 3, 3), (27 * HID) ** -0.5, 0.15625),
        "bias_two": centred(arg_keys[5], (HID,), 0.5, 3.0, (), jnp.float32),
        "conv_three": centred(arg_keys[6], (FIELDS, HID, 3, 3, 3), (27 * HID) ** -0.5, 0.15625),
        "bias_three": centred(arg_keys[7], (FIELDS,), 0.5, 3.0, (), jnp.float32),
        "day_of_frame": jnp.searchsorted(jnp.cumsum(ragged_sizes(arg_keys[8], DAYS, FRAMES, MOST, 0)), jnp.arange(FRAMES), side="right").astype(jnp.int32),
        "observed": centred(arg_keys[9], (DAYS, TILES, TY, TX), 3.0, 18.0, ((1, 8),), jnp.float32),
        "obs_mask": place_ends((jax.random.randint(arg_keys[10], (TILES, TY, TX), 0, 4) < 3).astype(jnp.int32), jax.random.fold_in(arg_keys[10], 1), 0, 1),
    }


def to_grid(tiled):
    lead, chans = tiled.shape[0], tiled.shape[1]
    shaped = tiled.reshape(lead, chans, GY, GX, TY, TX)
    return shaped.transpose(0, 1, 2, 4, 3, 5).reshape(lead, chans, GY * TY, GX * TX)


def to_tiles(gridded):
    lead, chans = gridded.shape[0], gridded.shape[1]
    shaped = gridded.reshape(lead, chans, GY, TY, GX, TX)
    return shaped.transpose(0, 1, 2, 4, 3, 5).reshape(lead, chans, GY * GX, TY, TX)


def conv_same(field, kernel):
    out = lax.conv_general_dilated(field[None].astype(jnp.float32), kernel.astype(jnp.float32), (1, 1, 1), ((1, 1), (1, 1), (1, 1)), dimension_numbers=("NDCHW", "OIDHW", "NDCHW"), precision=lax.Precision.HIGHEST)
    return out[0]


def reference(state, noise, conv_one, bias_one, conv_two, bias_two, conv_three, bias_three, day_of_frame, observed, obs_mask):
    grid_state = to_grid(state)
    grid_noise = to_grid(noise)
    hidden_one = jax.nn.silu(conv_same(grid_state, conv_one) + bias_one[None, :, None, None]).astype(jnp.bfloat16)
    hidden_two = jax.nn.silu(conv_same(hidden_one, conv_two) + bias_two[None, :, None, None]).astype(jnp.bfloat16)
    score = conv_same(hidden_two, conv_three) + bias_three[None, :, None, None]
    estimate = grid_state[:, 0].astype(jnp.float32) + 0.5 * score[:, 0]
    frame_count = estimate.shape[0]
    flat_cells = estimate.reshape(frame_count, -1)
    onehot = (day_of_frame[:, None] == jnp.arange(DAYS, dtype=jnp.int32)[None, :]).astype(jnp.float32)
    totals = jnp.dot(onehot.T, flat_cells, precision=lax.Precision.HIGHEST)
    obs_grid = to_grid(observed[:, None]).reshape(DAYS, -1)
    mask_grid = to_grid(obs_mask[None, None].astype(jnp.float32)).reshape(1, -1)
    misfit = mask_grid * (totals - obs_grid)
    per_frame = jnp.dot(onehot, misfit, precision=lax.Precision.HIGHEST).reshape(estimate.shape)
    moved = grid_state.astype(jnp.float32) + 0.8 * score + 0.5 * grid_noise.astype(jnp.float32)
    moved = moved.at[:, 0].add(-0.15 * per_frame)
    return to_tiles(moved).astype(jnp.bfloat16)
```

```python
import functools

import jax
import jax.numpy as jnp
from jax import lax
from jax.experimental import pallas as pl
from jax.experimental.pallas import tpu as pltpu
from jax.sharding import PartitionSpec as P

BF = jnp.bfloat16
F32 = jnp.float32
LANES = 128
DEPTH = 3
PITCH = 16
VMEM = pl.BlockSpec(memory_space=pltpu.VMEM)
SMEM = pl.BlockSpec(memory_space=pltpu.SMEM)
LIMIT = 48 * 1024 * 1024


def params():
    return pltpu.CompilerParams(vmem_limit_bytes=LIMIT)


def silu(v):
    half = 0.5 * v
    return half + half * jnp.tanh(half)


def lanes(shape):
    return lax.broadcasted_iota(jnp.int32, shape, len(shape) - 1)


def turn(v, steps):
    steps = steps % LANES
    if steps == 0:
        return v
    return pltpu.roll(v, steps, 1)


def tile(i):
    return slice(i * LANES, (i + 1) * LANES)


def rows_kernel(state_ref, w1_ref, w2_ref, w3_ref, own_ref, lo_ref, hi_ref, k1_ref, k2_ref, k3_ref, scr):
    frames, chans, rows, _ = state_ref.shape
    for f in range(frames):
        scr[f] = state_ref[f].astype(F32).reshape(chans * rows, LANES)
    for f in range(frames):
        for y in range(rows):
            v = scr[f, pl.ds(y, chans, stride=rows), :].astype(BF)
            own_ref[f, :, tile(y)] = v
            if f < DEPTH:
                lo_ref[f, :, tile(y)] = v
            if f >= frames - DEPTH:
                hi_ref[f - (frames - DEPTH), :, tile(y)] = v
    hid = w2_ref.shape[1]
    k1_ref[...] = w1_ref[...].astype(F32).T.astype(BF)
    for t in range(27):
        k2_ref[:, t * hid : (t + 1) * hid] = w2_ref[t]
        k3_ref[:, t * hid : (t + 1) * hid] = w3_ref[t]


def make_rows(state, w1, w2, w3):
    frames, chans, rows, _ = state.shape
    hid, fields = w2.shape[1], w3.shape[1]
    slab = jax.ShapeDtypeStruct((DEPTH, chans, rows * LANES), BF)
    return pl.pallas_call(
        rows_kernel,
        out_shape=(
            jax.ShapeDtypeStruct((frames, chans, rows * LANES), BF),
            slab,
            slab,
            jax.ShapeDtypeStruct((hid, 27 * chans), BF),
            jax.ShapeDtypeStruct((hid, 27 * hid), BF),
            jax.ShapeDtypeStruct((fields, 27 * hid), BF),
        ),
        in_specs=[VMEM] * 4,
        out_specs=(VMEM,) * 6,
        scratch_shapes=[pltpu.VMEM((frames, chans * rows, LANES), F32)],
        compiler_params=params(),
        name="rows",
    )(state, w1, w2, w3)


def edges_kernel(own_ref, below_ref, above_ref, west_ref, east_ref):
    frames = own_ref.shape[0]
    rows = own_ref.shape[2] // LANES
    shape = (own_ref.shape[1], LANES)
    lane = lanes(shape)
    group, place = lane // PITCH, lane % PITCH
    for f in range(frames + 2 * DEPTH):
        if f < DEPTH:
            src, g = below_ref, f
        elif f < DEPTH + frames:
            src, g = own_ref, f - DEPTH
        else:
            src, g = above_ref, f - DEPTH - frames
        west = jnp.zeros(shape, BF)
        east = jnp.zeros(shape, BF)
        for y in range(rows):
            v = src[g, :, tile(y)]
            here = group == y
            west = jnp.where(here & (place >= DEPTH), turn(v, y * PITCH + DEPTH), west)
            east = jnp.where(here & (place < PITCH - DEPTH), turn(v, y * PITCH + PITCH - DEPTH), east)
        west_ref[f] = west
        east_ref[f] = east


def make_edges(own, below, above):
    frames, chans, _ = own.shape
    strip = jax.ShapeDtypeStruct((frames + 2 * DEPTH, chans, LANES), BF)
    return pl.pallas_call(
        edges_kernel,
        out_shape=(strip, strip),
        in_specs=[VMEM] * 3,
        out_specs=(VMEM,) * 2,
        compiler_params=params(),
        name="edges",
    )(own, below, above)


def spread(dst, f, y, v):
    chans = v.shape[0]
    at = tile(y + 1)
    dst[f, 0:chans, at] = turn(v, 1)
    dst[f, chans : 2 * chans, at] = v
    dst[f, 2 * chans : 3 * chans, at] = turn(v, -1)


def window(src, f, y):
    return jnp.concatenate(
        [src[f + dt, :, (y + dy) * LANES : (y + dy + 2) * LANES] for dt in range(3) for dy in range(3)], axis=0
    )


def in_trajectory(local, frames):
    step = lax.axis_index("tm") * frames + local
    return (step >= 0) & (step < frames * lax.axis_size("tm"))


def main_kernel(own_ref, below_ref, above_ref, k1_ref, k2_ref, k3_ref, b1_ref, b2_ref, score_ref, s1, s2, s3):
    frames = own_ref.shape[0]
    rows = own_ref.shape[2] // LANES
    for s in (s1, s2, s3):
        s[:, :, tile(0)] = jnp.zeros(s.shape[:2] + (LANES,), BF)
        s[:, :, tile(rows + 1)] = jnp.zeros(s.shape[:2] + (LANES,), BF)
    for f in range(frames + 2 * DEPTH):
        if f < DEPTH:
            src, g = below_ref, f
        elif f < DEPTH + frames:
            src, g = own_ref, f - DEPTH
        else:
            src, g = above_ref, f - DEPTH - frames
        for y in range(rows):
            spread(s1, f, y, src[g, :, tile(y)])

    def layer(src, dst, k_ref, b_ref, count, first):
        def step(f, carry):
            keep = in_trajectory(f + first, frames)
            for y in range(0, rows, 2):
                acc = jnp.dot(k_ref[...], window(src, f, y), preferred_element_type=F32)
                h = jnp.where(keep, silu(acc + b_ref[...]), 0.0).astype(BF)
                spread(dst, f, y, h[:, tile(0)])
                spread(dst, f, y + 1, h[:, tile(1)])
            return carry

        lax.fori_loop(0, count, step, 0)

    layer(s1, s2, k1_ref, b1_ref, frames + 4, -2)
    layer(s2, s3, k2_ref, b2_ref, frames + 2, -1)

    def last(f, carry):
        for y in range(0, rows, 2):
            score_ref[f, :, y * LANES : (y + 2) * LANES] = jnp.dot(
                k3_ref[...], window(s3, f, y), preferred_element_type=F32
            )
        return carry

    lax.fori_loop(0, frames, last, 0)


def make_main(own, below, above, k1, k2, k3, b1, b2):
    frames, chans, width = own.shape
    hid, fields = k2.shape[0], k3.shape[0]
    wide = width + 2 * LANES
    return pl.pallas_call(
        main_kernel,
        out_shape=jax.ShapeDtypeStruct((frames, fields, width), F32),
        in_specs=[VMEM] * 8,
        out_specs=VMEM,
        scratch_shapes=[
            pltpu.VMEM((frames + 6, 3 * chans, wide), BF),
            pltpu.VMEM((frames + 4, 3 * hid, wide), BF),
            pltpu.VMEM((frames + 2, 3 * hid, wide), BF),
        ],
        compiler_params=params(),
        cost_estimate=pl.CostEstimate(flops=5_000_000_000, bytes_accessed=4_000_000, transcendentals=1_000_000),
        name="main",
    )(own, below, above, k1, k2, k3, b1, b2)


def spread_side(dst, f, v):
    chans = v.shape[0]
    lane = lanes((chans, LANES))
    for half in range(2):
        w = v[:, tile(half)]
        for i, shifted in enumerate((turn(w, 1), w, turn(w, -1))):
            down = jnp.where(lane >= PITCH, turn(shifted, PITCH), jnp.zeros_like(shifted))
            up = jnp.where(lane < LANES - PITCH, turn(shifted, -PITCH), jnp.zeros_like(shifted))
            for dy, piece in enumerate((down, shifted, up)):
                at = (dy * 3 + i) * chans
                dst[f, at : at + chans, tile(half)] = piece


def finish_kernel(
    score_ref, west_ref, east_ref, from_west_ref, from_east_ref, k1_ref, k2_ref, k3_ref, b1_ref, b2_ref, b3_ref,
    state_ref, noise_ref, day_ref, out_ref, first_ref, part_ref, t1, t2, t3, scr,
):
    frames, fields = state_ref.shape[:2]
    rows = state_ref.shape[2]
    chans = west_ref.shape[1]
    lane = lanes((chans, LANES)) % PITCH
    for f in range(frames + 2 * DEPTH):
        west = jnp.where(lane < DEPTH, turn(from_west_ref[f], 2 * DEPTH - PITCH), west_ref[f])
        east = jnp.where(lane >= PITCH - DEPTH, turn(from_east_ref[f], PITCH - 2 * DEPTH), east_ref[f])
        spread_side(t1, f, jnp.concatenate([west, east], axis=1))

    me, last = lax.axis_index("space"), lax.axis_size("space") - 1
    pair = lanes((1, 2 * LANES))
    place = pair % PITCH
    outside = ((pair < LANES) & (place < DEPTH) & (me == 0)) | (
        (pair >= LANES) & (place >= PITCH - DEPTH) & (me == last)
    )

    def layer(src, dst, k_ref, b_ref, count, first):
        def step(f, carry):
            keep = in_trajectory(f + first, frames)
            z = jnp.concatenate([src[f + dt] for dt in range(3)], axis=0)
            acc = jnp.dot(k_ref[...], z, preferred_element_type=F32)
            h = jnp.where(keep & ~outside, silu(acc + b_ref[...]), 0.0).astype(BF)
            spread_side(dst, f, h)
            return carry

        lax.fori_loop(0, count, step, 0)

    layer(t1, t2, k1_ref, b1_ref, frames + 4, -2)
    layer(t2, t3, k2_ref, b2_ref, frames + 2, -1)

    col = lanes((fields, LANES))
    days = part_ref.shape[0]
    totals = [jnp.zeros((rows, LANES), F32) for _ in range(days)]
    for f in range(frames):
        z = jnp.concatenate([t3[f + dt] for dt in range(3)], axis=0)
        side = jnp.dot(k3_ref[...], z, preferred_element_type=F32)
        west, east = side[:, tile(0)], side[:, tile(1)]
        for y in range(rows):
            v = score_ref[f, :, tile(y)]
            v = jnp.where(col < DEPTH, turn(west, -(y * PITCH + DEPTH)), v)
            v = jnp.where(col >= LANES - DEPTH, turn(east, DEPTH - (y + 1) * PITCH), v)
            scr[f, pl.ds(y, fields, stride=rows), :] = v + b3_ref[...]
        score = scr[f].reshape(fields, rows, LANES)
        now = state_ref[f].astype(F32)
        moved = now + 0.8 * score + 0.5 * noise_ref[f].astype(F32)
        out_ref[f] = moved.astype(BF)
        first_ref[f] = moved[0]
        estimate = now[0] + 0.5 * score[0]
        for d in range(days):
            totals[d] = totals[d] + jnp.where(day_ref[f] == d, estimate, 0.0)
    for d in range(days):
        part_ref[d] = totals[d]


def make_finish(score, west, east, from_west, from_east, k1, k2, k3, b1, b2, b3, state, noise, day, days):
    frames, fields, rows, _ = state.shape
    chans, hid = west.shape[1], k2.shape[0]
    return pl.pallas_call(
        finish_kernel,
        out_shape=(
            jax.ShapeDtypeStruct(state.shape, BF),
            jax.ShapeDtypeStruct((frames, rows, LANES), F32),
            jax.ShapeDtypeStruct((days, rows, LANES), F32),
        ),
        in_specs=[VMEM] * 13 + [SMEM],
        out_specs=(VMEM,) * 3,
        scratch_shapes=[
            pltpu.VMEM((frames + 6, 9 * chans, 2 * LANES), BF),
            pltpu.VMEM((frames + 4, 9 * hid, 2 * LANES), BF),
            pltpu.VMEM((frames + 2, 9 * hid, 2 * LANES), BF),
            pltpu.VMEM((frames, fields * rows, LANES), F32),
        ],
        compiler_params=params(),
        name="finish",
    )(score, west, east, from_west, from_east, k1, k2, k3, b1, b2, b3, state, noise, day)


def correct_kernel(count, *refs):
    parts = refs[:count]
    observed_ref, mask_ref, first_ref, day_ref, _, out_ref, buf, sem = refs[count:]
    frames = first_ref.shape[0]
    days = observed_ref.shape[0]
    mask = mask_ref[...].astype(F32)
    misfit = []
    for d in range(days):
        total = parts[0][d]
        for p in parts[1:]:
            total = total + p[d]
        misfit.append(0.15 * (mask * (total - observed_ref[d])))
    for f in range(frames):
        v = first_ref[f]
        for d in range(days):
            v = v - jnp.where(day_ref[f] == d, misfit[d], 0.0)
        buf[f, 0] = v.astype(BF)
    copy = pltpu.make_async_copy(buf, out_ref.at[:, 0:1], sem)
    copy.start()
    copy.wait()


def make_correct(parts, observed, mask, first, day, out):
    frames, rows, _ = first.shape
    anywhere = pl.BlockSpec(memory_space=pl.ANY)
    return pl.pallas_call(
        functools.partial(correct_kernel, len(parts)),
        out_shape=jax.ShapeDtypeStruct(out.shape, BF),
        in_specs=[VMEM] * (len(parts) + 3) + [SMEM, anywhere],
        out_specs=anywhere,
        scratch_shapes=[pltpu.VMEM((frames, 1, rows, LANES), BF), pltpu.SemaphoreType.DMA],
        input_output_aliases={len(parts) + 4: 0},
        compiler_params=params(),
        name="correct",
    )(*parts, observed, mask, first, day, out)


def passed(value, axis, steps):
    count = lax.axis_size(axis)
    return lax.ppermute(value, axis, [(i, i + steps) for i in range(count) if 0 <= i + steps < count])


def body(
    state, noise, conv_one, bias_one, conv_two, bias_two, conv_three, bias_three, day_of_frame, observed, obs_mask
):
    state, noise = state[:, :, 0], noise[:, :, 0]
    hid, chans = conv_one.shape[:2]
    fields = conv_three.shape[0]
    w1 = conv_one.transpose(2, 3, 4, 1, 0).reshape(27 * chans, hid)
    w2 = conv_two.transpose(2, 3, 4, 0, 1).reshape(27, hid, hid)
    w3 = conv_three.transpose(2, 3, 4, 0, 1).reshape(27, fields, hid)
    b1, b2, b3 = bias_one[:, None], bias_two[:, None], bias_three[:, None]
    own, lo, hi, k1, k2, k3 = make_rows(state, w1, w2, w3)
    below = passed(hi, "tm", 1)
    above = passed(lo, "tm", -1)
    west, east = make_edges(own, below, above)
    from_west = passed(east, "space", 1)
    from_east = passed(west, "space", -1)
    score = make_main(own, below, above, k1, k2, k3, b1, b2)
    out, first, part = make_finish(
        score, west, east, from_west, from_east, k1, k2, k3, b1, b2, b3, state, noise, day_of_frame, observed.shape[0]
    )
    count = lax.axis_size("tm")
    if count <= 4:
        parts = [part] + [
            lax.ppermute(part, "tm", [(i, (i + s) % count) for i in range(count)]) for s in range(1, count)
        ]
    else:
        parts = [lax.psum(part, "tm")]
    out = make_correct(parts, observed[:, 0], obs_mask[0], first, day_of_frame, out)
    return out[:, :, None]


def solution(mesh):
    in_specs = (
        P("tm", None, "space", None, None),
        P("tm", None, "space", None, None),
        P(),
        P(),
        P(),
        P(),
        P(),
        P(),
        P("tm"),
        P(None, "space", None, None),
        P("space", None, None),
    )
    out_specs = P("tm", None, "space", None, None)
    return jax.shard_map(body, mesh=mesh, in_specs=in_specs, out_specs=out_specs, check_vma=False)
```

```python
import jax
import jax.numpy as jnp
from jax import lax
from jax.experimental import pallas as pl
from jax.experimental.pallas import tpu as pltpu
from jax.sharding import PartitionSpec as P

BF = jnp.bfloat16
F32 = jnp.float32
LANES = 128
DEPTH = 3
PITCH = 16
VMEM = pl.BlockSpec(memory_space=pltpu.VMEM)
SMEM = pl.BlockSpec(memory_space=pltpu.SMEM)
ANYWHERE = pl.BlockSpec(memory_space=pltpu.HBM)
LIMIT = 24 * 1024 * 1024


def shape_of(dims, kind):
    return jax.ShapeDtypeStruct(dims, kind)


def call(kernel, name, outs, specs, scratch=(), cost=None, alias=None, out_specs=None):
    return pl.pallas_call(
        kernel,
        out_shape=outs,
        in_specs=specs,
        out_specs=out_specs or (VMEM,) * len(outs),
        scratch_shapes=list(scratch),
        input_output_aliases=alias or {},
        compiler_params=pltpu.CompilerParams(vmem_limit_bytes=LIMIT),
        cost_estimate=cost and pl.CostEstimate(flops=cost, bytes_accessed=1_000_000, transcendentals=0),
        name=name,
    )


def silu(v):
    half = 0.5 * v
    return half + half * jnp.tanh(half)


def lanes(shape):
    return lax.broadcasted_iota(jnp.int32, shape, len(shape) - 1)


def turn(v, steps):
    steps = steps % LANES
    return pltpu.roll(v, steps, 1) if steps else v


def tile(i):
    return slice(i * LANES, (i + 1) * LANES)


def is_even(axis):
    return lax.axis_index(axis) % 2 == 0


def rows_kernel(state_ref, own_ref, first_ref, second_ref, raw, scr, sems):
    frames, chans, rows, _ = state_ref.shape
    copies = [pltpu.make_async_copy(state_ref.at[f], raw.at[f], sems.at[f]) for f in range(frames)]
    for c in copies:
        c.start()
    for f in range(frames):
        copies[f].wait()
        scr[f] = raw[f].astype(F32).reshape(chans * rows, LANES)
        for y in range(rows):
            own_ref[f, :, tile(y)] = scr[f, pl.ds(y, chans, stride=rows), :].astype(BF)
    even = is_even("tm")
    to_first = jnp.where(even, frames - DEPTH, 0)
    to_second = jnp.where(even, 0, frames - DEPTH)
    for f in range(DEPTH):
        first_ref[f] = own_ref[to_first + f]
        second_ref[f] = own_ref[to_second + f]


def make_rows(state):
    frames, chans, rows, _ = state.shape
    slab = shape_of((DEPTH, chans, rows * LANES), BF)
    return call(
        rows_kernel,
        "rows",
        (shape_of((frames, chans, rows * LANES), BF), slab, slab),
        [ANYWHERE],
        [
            pltpu.VMEM(state.shape, BF),
            pltpu.VMEM((frames, chans * rows, LANES), F32),
            pltpu.SemaphoreType.DMA((frames,)),
        ],
    )(state)


def column(ref):
    n = ref.shape[1]
    return jnp.broadcast_to(ref[...], (8, n)).T[:, 0:1]


def weights_kernel(
    w1_ref, w2_ref, w3_ref, b1_ref, b2_ref, b3_ref,
    m1_ref, m2_ref, m3_ref, s1_ref, s2_ref, s3_ref, c1_ref, c2_ref, c3_ref, r1, r2, r3, sems,
):
    copies = [
        pltpu.make_async_copy(a, b, sems.at[i])
        for i, (a, b) in enumerate(((w1_ref, r1), (w2_ref, r2), (w3_ref, r3)))
    ]
    for c in copies:
        c.start()
    c1_ref[...], c2_ref[...], c3_ref[...] = column(b1_ref), column(b2_ref), column(b3_ref)
    for ref in (m1_ref, m2_ref, m3_ref, s1_ref, s2_ref, s3_ref):
        ref[...] = jnp.zeros_like(ref)
    hid = c1_ref.shape[0]
    chans = r1.shape[0] // 27
    fields = c3_ref.shape[0]
    frames = m3_ref.shape[0] // fields
    copies[0].wait()
    flat = r1[...].astype(F32).T.astype(BF)
    for p in range(2):
        m1_ref[p * hid : (p + 1) * hid, p * 9 * chans : (p + 3) * 9 * chans] = flat
        for dt in range(3):
            for dy in range(3):
                at = (dt * 3 + dy) * 3 * chans
                s1_ref[(p * 3 + dy) * hid : (p * 3 + dy + 1) * hid, (dt + p) * 3 * chans : (dt + p + 1) * 3 * chans] = (
                    flat[:, at : at + 3 * chans]
                )

    def place(raw, main, side, count, outs):
        for dt in range(3):
            for dy in range(3):
                for dx in range(3):
                    w = raw[(dt * 3 + dy) * 3 + dx]
                    for p in range(count):
                        at = (((dt + p) * 3 + dy) * 3 + dx) * hid
                        main[p * outs : (p + 1) * outs, at : at + hid] = w
                        at = ((dt + p) * 3 + dx) * hid
                        side[(p * 3 + dy) * outs : (p * 3 + dy + 1) * outs, at : at + hid] = w

    copies[1].wait()
    place(r2, m2_ref, s2_ref, 2, hid)
    copies[2].wait()
    place(r3, m3_ref, s3_ref, frames, fields)


def make_weights(w1, w2, w3, b1, b2, b3, frames):
    hid, fields, chans = w2.shape[1], w3.shape[1], w1.shape[0] // 27
    return call(
        weights_kernel,
        "weights",
        (
            shape_of((2 * hid, 4 * 9 * chans), BF),
            shape_of((2 * hid, 4 * 9 * hid), BF),
            shape_of((frames * fields, (frames + 2) * 9 * hid), BF),
            shape_of((6 * hid, 4 * 3 * chans), BF),
            shape_of((6 * hid, 4 * 3 * hid), BF),
            shape_of((frames * 3 * fields, (frames + 2) * 3 * hid), BF),
            shape_of((hid, 1), F32),
            shape_of((hid, 1), F32),
            shape_of((fields, 1), F32),
        ),
        [ANYWHERE] * 3 + [VMEM] * 3,
        [pltpu.VMEM(w.shape, BF) for w in (w1, w2, w3)] + [pltpu.SemaphoreType.DMA((3,))],
        cost=1_000_000_000,
    )(w1, w2, w3, b1, b2, b3)


def slab_order(frames):
    even = is_even("tm")
    return jnp.where(even, frames + DEPTH, 0), jnp.where(even, 0, frames + DEPTH)


def edges_kernel(own_ref, first_ref, second_ref, west_ref, east_ref, send1_ref, send2_ref):
    frames = own_ref.shape[0]
    rows = own_ref.shape[2] // LANES
    shape = (own_ref.shape[1], LANES)
    lane = lanes(shape)
    group, place = lane // PITCH, lane % PITCH
    at1, at2 = slab_order(frames)
    even = is_even("space")
    for src, base, count in ((own_ref, DEPTH, frames), (first_ref, at1, DEPTH), (second_ref, at2, DEPTH)):
        for f in range(count):
            west = jnp.zeros(shape, BF)
            east = jnp.zeros(shape, BF)
            for y in range(rows):
                v = src[f, :, tile(y)]
                here = group == y
                west = jnp.where(here & (place >= DEPTH), turn(v, y * PITCH + DEPTH), west)
                east = jnp.where(here & (place < PITCH - DEPTH), turn(v, y * PITCH + PITCH - DEPTH), east)
            west_ref[base + f] = west
            east_ref[base + f] = east
            send1_ref[base + f] = jnp.where(even, east, west)
            send2_ref[base + f] = jnp.where(even, west, east)


def make_edges(own, first, second):
    frames, chans, _ = own.shape
    strip = shape_of((frames + 2 * DEPTH, chans, LANES), BF)
    return call(edges_kernel, "edges", (strip,) * 4, [VMEM] * 3)(own, first, second)


def spread(dst, f, y, v):
    chans = v.shape[0]
    at = tile(y + 1)
    dst[f, 0:chans, at] = turn(v, 1)
    dst[f, chans : 2 * chans, at] = v
    dst[f, 2 * chans : 3 * chans, at] = turn(v, -1)


def window(src, f, count, y):
    return jnp.concatenate(
        [src[f + j, :, (y + dy) * LANES : (y + dy + 2) * LANES] for j in range(count) for dy in range(3)], axis=0
    )


def in_trajectory(local, frames):
    step = lax.axis_index("tm") * frames + local
    return (step >= 0) & (step < frames * lax.axis_size("tm"))


def main_kernel(
    own_ref, first_ref, second_ref, m1_ref, m2_ref, m3_ref, c1_ref, c2_ref, score_ref, s1, s2, s3
):
    frames = own_ref.shape[0]
    rows = own_ref.shape[2] // LANES
    hid = c1_ref.shape[0]
    for s in (s1, s2, s3):
        s[:, :, tile(0)] = jnp.zeros(s.shape[:2] + (LANES,), BF)
        s[:, :, tile(rows + 1)] = jnp.zeros(s.shape[:2] + (LANES,), BF)
    at1, at2 = slab_order(frames)
    for src, base, count in ((own_ref, DEPTH, frames), (first_ref, at1, DEPTH), (second_ref, at2, DEPTH)):
        for f in range(count):
            for y in range(rows):
                spread(s1, base + f, y, src[f, :, tile(y)])

    def layer(src, dst, m_ref, c_ref, count, first):
        def step(i, carry):
            f = 2 * i
            for y in range(0, rows, 2):
                acc = jnp.dot(m_ref[...], window(src, f, 4, y), preferred_element_type=F32)
                for p in range(2):
                    h = silu(acc[p * hid : (p + 1) * hid] + c_ref[...]).astype(BF)
                    h = jnp.where(in_trajectory(f + p + first, frames), h, jnp.zeros_like(h))
                    spread(dst, f + p, y, h[:, tile(0)])
                    spread(dst, f + p, y + 1, h[:, tile(1)])
            return carry

        lax.fori_loop(0, count // 2, step, 0, unroll=UNROLL)

    layer(s1, s2, m1_ref, c1_ref, frames + 4, -2)
    layer(s2, s3, m2_ref, c2_ref, frames + 2, -1)
    for y in range(0, rows, 2):
        acc = jnp.dot(m3_ref[...], window(s3, 0, frames + 2, y), preferred_element_type=F32)
        score_ref[y], score_ref[y + 1] = acc[:, tile(0)], acc[:, tile(1)]


UNROLL = False


def make_main(own, first, second, m1, m2, m3, c1, c2):
    frames, chans, width = own.shape
    hid = c1.shape[0]
    wide = width + 2 * LANES
    return call(
        main_kernel,
        "main",
        (shape_of((width // LANES, m3.shape[0], LANES), F32),),
        [VMEM] * 8,
        [
            pltpu.VMEM((frames + 6, 3 * chans, wide), BF),
            pltpu.VMEM((frames + 4, 3 * hid, wide), BF),
            pltpu.VMEM((frames + 2, 3 * hid, wide), BF),
        ],
        cost=5_000_000_000,
    )(own, first, second, m1, m2, m3, c1, c2)[0]


def spread_side(dst, f, v):
    chans = v.shape[0]
    for half in range(2):
        w = v[:, tile(half)]
        dst[f, 0:chans, tile(half)] = turn(w, 1)
        dst[f, chans : 2 * chans, tile(half)] = w
        dst[f, 2 * chans : 3 * chans, tile(half)] = turn(w, -1)


def over_rows(acc, at, outs):
    halves = []
    for half in range(2):
        up, mid, down = (acc[at + d * outs : at + (d + 1) * outs, tile(half)] for d in range(3))
        lane = lanes((outs, LANES))
        up = jnp.where(lane >= PITCH, turn(up, PITCH), 0.0)
        down = jnp.where(lane < LANES - PITCH, turn(down, -PITCH), 0.0)
        halves.append(mid + up + down)
    return jnp.concatenate(halves, axis=1)


def patched(v, west, east, y):
    col = lanes(v.shape)
    v = jnp.where(col < DEPTH, turn(west, -(y * PITCH + DEPTH)), v)
    return jnp.where(col >= LANES - DEPTH, turn(east, DEPTH - (y + 1) * PITCH), v)


def side_kernel(
    score_ref, west_ref, east_ref, first_ref, second_ref, s1_ref, s2_ref, s3_ref, c1_ref, c2_ref, c3_ref,
    state_ref, day_ref, side_ref, part_ref, t1, t2, t3,
):
    frames, fields, rows, _ = state_ref.shape
    chans, hid = west_ref.shape[1], c1_ref.shape[0]
    place = lanes((chans, LANES)) % PITCH
    even = is_even("space")
    for f in range(frames + 2 * DEPTH):
        a, b = first_ref[f], second_ref[f]
        west = jnp.where(place < DEPTH, turn(jnp.where(even, b, a), 2 * DEPTH - PITCH), west_ref[f])
        east = jnp.where(place >= PITCH - DEPTH, turn(jnp.where(even, a, b), PITCH - 2 * DEPTH), east_ref[f])
        spread_side(t1, f, jnp.concatenate([west, east], axis=1))

    me, last = lax.axis_index("space"), lax.axis_size("space") - 1
    pair = lanes((1, 2 * LANES))
    place = pair % PITCH
    outside = ((pair < LANES) & (place < DEPTH) & (me == 0)) | (
        (pair >= LANES) & (place >= PITCH - DEPTH) & (me == last)
    )

    def layer(src, dst, m_ref, c_ref, count, first):
        for f in range(0, count, 2):
            z = jnp.concatenate([src[f + j] for j in range(4)], axis=0)
            acc = jnp.dot(m_ref[...], z, preferred_element_type=F32)
            for p in range(2):
                h = silu(over_rows(acc, p * 3 * hid, hid) + c_ref[...])
                keep = in_trajectory(f + p + first, frames) & ~outside
                spread_side(dst, f + p, jnp.where(keep, h, 0.0).astype(BF))

    layer(t1, t2, s1_ref, c1_ref, frames + 4, -2)
    layer(t2, t3, s2_ref, c2_ref, frames + 2, -1)
    z = jnp.concatenate([t3[j] for j in range(frames + 2)], axis=0)
    acc = jnp.dot(s3_ref[...], z, preferred_element_type=F32)
    for f in range(frames):
        both = over_rows(acc, f * 3 * fields, fields)
        for half in range(2):
            side_ref[half, f * fields : (f + 1) * fields] = both[:, tile(half)]

    days = part_ref.shape[0]
    heads = pl.ds(0, frames, stride=fields)
    west, east = side_ref[0, heads], side_ref[1, heads]
    row = lax.broadcasted_iota(jnp.int32, (frames, LANES), 0)
    day = jnp.zeros((frames, LANES), jnp.int32)
    for f in range(frames):
        day = jnp.where(row == f, day_ref[f], day)
    for y in range(rows):
        v = patched(score_ref[y, heads], west, east, y)
        for d in range(days):
            part_ref[d, y : y + 1, :] = jnp.sum(jnp.where(day == d, v, 0.0), axis=0, keepdims=True)
    base = c3_ref[0:1, 0:1]
    for d in range(days):
        total = 0.5 * part_ref[d]
        for f in range(frames):
            total = total + jnp.where(day_ref[f] == d, state_ref[f, 0].astype(F32) + 0.5 * base, 0.0)
        part_ref[d] = total


def make_side(score, west, east, first, second, s1, s2, s3, c1, c2, c3, state, day, days):
    frames, fields, rows, _ = state.shape
    chans, hid = west.shape[1], c1.shape[0]
    return call(
        side_kernel,
        "side",
        (shape_of((2, frames * fields, LANES), F32), shape_of((days, rows, LANES), F32)),
        [VMEM] * 12 + [SMEM],
        [
            pltpu.VMEM((frames + 6, 3 * chans, 2 * LANES), BF),
            pltpu.VMEM((frames + 4, 3 * hid, 2 * LANES), BF),
            pltpu.VMEM((frames + 2, 3 * hid, 2 * LANES), BF),
        ],
    )(score, west, east, first, second, s1, s2, s3, c1, c2, c3, state, day)


def update_kernel(score_ref, side_ref, c3_ref, state_ref, noise_ref, out_ref, head_ref, scr):
    frames, fields, rows, _ = state_ref.shape
    for f in range(frames):
        at = slice(f * fields, (f + 1) * fields)
        west, east = side_ref[0, at], side_ref[1, at]
        for y in range(rows):
            scr[f, pl.ds(y, fields, stride=rows), :] = (
                patched(score_ref[y, at], west, east, y) + c3_ref[...]
            )
        score = scr[f].reshape(fields, rows, LANES)
        moved = state_ref[f].astype(F32) + 0.8 * score + 0.5 * noise_ref[f].astype(F32)
        out_ref[f] = moved.astype(BF)
        head_ref[f] = moved[0]


def make_update(score, side, c3, state, noise):
    frames, fields, rows, _ = state.shape
    return call(
        update_kernel,
        "update",
        (shape_of(state.shape, BF), shape_of((frames, rows, LANES), F32)),
        [VMEM] * 5,
        [pltpu.VMEM((frames, fields * rows, LANES), F32)],
        cost=1_000_000_000,
    )(score, side, c3, state, noise)


def correct_kernel(mine_ref, theirs_ref, observed_ref, mask_ref, head_ref, day_ref, _, out_ref, buf, sem):
    frames = head_ref.shape[0]
    days = observed_ref.shape[0]
    mask = mask_ref[...].astype(F32)
    misfit = [0.15 * (mask * (mine_ref[d] + theirs_ref[d] - observed_ref[d])) for d in range(days)]
    for f in range(frames):
        v = head_ref[f]
        for d in range(days):
            v = v - jnp.where(day_ref[f] == d, misfit[d], 0.0)
        buf[f, 0] = v.astype(BF)
    copy = pltpu.make_async_copy(buf, out_ref.at[:, 0:1], sem)
    copy.start()
    copy.wait()


def make_correct(mine, theirs, observed, mask, head, day, out):
    frames, rows, _ = head.shape
    return call(
        correct_kernel,
        "correct",
        (shape_of(out.shape, BF),),
        [VMEM] * 5 + [SMEM, ANYWHERE],
        [pltpu.VMEM((frames, 1, rows, LANES), BF), pltpu.SemaphoreType.DMA],
        alias={6: 0},
        out_specs=(ANYWHERE,),
    )(mine, theirs, observed, mask, head, day, out)[0]


def exchanged(value, axis, start):
    pairs = [(i, i + 1) for i in range(start, lax.axis_size(axis) - 1, 2)]
    return lax.ppermute(value, axis, pairs + [(j, i) for i, j in pairs])


def body(
    state, noise, conv_one, bias_one, conv_two, bias_two, conv_three, bias_three, day_of_frame, observed, obs_mask
):
    state, noise = state[:, :, 0], noise[:, :, 0]
    hid, chans = conv_one.shape[:2]
    fields = conv_three.shape[0]
    w1 = conv_one.transpose(2, 3, 4, 1, 0).reshape(27 * chans, hid)
    w2 = conv_two.transpose(2, 3, 4, 0, 1).reshape(27, hid, hid)
    w3 = conv_three.transpose(2, 3, 4, 0, 1).reshape(27, fields, hid)
    own, send1, send2 = make_rows(state)
    first, second = exchanged(send1, "tm", 0), exchanged(send2, "tm", 1)
    m1, m2, m3, s1, s2, s3, c1, c2, c3 = make_weights(
        w1, w2, w3, bias_one[None], bias_two[None], bias_three[None], state.shape[0]
    )
    west, east, send1, send2 = make_edges(own, first, second)
    near, far = exchanged(send1, "space", 0), exchanged(send2, "space", 1)
    score = make_main(own, first, second, m1, m2, m3, c1, c2)
    side, mine = make_side(
        score, west, east, near, far, s1, s2, s3, c1, c2, c3, state, day_of_frame, observed.shape[0]
    )
    out, head = make_update(score, side, c3, state, noise)
    count = lax.axis_size("tm")
    reach = 1
    while True:
        theirs = lax.ppermute(mine, "tm", [(i, i ^ reach) for i in range(count)])
        reach *= 2
        if reach >= count:
            break
        mine = mine + theirs
    out = make_correct(mine, theirs, observed[:, 0], obs_mask[0], head, day_of_frame, out)
    return out[:, :, None]


def solution(mesh):
    in_specs = (
        P("tm", None, "space", None, None),
        P("tm", None, "space", None, None),
        P(),
        P(),
        P(),
        P(),
        P(),
        P(),
        P("tm"),
        P(None, "space", None, None),
        P("space", None, None),
    )
    out_specs = P("tm", None, "space", None, None)
    return jax.shard_map(body, mesh=mesh, in_specs=in_specs, out_specs=out_specs, check_vma=False)
```

```python
import jax
import jax.numpy as jnp
from jax import lax
from jax.experimental import pallas as pl
from jax.experimental.pallas import tpu as pltpu
from jax.sharding import PartitionSpec as P

BF = jnp.bfloat16
F32 = jnp.float32
LANES = 128
DEPTH = 3
PITCH = 16
VMEM = pl.BlockSpec(memory_space=pltpu.VMEM)
ANYWHERE = pl.BlockSpec(memory_space=pltpu.HBM)
LIMIT = 24 * 1024 * 1024


def shape_of(dims, kind):
    return jax.ShapeDtypeStruct(dims, kind)


def call(kernel, name, outs, specs, scratch=(), cost=None, alias=None, out_specs=None):
    return pl.pallas_call(
        kernel,
        out_shape=outs,
        in_specs=specs,
        out_specs=out_specs or (VMEM,) * len(outs),
        scratch_shapes=list(scratch),
        input_output_aliases=alias or {},
        compiler_params=pltpu.CompilerParams(vmem_limit_bytes=LIMIT),
        cost_estimate=cost and pl.CostEstimate(flops=cost, bytes_accessed=1_000_000, transcendentals=0),
        name=name,
    )


def silu(v):
    half = 0.5 * v
    return half + half * jnp.tanh(half)


def lanes(shape):
    return lax.broadcasted_iota(jnp.int32, shape, len(shape) - 1)


def turn(v, steps):
    steps = steps % LANES
    return pltpu.roll(v, steps, 1) if steps else v


def tile(i):
    return slice(i * LANES, (i + 1) * LANES)


def is_even(axis):
    return lax.axis_index(axis) % 2 == 0


def rows_kernel(state_ref, own_ref, first_ref, second_ref, scr):
    frames, chans, rows, _ = state_ref.shape
    for f in range(frames):
        scr[f] = state_ref[f].astype(F32).reshape(chans * rows, LANES)
        for y in range(rows):
            own_ref[f, :, tile(y)] = scr[f, pl.ds(y, chans, stride=rows), :].astype(BF)
    even = is_even("tm")
    to_first = jnp.where(even, frames - DEPTH, 0)
    to_second = jnp.where(even, 0, frames - DEPTH)
    for f in range(DEPTH):
        first_ref[f] = own_ref[to_first + f]
        second_ref[f] = own_ref[to_second + f]


def make_rows(state):
    frames, chans, rows, _ = state.shape
    slab = shape_of((DEPTH, chans, rows * LANES), BF)
    return call(
        rows_kernel,
        "rows",
        (shape_of((frames, chans, rows * LANES), BF), slab, slab),
        [VMEM],
        [pltpu.VMEM((frames, chans * rows, LANES), F32)],
        cost=4_000_000_000,
    )(state)


def weights_kernel(
    w1_ref, w2_ref, w3_ref, small_ref,
    m1_ref, m2_ref, m3_ref, s1_ref, s2_ref, s3_ref, c1_ref, c2_ref, c3_ref, days_ref, f2, f3,
):
    small = jnp.broadcast_to(small_ref[...], (8, small_ref.shape[1])).T[:, 0:1]
    at = 0
    for ref in (c1_ref, c2_ref, c3_ref, days_ref):
        ref[...] = jnp.broadcast_to(small[at : at + ref.shape[0]], ref.shape)
        at += ref.shape[0]
    for ref in (m1_ref, m2_ref, m3_ref, s1_ref, s2_ref, s3_ref):
        ref[...] = jnp.zeros_like(ref)
    hid, fields, chans = w2_ref.shape[1], w3_ref.shape[1], w1_ref.shape[0] // 27
    frames = days_ref.shape[0]
    flat = w1_ref[...].astype(F32).T.astype(BF)
    for p in range(2):
        m1_ref[p * hid : (p + 1) * hid, p * 9 * chans : (p + 3) * 9 * chans] = flat
        for dt in range(3):
            for dy in range(3):
                at = (dt * 3 + dy) * 3 * chans
                s1_ref[(p * 3 + dy) * hid : (p * 3 + dy + 1) * hid, (dt + p) * 3 * chans : (dt + p + 1) * 3 * chans] = (
                    flat[:, at : at + 3 * chans]
                )

    def place(raw, flat, main, side, count, outs):
        half = LANES // 2
        for t in range(27):
            for k in range(2):
                flat[k, :, t * hid + k * half : (t + 1) * hid + k * half] = raw[t]
        for p in range(count):
            rows, at = slice(p * outs, (p + 1) * outs), p * 9 * hid
            k = at % LANES // half
            main[rows, at : at + 27 * hid] = flat[k, :, k * half : k * half + 27 * hid]
            for dt in range(3):
                for dy in range(3):
                    rows = slice((p * 3 + dy) * outs, (p * 3 + dy + 1) * outs)
                    at, src = (dt + p) * 3 * hid, (dt * 3 + dy) * 3 * hid
                    k = (at - src) % LANES // half
                    side[rows, at : at + 3 * hid] = flat[k, :, src + k * half : src + k * half + 3 * hid]

    place(w2_ref, f2, m2_ref, s2_ref, 2, hid)
    place(w3_ref, f3, m3_ref, s3_ref, frames, fields)


def make_weights(w1, w2, w3, small, frames):
    hid, fields, chans = w2.shape[1], w3.shape[1], w1.shape[0] // 27
    return call(
        weights_kernel,
        "weights",
        (
            shape_of((2 * hid, 4 * 9 * chans), BF),
            shape_of((2 * hid, 4 * 9 * hid), BF),
            shape_of((frames * fields, (frames + 2) * 9 * hid), BF),
            shape_of((6 * hid, 4 * 3 * chans), BF),
            shape_of((6 * hid, 4 * 3 * hid), BF),
            shape_of((frames * 3 * fields, (frames + 2) * 3 * hid), BF),
            shape_of((hid, 1), F32),
            shape_of((hid, 1), F32),
            shape_of((fields, 1), F32),
            shape_of((frames, LANES), F32),
        ),
        [VMEM] * 4,
        [pltpu.VMEM((2, w.shape[1], 27 * hid + LANES // 2), BF) for w in (w2, w3)],
        cost=1_000_000_000,
    )(w1, w2, w3, small)


def slab_order(frames):
    even = is_even("tm")
    return jnp.where(even, frames + DEPTH, 0), jnp.where(even, 0, frames + DEPTH)


def edges_kernel(own_ref, first_ref, second_ref, west_ref, east_ref, send1_ref, send2_ref):
    frames = own_ref.shape[0]
    rows = own_ref.shape[2] // LANES
    shape = (own_ref.shape[1], LANES)
    lane = lanes(shape)
    group, place = lane // PITCH, lane % PITCH
    at1, at2 = slab_order(frames)
    even = is_even("space")
    for src, base, count in ((own_ref, DEPTH, frames), (first_ref, at1, DEPTH), (second_ref, at2, DEPTH)):
        for f in range(count):
            west = jnp.zeros(shape, BF)
            east = jnp.zeros(shape, BF)
            for y in range(rows):
                v = src[f, :, tile(y)]
                here = group == y
                west = jnp.where(here & (place >= DEPTH), turn(v, y * PITCH + DEPTH), west)
                east = jnp.where(here & (place < PITCH - DEPTH), turn(v, y * PITCH + PITCH - DEPTH), east)
            west_ref[base + f] = west
            east_ref[base + f] = east
            send1_ref[base + f] = jnp.where(even, east, west)
            send2_ref[base + f] = jnp.where(even, west, east)


def make_edges(own, first, second):
    frames, chans, _ = own.shape
    strip = shape_of((frames + 2 * DEPTH, chans, LANES), BF)
    return call(edges_kernel, "edges", (strip,) * 4, [VMEM] * 3)(own, first, second)


def spread(dst, f, y, v):
    chans = v.shape[0]
    at = tile(y + 1)
    dst[f, 0:chans, at] = turn(v, 1)
    dst[f, chans : 2 * chans, at] = v
    dst[f, 2 * chans : 3 * chans, at] = turn(v, -1)


def window(src, f, count, y):
    return jnp.concatenate(
        [src[f + j, :, (y + dy) * LANES : (y + dy + 2) * LANES] for j in range(count) for dy in range(3)], axis=0
    )


def in_trajectory(local, frames):
    step = lax.axis_index("tm") * frames + local
    return (step >= 0) & (step < frames * lax.axis_size("tm"))


def main_kernel(
    own_ref, first_ref, second_ref, m1_ref, m2_ref, m3_ref, c1_ref, c2_ref, score_ref, s1, s2, s3
):
    frames = own_ref.shape[0]
    rows = own_ref.shape[2] // LANES
    hid = c1_ref.shape[0]
    for s in (s1, s2, s3):
        s[:, :, tile(0)] = jnp.zeros(s.shape[:2] + (LANES,), BF)
        s[:, :, tile(rows + 1)] = jnp.zeros(s.shape[:2] + (LANES,), BF)
    at1, at2 = slab_order(frames)
    for src, base, count in ((own_ref, DEPTH, frames), (first_ref, at1, DEPTH), (second_ref, at2, DEPTH)):
        for f in range(count):
            for y in range(rows):
                spread(s1, base + f, y, src[f, :, tile(y)])

    def layer(src, dst, m_ref, bias, count, first):
        def step(i, carry):
            f = 2 * i
            for y in range(0, rows, 2):
                acc = jnp.dot(m_ref[...], window(src, f, 4, y), preferred_element_type=F32)
                for p in range(2):
                    h = silu(acc[p * hid : (p + 1) * hid] + bias).astype(BF)
                    h = jnp.where(in_trajectory(f + p + first, frames), h, jnp.zeros_like(h))
                    spread(dst, f + p, y, h[:, tile(0)])
                    spread(dst, f + p, y + 1, h[:, tile(1)])
            return carry

        lax.fori_loop(0, count // 2, step, 0, unroll=UNROLL)

    layer(s1, s2, m1_ref, c1_ref[...], frames + 4, -2)
    layer(s2, s3, m2_ref, c2_ref[...], frames + 2, -1)
    for y in range(0, rows, 2):
        acc = jnp.dot(m3_ref[...], window(s3, 0, frames + 2, y), preferred_element_type=F32)
        score_ref[y], score_ref[y + 1] = acc[:, tile(0)], acc[:, tile(1)]


UNROLL = True


def make_main(own, first, second, m1, m2, m3, c1, c2):
    frames, chans, width = own.shape
    hid = c1.shape[0]
    wide = width + 2 * LANES
    return call(
        main_kernel,
        "main",
        (shape_of((width // LANES, m3.shape[0], LANES), F32),),
        [VMEM] * 8,
        [
            pltpu.VMEM((frames + 6, 3 * chans, wide), BF),
            pltpu.VMEM((frames + 4, 3 * hid, wide), BF),
            pltpu.VMEM((frames + 2, 3 * hid, wide), BF),
        ],
        cost=5_000_000_000,
    )(own, first, second, m1, m2, m3, c1, c2)[0]


def spread_side(dst, f, v):
    chans = v.shape[0]
    for half in range(2):
        w = v[:, tile(half)]
        dst[f, 0:chans, tile(half)] = turn(w, 1)
        dst[f, chans : 2 * chans, tile(half)] = w
        dst[f, 2 * chans : 3 * chans, tile(half)] = turn(w, -1)


def over_rows(acc, at, outs):
    halves = []
    for half in range(2):
        up, mid, down = (acc[at + d * outs : at + (d + 1) * outs, tile(half)] for d in range(3))
        lane = lanes((outs, LANES))
        up = jnp.where(lane >= PITCH, turn(up, PITCH), 0.0)
        down = jnp.where(lane < LANES - PITCH, turn(down, -PITCH), 0.0)
        halves.append(mid + up + down)
    return jnp.concatenate(halves, axis=1)


def patched(v, west, east, y):
    col = lanes(v.shape)
    v = jnp.where(col < DEPTH, turn(west, -(y * PITCH + DEPTH)), v)
    return jnp.where(col >= LANES - DEPTH, turn(east, DEPTH - (y + 1) * PITCH), v)


def side_kernel(
    score_ref, west_ref, east_ref, first_ref, second_ref, s1_ref, s2_ref, s3_ref, c1_ref, c2_ref, c3_ref,
    state_ref, day_ref, side_ref, part_ref, t1, t2, t3,
):
    frames, fields, rows, _ = state_ref.shape
    chans, hid = west_ref.shape[1], c1_ref.shape[0]
    place = lanes((chans, LANES)) % PITCH
    even = is_even("space")
    for f in range(frames + 2 * DEPTH):
        a, b = first_ref[f], second_ref[f]
        west = jnp.where(place < DEPTH, turn(jnp.where(even, b, a), 2 * DEPTH - PITCH), west_ref[f])
        east = jnp.where(place >= PITCH - DEPTH, turn(jnp.where(even, a, b), PITCH - 2 * DEPTH), east_ref[f])
        spread_side(t1, f, jnp.concatenate([west, east], axis=1))

    me, last = lax.axis_index("space"), lax.axis_size("space") - 1
    pair = lanes((1, 2 * LANES))
    place = pair % PITCH
    outside = ((pair < LANES) & (place < DEPTH) & (me == 0)) | (
        (pair >= LANES) & (place >= PITCH - DEPTH) & (me == last)
    )

    def layer(src, dst, m_ref, bias, count, first):
        for f in range(0, count, 2):
            z = jnp.concatenate([src[f + j] for j in range(4)], axis=0)
            acc = jnp.dot(m_ref[...], z, preferred_element_type=F32)
            for p in range(2):
                h = silu(over_rows(acc, p * 3 * hid, hid) + bias)
                keep = in_trajectory(f + p + first, frames) & ~outside
                spread_side(dst, f + p, jnp.where(keep, h, 0.0).astype(BF))

    layer(t1, t2, s1_ref, c1_ref[...], frames + 4, -2)
    layer(t2, t3, s2_ref, c2_ref[...], frames + 2, -1)
    z = jnp.concatenate([t3[j] for j in range(frames + 2)], axis=0)
    acc = jnp.dot(s3_ref[...], z, preferred_element_type=F32)
    for f in range(frames):
        both = over_rows(acc, f * 3 * fields, fields)
        for half in range(2):
            side_ref[half, f * fields : (f + 1) * fields] = both[:, tile(half)]

    days = part_ref.shape[0]
    heads = pl.ds(0, frames, stride=fields)
    west, east = side_ref[0, heads], side_ref[1, heads]
    day = day_ref[...]
    for y in range(rows):
        v = patched(score_ref[y, heads], west, east, y)
        for d in range(days):
            part_ref[d, y : y + 1, :] = jnp.sum(jnp.where(day == d, v, 0.0), axis=0, keepdims=True)
    base = c3_ref[0:1, 0:1]
    for d in range(days):
        total = 0.5 * part_ref[d]
        for f in range(frames):
            total = total + jnp.where(day[f : f + 1] == d, state_ref[f, 0].astype(F32) + 0.5 * base, 0.0)
        part_ref[d] = total


def make_side(score, west, east, first, second, s1, s2, s3, c1, c2, c3, state, day, days):
    frames, fields, rows, _ = state.shape
    chans, hid = west.shape[1], c1.shape[0]
    return call(
        side_kernel,
        "side",
        (shape_of((2, frames * fields, LANES), F32), shape_of((days, rows, LANES), F32)),
        [VMEM] * 13,
        [
            pltpu.VMEM((frames + 6, 3 * chans, 2 * LANES), BF),
            pltpu.VMEM((frames + 4, 3 * hid, 2 * LANES), BF),
            pltpu.VMEM((frames + 2, 3 * hid, 2 * LANES), BF),
        ],
    )(score, west, east, first, second, s1, s2, s3, c1, c2, c3, state, day)


def update_kernel(score_ref, side_ref, c3_ref, state_ref, noise_ref, out_ref, head_ref, scr):
    frames, fields, rows, _ = state_ref.shape
    bias = c3_ref[...]
    for f in range(frames):
        at = slice(f * fields, (f + 1) * fields)
        west, east = side_ref[0, at], side_ref[1, at]
        for y in range(rows):
            scr[f, pl.ds(y, fields, stride=rows), :] = (
                patched(score_ref[y, at], west, east, y) + bias
            )
        score = scr[f].reshape(fields, rows, LANES)
        moved = state_ref[f].astype(F32) + 0.8 * score + 0.5 * noise_ref[f].astype(F32)
        out_ref[f] = moved.astype(BF)
        head_ref[f] = moved[0]


def make_update(score, side, c3, state, noise):
    frames, fields, rows, _ = state.shape
    return call(
        update_kernel,
        "update",
        (shape_of(state.shape, BF), shape_of((frames, rows, LANES), F32)),
        [VMEM] * 5,
        [pltpu.VMEM((frames, fields * rows, LANES), F32)],
        cost=1_000_000_000,
    )(score, side, c3, state, noise)


def correct_kernel(mine_ref, theirs_ref, observed_ref, mask_ref, head_ref, day_ref, _, out_ref, buf, sem):
    frames = head_ref.shape[0]
    days = observed_ref.shape[0]
    mask = mask_ref[...].astype(F32)
    misfit = [0.15 * (mask * (mine_ref[d] + theirs_ref[d] - observed_ref[d])) for d in range(days)]
    for f in range(frames):
        v = head_ref[f]
        for d in range(days):
            v = v - jnp.where(day_ref[f : f + 1] == d, misfit[d], 0.0)
        buf[f, 0] = v.astype(BF)
    copy = pltpu.make_async_copy(buf, out_ref.at[:, 0:1], sem)
    copy.start()
    copy.wait()


def make_correct(mine, theirs, observed, mask, head, day, out):
    frames, rows, _ = head.shape
    return call(
        correct_kernel,
        "correct",
        (shape_of(out.shape, BF),),
        [VMEM] * 6 + [ANYWHERE],
        [pltpu.VMEM((frames, 1, rows, LANES), BF), pltpu.SemaphoreType.DMA],
        alias={6: 0},
        out_specs=(ANYWHERE,),
    )(mine, theirs, observed, mask, head, day, out)[0]


def exchanged(value, axis, start):
    pairs = [(i, i + 1) for i in range(start, lax.axis_size(axis) - 1, 2)]
    return lax.ppermute(value, axis, pairs + [(j, i) for i, j in pairs])


def body(
    state, noise, conv_one, bias_one, conv_two, bias_two, conv_three, bias_three, day_of_frame, observed, obs_mask
):
    state, noise = state[:, :, 0], noise[:, :, 0]
    hid, chans = conv_one.shape[:2]
    fields = conv_three.shape[0]
    w1 = conv_one.transpose(2, 3, 4, 1, 0).reshape(27 * chans, hid)
    w2 = conv_two.transpose(2, 3, 4, 0, 1).reshape(27, hid, hid)
    w3 = conv_three.transpose(2, 3, 4, 0, 1).reshape(27, fields, hid)
    own, send1, send2 = make_rows(state)
    first, second = exchanged(send1, "tm", 0), exchanged(send2, "tm", 1)
    small = jnp.concatenate([bias_one, bias_two, bias_three, day_of_frame.astype(F32)])[None]
    m1, m2, m3, s1, s2, s3, c1, c2, c3, days = make_weights(w1, w2, w3, small, state.shape[0])
    west, east, send1, send2 = make_edges(own, first, second)
    near, far = exchanged(send1, "space", 0), exchanged(send2, "space", 1)
    score = make_main(own, first, second, m1, m2, m3, c1, c2)
    side, mine = make_side(
        score, west, east, near, far, s1, s2, s3, c1, c2, c3, state, days, observed.shape[0]
    )
    out, head = make_update(score, side, c3, state, noise)
    count = lax.axis_size("tm")
    reach = 1
    while True:
        theirs = lax.ppermute(mine, "tm", [(i, i ^ reach) for i in range(count)])
        reach *= 2
        if reach >= count:
            break
        mine = mine + theirs
    out = make_correct(mine, theirs, observed[:, 0], obs_mask[0], head, days, out)
    return out[:, :, None]


def solution(mesh):
    in_specs = (
        P("tm", None, "space", None, None),
        P("tm", None, "space", None, None),
        P(),
        P(),
        P(),
        P(),
        P(),
        P(),
        P("tm"),
        P(None, "space", None, None),
        P("space", None, None),
    )
    out_specs = P("tm", None, "space", None, None)
    return jax.shard_map(body, mesh=mesh, in_specs=in_specs, out_specs=out_specs, check_vma=False)
```

```python
import jax
import jax.numpy as jnp
from jax import lax
from jax.experimental import pallas as pl
from jax.experimental.pallas import tpu as pltpu
from jax.sharding import PartitionSpec as P

BF = jnp.bfloat16
F32 = jnp.float32
LANES = 128
DEPTH = 3
PITCH = 16
VMEM = pl.BlockSpec(memory_space=pltpu.VMEM)
ANYWHERE = pl.BlockSpec(memory_space=pltpu.HBM)
LIMIT = 24 * 1024 * 1024


def shape_of(dims, kind):
    return jax.ShapeDtypeStruct(dims, kind)


def call(kernel, name, outs, specs, scratch=(), cost=None, alias=None, out_specs=None):
    return pl.pallas_call(
        kernel,
        out_shape=outs,
        in_specs=specs,
        out_specs=out_specs or (VMEM,) * len(outs),
        scratch_shapes=list(scratch),
        input_output_aliases=alias or {},
        compiler_params=pltpu.CompilerParams(vmem_limit_bytes=LIMIT),
        cost_estimate=cost and pl.CostEstimate(flops=cost, bytes_accessed=1_000_000, transcendentals=0),
        name=name,
    )


def silu(v):
    half = 0.5 * v
    return half + half * jnp.tanh(half)


def lanes(shape):
    return lax.broadcasted_iota(jnp.int32, shape, len(shape) - 1)


def turn(v, steps):
    steps = steps % LANES
    return pltpu.roll(v, steps, 1) if steps else v


def tile(i):
    return slice(i * LANES, (i + 1) * LANES)


def is_even(axis):
    return lax.axis_index(axis) % 2 == 0


def rows_kernel(state_ref, own_ref, low_ref, high_ref, scr):
    frames, chans, rows, _ = state_ref.shape
    for f in range(frames):
        scr[f] = state_ref[f].astype(F32).reshape(chans * rows, LANES)
        for y in range(rows):
            v = scr[f, pl.ds(y, chans, stride=rows), :].astype(BF)
            own_ref[f, :, tile(y)] = v
            if f < DEPTH:
                low_ref[f, :, tile(y)] = v
            if f >= frames - DEPTH:
                high_ref[f - (frames - DEPTH), :, tile(y)] = v


def make_rows(state):
    frames, chans, rows, _ = state.shape
    slab = shape_of((DEPTH, chans, rows * LANES), BF)
    return call(
        rows_kernel,
        "rows",
        (shape_of((frames, chans, rows * LANES), BF), slab, slab),
        [VMEM],
        [pltpu.VMEM((frames, chans * rows, LANES), F32)],
        cost=4_000_000_000,
    )(state)


def weights_kernel(
    w1_ref, w2_ref, w3_ref, small_ref,
    m1_ref, m2_ref, m3_ref, s1_ref, s2_ref, s3_ref, c1_ref, c2_ref, c3_ref, days_ref, f2, f3,
):
    small = jnp.broadcast_to(small_ref[...], (8, small_ref.shape[1])).T[:, 0:1]
    at = 0
    for ref in (c1_ref, c2_ref, c3_ref, days_ref):
        ref[...] = jnp.broadcast_to(small[at : at + ref.shape[0]], ref.shape)
        at += ref.shape[0]
    for ref in (m1_ref, m2_ref, m3_ref, s1_ref, s2_ref, s3_ref):
        ref[...] = jnp.zeros_like(ref)
    hid, fields, chans = w2_ref.shape[1], w3_ref.shape[1], w1_ref.shape[0] // 27
    frames = days_ref.shape[0]
    flat = w1_ref[...].astype(F32).T.astype(BF)
    for p in range(2):
        m1_ref[p * hid : (p + 1) * hid, p * 9 * chans : (p + 3) * 9 * chans] = flat
        for dt in range(3):
            for dy in range(3):
                at = (dt * 3 + dy) * 3 * chans
                s1_ref[(p * 3 + dy) * hid : (p * 3 + dy + 1) * hid, (dt + p) * 3 * chans : (dt + p + 1) * 3 * chans] = (
                    flat[:, at : at + 3 * chans]
                )

    def place(raw, flat, main, side, count, outs):
        half = LANES // 2
        for t in range(27):
            for k in range(2):
                flat[k, :, t * hid + k * half : (t + 1) * hid + k * half] = raw[t]
        for p in range(count):
            rows, at = slice(p * outs, (p + 1) * outs), p * 9 * hid
            k = at % LANES // half
            main[rows, at : at + 27 * hid] = flat[k, :, k * half : k * half + 27 * hid]
            for dt in range(3):
                for dy in range(3):
                    rows = slice((p * 3 + dy) * outs, (p * 3 + dy + 1) * outs)
                    at, src = (dt + p) * 3 * hid, (dt * 3 + dy) * 3 * hid
                    k = (at - src) % LANES // half
                    side[rows, at : at + 3 * hid] = flat[k, :, src + k * half : src + k * half + 3 * hid]

    place(w2_ref, f2, m2_ref, s2_ref, 2, hid)
    place(w3_ref, f3, m3_ref, s3_ref, frames, fields)


def make_weights(w1, w2, w3, small, frames):
    hid, fields, chans = w2.shape[1], w3.shape[1], w1.shape[0] // 27
    return call(
        weights_kernel,
        "weights",
        (
            shape_of((2 * hid, 4 * 9 * chans), BF),
            shape_of((2 * hid, 4 * 9 * hid), BF),
            shape_of((frames * fields, (frames + 2) * 9 * hid), BF),
            shape_of((6 * hid, 4 * 3 * chans), BF),
            shape_of((6 * hid, 4 * 3 * hid), BF),
            shape_of((frames * 3 * fields, (frames + 2) * 3 * hid), BF),
            shape_of((hid, 1), F32),
            shape_of((hid, 1), F32),
            shape_of((fields, 1), F32),
            shape_of((frames, LANES), F32),
        ),
        [VMEM] * 4,
        [pltpu.VMEM((2, w.shape[1], 27 * hid + LANES // 2), BF) for w in (w2, w3)],
        cost=1_000_000_000,
    )(w1, w2, w3, small)


def widened(own_ref, below_ref, above_ref):
    frames = own_ref.shape[0]
    step, last = lax.axis_index("tm"), lax.axis_size("tm") - 1
    parts = (own_ref, DEPTH, None), (below_ref, 0, step > 0), (above_ref, DEPTH + frames, step < last)
    for src, base, inside in parts:
        for f in range(src.shape[0]):
            for y in range(src.shape[2] // LANES):
                v = src[f, :, tile(y)]
                yield base + f, y, v if inside is None else jnp.where(inside, v, jnp.zeros_like(v))


def edges_kernel(own_ref, below_ref, above_ref, west_ref, east_ref, send1_ref, send2_ref):
    rows = own_ref.shape[2] // LANES
    shape = (own_ref.shape[1], LANES)
    lane = lanes(shape)
    group, place = lane // PITCH, lane % PITCH
    even = is_even("space")
    for f, y, v in widened(own_ref, below_ref, above_ref):
        if y == 0:
            west, east = jnp.zeros(shape, BF), jnp.zeros(shape, BF)
        here = group == y
        west = jnp.where(here & (place >= DEPTH), turn(v, y * PITCH + DEPTH), west)
        east = jnp.where(here & (place < PITCH - DEPTH), turn(v, y * PITCH + PITCH - DEPTH), east)
        if y == rows - 1:
            west_ref[f], east_ref[f] = west, east
            send1_ref[f], send2_ref[f] = jnp.where(even, east, west), jnp.where(even, west, east)


def make_edges(own, below, above):
    frames, chans, _ = own.shape
    strip = shape_of((frames + 2 * DEPTH, chans, LANES), BF)
    return call(edges_kernel, "edges", (strip,) * 4, [VMEM] * 3)(own, below, above)


def spread(dst, f, y, v):
    chans = v.shape[0]
    at = tile(y + 1)
    dst[f, 0:chans, at] = turn(v, 1)
    dst[f, chans : 2 * chans, at] = v
    dst[f, 2 * chans : 3 * chans, at] = turn(v, -1)


def window(src, f, count, y):
    return jnp.concatenate(
        [src[f + j, :, (y + dy) * LANES : (y + dy + 2) * LANES] for j in range(count) for dy in range(3)], axis=0
    )


def in_trajectory(local, frames):
    step = lax.axis_index("tm") * frames + local
    return (step >= 0) & (step < frames * lax.axis_size("tm"))


def main_kernel(
    own_ref, below_ref, above_ref, m1_ref, m2_ref, m3_ref, c1_ref, c2_ref, score_ref, s1, s2, s3
):
    frames = own_ref.shape[0]
    rows = own_ref.shape[2] // LANES
    hid = c1_ref.shape[0]
    for s in (s1, s2, s3):
        s[:, :, tile(0)] = jnp.zeros(s.shape[:2] + (LANES,), BF)
        s[:, :, tile(rows + 1)] = jnp.zeros(s.shape[:2] + (LANES,), BF)
    for f, y, v in widened(own_ref, below_ref, above_ref):
        spread(s1, f, y, v)

    def layer(src, dst, m_ref, bias, count, first):
        def step(i, carry):
            f = 2 * i
            for y in range(0, rows, 2):
                acc = jnp.dot(m_ref[...], window(src, f, 4, y), preferred_element_type=F32)
                for p in range(2):
                    h = silu(acc[p * hid : (p + 1) * hid] + bias).astype(BF)
                    h = jnp.where(in_trajectory(f + p + first, frames), h, jnp.zeros_like(h))
                    spread(dst, f + p, y, h[:, tile(0)])
                    spread(dst, f + p, y + 1, h[:, tile(1)])
            return carry

        lax.fori_loop(0, count // 2, step, 0, unroll=UNROLL)

    layer(s1, s2, m1_ref, c1_ref[...], frames + 4, -2)
    layer(s2, s3, m2_ref, c2_ref[...], frames + 2, -1)
    for y in range(0, rows, 2):
        acc = jnp.dot(m3_ref[...], window(s3, 0, frames + 2, y), preferred_element_type=F32)
        score_ref[y], score_ref[y + 1] = acc[:, tile(0)], acc[:, tile(1)]


UNROLL = True


def make_main(own, below, above, m1, m2, m3, c1, c2):
    frames, chans, width = own.shape
    hid = c1.shape[0]
    wide = width + 2 * LANES
    return call(
        main_kernel,
        "main",
        (shape_of((width // LANES, m3.shape[0], LANES), F32),),
        [VMEM] * 8,
        [
            pltpu.VMEM((frames + 6, 3 * chans, wide), BF),
            pltpu.VMEM((frames + 4, 3 * hid, wide), BF),
            pltpu.VMEM((frames + 2, 3 * hid, wide), BF),
        ],
        cost=5_000_000_000,
    )(own, below, above, m1, m2, m3, c1, c2)[0]


def spread_side(dst, f, v):
    chans = v.shape[0]
    for half in range(2):
        w = v[:, tile(half)]
        dst[f, 0:chans, tile(half)] = turn(w, 1)
        dst[f, chans : 2 * chans, tile(half)] = w
        dst[f, 2 * chans : 3 * chans, tile(half)] = turn(w, -1)


def over_rows(acc, at, outs):
    halves = []
    for half in range(2):
        up, mid, down = (acc[at + d * outs : at + (d + 1) * outs, tile(half)] for d in range(3))
        lane = lanes((outs, LANES))
        up = jnp.where(lane >= PITCH, turn(up, PITCH), 0.0)
        down = jnp.where(lane < LANES - PITCH, turn(down, -PITCH), 0.0)
        halves.append(mid + up + down)
    return jnp.concatenate(halves, axis=1)


def patched(v, west, east, y):
    col = lanes(v.shape)
    v = jnp.where(col < DEPTH, turn(west, -(y * PITCH + DEPTH)), v)
    return jnp.where(col >= LANES - DEPTH, turn(east, DEPTH - (y + 1) * PITCH), v)


def side_kernel(
    score_ref, west_ref, east_ref, first_ref, second_ref, s1_ref, s2_ref, s3_ref, c1_ref, c2_ref, c3_ref,
    state_ref, day_ref, side_ref, part_ref, t1, t2, t3,
):
    frames, fields, rows, _ = state_ref.shape
    chans, hid = west_ref.shape[1], c1_ref.shape[0]
    place = lanes((chans, LANES)) % PITCH
    even = is_even("space")
    me, last = lax.axis_index("space"), lax.axis_size("space") - 1
    none = jnp.zeros((chans, LANES), BF)
    for f in range(frames + 2 * DEPTH):
        a, b = first_ref[f], second_ref[f]
        a, b = jnp.where(even, b, a), jnp.where(even, a, b)
        a, b = jnp.where(me > 0, a, none), jnp.where(me < last, b, none)
        west = jnp.where(place < DEPTH, turn(a, 2 * DEPTH - PITCH), west_ref[f])
        east = jnp.where(place >= PITCH - DEPTH, turn(b, PITCH - 2 * DEPTH), east_ref[f])
        spread_side(t1, f, jnp.concatenate([west, east], axis=1))

    pair = lanes((1, 2 * LANES))
    place = pair % PITCH
    outside = ((pair < LANES) & (place < DEPTH) & (me == 0)) | (
        (pair >= LANES) & (place >= PITCH - DEPTH) & (me == last)
    )

    def layer(src, dst, m_ref, bias, count, first):
        for f in range(0, count, 2):
            z = jnp.concatenate([src[f + j] for j in range(4)], axis=0)
            acc = jnp.dot(m_ref[...], z, preferred_element_type=F32)
            for p in range(2):
                h = silu(over_rows(acc, p * 3 * hid, hid) + bias)
                keep = in_trajectory(f + p + first, frames) & ~outside
                spread_side(dst, f + p, jnp.where(keep, h, 0.0).astype(BF))

    layer(t1, t2, s1_ref, c1_ref[...], frames + 4, -2)
    layer(t2, t3, s2_ref, c2_ref[...], frames + 2, -1)
    z = jnp.concatenate([t3[j] for j in range(frames + 2)], axis=0)
    acc = jnp.dot(s3_ref[...], z, preferred_element_type=F32)
    for f in range(frames):
        both = over_rows(acc, f * 3 * fields, fields)
        for half in range(2):
            side_ref[half, f * fields : (f + 1) * fields] = both[:, tile(half)]

    days = part_ref.shape[0]
    heads = pl.ds(0, frames, stride=fields)
    west, east = side_ref[0, heads], side_ref[1, heads]
    day = day_ref[...]
    for y in range(rows):
        v = patched(score_ref[y, heads], west, east, y)
        for d in range(days):
            part_ref[d, y : y + 1, :] = jnp.sum(jnp.where(day == d, v, 0.0), axis=0, keepdims=True)
    base = c3_ref[0:1, 0:1]
    for d in range(days):
        total = 0.5 * part_ref[d]
        for f in range(frames):
            total = total + jnp.where(day[f : f + 1] == d, state_ref[f, 0].astype(F32) + 0.5 * base, 0.0)
        part_ref[d] = total


def make_side(score, west, east, first, second, s1, s2, s3, c1, c2, c3, state, day, days):
    frames, fields, rows, _ = state.shape
    chans, hid = west.shape[1], c1.shape[0]
    return call(
        side_kernel,
        "side",
        (shape_of((2, frames * fields, LANES), F32), shape_of((days, rows, LANES), F32)),
        [VMEM] * 13,
        [
            pltpu.VMEM((frames + 6, 3 * chans, 2 * LANES), BF),
            pltpu.VMEM((frames + 4, 3 * hid, 2 * LANES), BF),
            pltpu.VMEM((frames + 2, 3 * hid, 2 * LANES), BF),
        ],
    )(score, west, east, first, second, s1, s2, s3, c1, c2, c3, state, day)


def update_kernel(score_ref, side_ref, c3_ref, state_ref, noise_ref, out_ref, head_ref, scr):
    frames, fields, rows, _ = state_ref.shape
    bias = c3_ref[...]
    for f in range(frames):
        at = slice(f * fields, (f + 1) * fields)
        west, east = side_ref[0, at], side_ref[1, at]
        for y in range(rows):
            scr[f, pl.ds(y, fields, stride=rows), :] = (
                patched(score_ref[y, at], west, east, y) + bias
            )
        score = scr[f].reshape(fields, rows, LANES)
        moved = state_ref[f].astype(F32) + 0.8 * score + 0.5 * noise_ref[f].astype(F32)
        out_ref[f] = moved.astype(BF)
        head_ref[f] = moved[0]


def make_update(score, side, c3, state, noise):
    frames, fields, rows, _ = state.shape
    return call(
        update_kernel,
        "update",
        (shape_of(state.shape, BF), shape_of((frames, rows, LANES), F32)),
        [VMEM] * 5,
        [pltpu.VMEM((frames, fields * rows, LANES), F32)],
        cost=1_000_000_000,
    )(score, side, c3, state, noise)


def correct_kernel(mine_ref, theirs_ref, observed_ref, mask_ref, head_ref, day_ref, _, out_ref, buf, sem):
    frames = head_ref.shape[0]
    days = observed_ref.shape[0]
    mask = mask_ref[...].astype(F32)
    misfit = [0.15 * (mask * (mine_ref[d] + theirs_ref[d] - observed_ref[d])) for d in range(days)]
    for f in range(frames):
        v = head_ref[f]
        for d in range(days):
            v = v - jnp.where(day_ref[f : f + 1] == d, misfit[d], 0.0)
        buf[f, 0] = v.astype(BF)
    copy = pltpu.make_async_copy(buf, out_ref.at[:, 0:1], sem)
    copy.start()
    copy.wait()


def make_correct(mine, theirs, observed, mask, head, day, out):
    frames, rows, _ = head.shape
    return call(
        correct_kernel,
        "correct",
        (shape_of(out.shape, BF),),
        [VMEM] * 6 + [ANYWHERE],
        [pltpu.VMEM((frames, 1, rows, LANES), BF), pltpu.SemaphoreType.DMA],
        alias={6: 0},
        out_specs=(ANYWHERE,),
    )(mine, theirs, observed, mask, head, day, out)[0]


def shifted(value, axis, steps):
    count = lax.axis_size(axis)
    return lax.ppermute(value, axis, [(i, (i + steps) % count) for i in range(count)])


def swapped(value, start):
    blocks, strips = lax.axis_size("tm"), lax.axis_size("space")
    pairs = []
    for t in range(blocks):
        for i in range(strips):
            other = i + 1 if i % 2 == start else i - 1
            if 0 <= other < strips:
                pairs.append((t * strips + i, t * strips + other))
            elif t ^ 1 < blocks:
                pairs.append((t * strips + i, (t ^ 1) * strips + i))
    return lax.ppermute(value, ("tm", "space"), pairs)


def body(
    state, noise, conv_one, bias_one, conv_two, bias_two, conv_three, bias_three, day_of_frame, observed, obs_mask
):
    state, noise = state[:, :, 0], noise[:, :, 0]
    hid, chans = conv_one.shape[:2]
    fields = conv_three.shape[0]
    w1 = conv_one.transpose(2, 3, 4, 1, 0).reshape(27 * chans, hid)
    w2 = conv_two.transpose(2, 3, 4, 0, 1).reshape(27, hid, hid)
    w3 = conv_three.transpose(2, 3, 4, 0, 1).reshape(27, fields, hid)
    own, low, high = make_rows(state)
    below, above = shifted(high, "tm", 1), shifted(low, "tm", -1)
    small = jnp.concatenate([bias_one, bias_two, bias_three, day_of_frame.astype(F32)])[None]
    m1, m2, m3, s1, s2, s3, c1, c2, c3, days = make_weights(w1, w2, w3, small, state.shape[0])
    west, east, send1, send2 = make_edges(own, below, above)
    near, far = swapped(send1, 0), swapped(send2, 1)
    score = make_main(own, below, above, m1, m2, m3, c1, c2)
    side, mine = make_side(
        score, west, east, near, far, s1, s2, s3, c1, c2, c3, state, days, observed.shape[0]
    )
    out, head = make_update(score, side, c3, state, noise)
    count = lax.axis_size("tm")
    reach = 1
    while True:
        theirs = lax.ppermute(mine, "tm", [(i, i ^ reach) for i in range(count)])
        reach *= 2
        if reach >= count:
            break
        mine = mine + theirs
    out = make_correct(mine, theirs, observed[:, 0], obs_mask[0], head, days, out)
    return out[:, :, None]


def solution(mesh):
    in_specs = (
        P("tm", None, "space", None, None),
        P("tm", None, "space", None, None),
        P(),
        P(),
        P(),
        P(),
        P(),
        P(),
        P("tm"),
        P(None, "space", None, None),
        P("space", None, None),
    )
    out_specs = P("tm", None, "space", None, None)
    return jax.shard_map(body, mesh=mesh, in_specs=in_specs, out_specs=out_specs, check_vma=False)
```

```python
import jax
import jax.numpy as jnp
from jax import lax
from jax.experimental import pallas as pl
from jax.experimental.pallas import tpu as pltpu
from jax.sharding import PartitionSpec as P

BF = jnp.bfloat16
F32 = jnp.float32
LANES = 128
DEPTH = 3
PITCH = 16
VMEM = pl.BlockSpec(memory_space=pltpu.VMEM)
ANYWHERE = pl.BlockSpec(memory_space=pltpu.HBM)
EARLY = 4
LIMIT = 24 * 1024 * 1024


def shape_of(dims, kind):
    return jax.ShapeDtypeStruct(dims, kind)


def call(kernel, name, outs, specs, scratch=(), cost=None, alias=None, out_specs=None):
    return pl.pallas_call(
        kernel,
        out_shape=outs,
        in_specs=specs,
        out_specs=out_specs or (VMEM,) * len(outs),
        scratch_shapes=list(scratch),
        input_output_aliases=alias or {},
        compiler_params=pltpu.CompilerParams(vmem_limit_bytes=LIMIT),
        cost_estimate=cost and pl.CostEstimate(flops=cost, bytes_accessed=1_000_000, transcendentals=0),
        name=name,
    )


def silu(v):
    half = 0.5 * v
    return half + half * jnp.tanh(half)


def lanes(shape):
    return lax.broadcasted_iota(jnp.int32, shape, len(shape) - 1)


def turn(v, steps):
    steps = steps % LANES
    return pltpu.roll(v, steps, 1) if steps else v


def tile(i):
    return slice(i * LANES, (i + 1) * LANES)


def is_even(axis):
    return lax.axis_index(axis) % 2 == 0


def rows_kernel(state_ref, own_ref, low_ref, high_ref, scr):
    frames, chans, rows, _ = state_ref.shape
    for f in range(frames):
        scr[f] = state_ref[f].astype(F32).reshape(chans * rows, LANES)
        for y in range(rows):
            v = scr[f, pl.ds(y, chans, stride=rows), :].astype(BF)
            own_ref[f, :, tile(y)] = v
            if f < DEPTH:
                low_ref[f, :, tile(y)] = v
            if f >= frames - DEPTH:
                high_ref[f - (frames - DEPTH), :, tile(y)] = v


def make_rows(state):
    frames, chans, rows, _ = state.shape
    slab = shape_of((DEPTH, chans, rows * LANES), BF)
    return call(
        rows_kernel,
        "rows",
        (shape_of((frames, chans, rows * LANES), BF), slab, slab),
        [VMEM],
        [pltpu.VMEM((frames, chans * rows, LANES), F32)],
        cost=4_000_000_000,
    )(state)


def weights_kernel(
    w1_ref, w2_ref, w3_ref, small_ref,
    m1_ref, m2_ref, m3_ref, s1_ref, s2_ref, s3_ref, c1_ref, c2_ref, c3_ref, days_ref, head_ref, f2, f3,
):
    small = jnp.broadcast_to(small_ref[...], (8, small_ref.shape[1])).T[:, 0:1]
    at = 0
    for ref in (c1_ref, c2_ref, c3_ref, days_ref):
        ref[...] = jnp.broadcast_to(small[at : at + ref.shape[0]], ref.shape)
        at += ref.shape[0]
    for ref in (m1_ref, m2_ref, m3_ref, s1_ref, s2_ref, s3_ref):
        ref[...] = jnp.zeros_like(ref)
    hid, fields, chans = w2_ref.shape[1], w3_ref.shape[1], w1_ref.shape[0] // 27
    frames = days_ref.shape[0]
    flat = w1_ref[...].astype(F32).T.astype(BF)
    for p in range(2):
        m1_ref[p * hid : (p + 1) * hid, p * 9 * chans : (p + 3) * 9 * chans] = flat
        for dt in range(3):
            for dy in range(3):
                at = (dt * 3 + dy) * 3 * chans
                s1_ref[(p * 3 + dy) * hid : (p * 3 + dy + 1) * hid, (dt + p) * 3 * chans : (dt + p + 1) * 3 * chans] = (
                    flat[:, at : at + 3 * chans]
                )

    def place(raw, flat, main, side, count, outs):
        half = LANES // 2
        for t in range(27):
            for k in range(2):
                flat[k, :, t * hid + k * half : (t + 1) * hid + k * half] = raw[t]
        for p in range(count):
            rows, at = slice(p * outs, (p + 1) * outs), p * 9 * hid
            k = at % LANES // half
            main[rows, at : at + 27 * hid] = flat[k, :, k * half : k * half + 27 * hid]
            for dt in range(3):
                for dy in range(3):
                    rows = slice((p * 3 + dy) * outs, (p * 3 + dy + 1) * outs)
                    at, src = (dt + p) * 3 * hid, (dt * 3 + dy) * 3 * hid
                    k = (at - src) % LANES // half
                    side[rows, at : at + 3 * hid] = flat[k, :, src + k * half : src + k * half + 3 * hid]

    place(w2_ref, f2, m2_ref, s2_ref, 2, hid)
    place(w3_ref, f3, m3_ref, s3_ref, frames, fields)
    shape = (head_ref.shape[0], s3_ref.shape[0])
    pick = lanes(shape) == fields * lax.broadcasted_iota(jnp.int32, shape, 0)
    head_ref[...] = jnp.dot(pick.astype(F32).astype(BF), s3_ref[...], preferred_element_type=F32).astype(BF)


def make_weights(w1, w2, w3, small, frames):
    hid, fields, chans = w2.shape[1], w3.shape[1], w1.shape[0] // 27
    return call(
        weights_kernel,
        "weights",
        (
            shape_of((2 * hid, 4 * 9 * chans), BF),
            shape_of((2 * hid, 4 * 9 * hid), BF),
            shape_of((frames * fields, (frames + 2) * 9 * hid), BF),
            shape_of((6 * hid, 4 * 3 * chans), BF),
            shape_of((6 * hid, 4 * 3 * hid), BF),
            shape_of((frames * 3 * fields, (frames + 2) * 3 * hid), BF),
            shape_of((hid, 1), F32),
            shape_of((hid, 1), F32),
            shape_of((fields, 1), F32),
            shape_of((frames, LANES), F32),
            shape_of((-(-3 * frames // 16) * 16, (frames + 2) * 3 * hid), BF),
        ),
        [VMEM] * 4,
        [pltpu.VMEM((2, w.shape[1], 27 * hid + LANES // 2), BF) for w in (w2, w3)],
        cost=1_000_000_000,
    )(w1, w2, w3, small)


def widened(own_ref, below_ref, above_ref):
    frames = own_ref.shape[0]
    step, last = lax.axis_index("tm"), lax.axis_size("tm") - 1
    parts = (own_ref, DEPTH, None), (below_ref, 0, step > 0), (above_ref, DEPTH + frames, step < last)
    for src, base, inside in parts:
        for f in range(src.shape[0]):
            for y in range(src.shape[2] // LANES):
                v = src[f, :, tile(y)]
                yield base + f, y, v if inside is None else jnp.where(inside, v, jnp.zeros_like(v))


def edges_kernel(own_ref, below_ref, above_ref, west_ref, east_ref, send1_ref, send2_ref):
    rows = own_ref.shape[2] // LANES
    shape = (own_ref.shape[1], LANES)
    lane = lanes(shape)
    group, place = lane // PITCH, lane % PITCH
    even = is_even("space")
    for f, y, v in widened(own_ref, below_ref, above_ref):
        if y == 0:
            west, east = jnp.zeros(shape, BF), jnp.zeros(shape, BF)
        here = group == y
        west = jnp.where(here & (place >= DEPTH), turn(v, y * PITCH + DEPTH), west)
        east = jnp.where(here & (place < PITCH - DEPTH), turn(v, y * PITCH + PITCH - DEPTH), east)
        if y == rows - 1:
            west_ref[f], east_ref[f] = west, east
            send1_ref[f], send2_ref[f] = jnp.where(even, east, west), jnp.where(even, west, east)


def make_edges(own, below, above):
    frames, chans, _ = own.shape
    strip = shape_of((frames + 2 * DEPTH, chans, LANES), BF)
    return call(edges_kernel, "edges", (strip,) * 4, [VMEM] * 3)(own, below, above)


def spread(dst, f, y, v):
    chans = v.shape[0]
    at = tile(y + 1)
    dst[f, 0:chans, at] = turn(v, 1)
    dst[f, chans : 2 * chans, at] = v
    dst[f, 2 * chans : 3 * chans, at] = turn(v, -1)


def window(src, f, count, y):
    return jnp.concatenate(
        [src[f + j, :, (y + dy) * LANES : (y + dy + 2) * LANES] for j in range(count) for dy in range(3)], axis=0
    )


def in_trajectory(local, frames):
    step = lax.axis_index("tm") * frames + local
    return (step >= 0) & (step < frames * lax.axis_size("tm"))


def main_kernel(
    own_ref, below_ref, above_ref, m1_ref, m2_ref, c1_ref, c2_ref, s3, s1, s2
):
    frames = own_ref.shape[0]
    rows = own_ref.shape[2] // LANES
    hid = c1_ref.shape[0]
    for s in (s1, s2, s3):
        s[:, :, tile(0)] = jnp.zeros(s.shape[:2] + (LANES,), BF)
        s[:, :, tile(rows + 1)] = jnp.zeros(s.shape[:2] + (LANES,), BF)
    for f, y, v in widened(own_ref, below_ref, above_ref):
        spread(s1, f, y, v)

    def layer(src, dst, m_ref, bias, count, first):
        def step(i, carry):
            f = 2 * i
            for y in range(0, rows, 2):
                acc = jnp.dot(m_ref[...], window(src, f, 4, y), preferred_element_type=F32)
                for p in range(2):
                    h = silu(acc[p * hid : (p + 1) * hid] + bias).astype(BF)
                    h = jnp.where(in_trajectory(f + p + first, frames), h, jnp.zeros_like(h))
                    spread(dst, f + p, y, h[:, tile(0)])
                    spread(dst, f + p, y + 1, h[:, tile(1)])
            return carry

        lax.fori_loop(0, count // 2, step, 0, unroll=UNROLL)

    layer(s1, s2, m1_ref, c1_ref[...], frames + 4, -2)
    layer(s2, s3, m2_ref, c2_ref[...], frames + 2, -1)


UNROLL = True


def make_main(own, below, above, m1, m2, c1, c2):
    frames, chans, width = own.shape
    hid = c1.shape[0]
    wide = width + 2 * LANES
    return call(
        main_kernel,
        "main",
        (shape_of((frames + 2, 3 * hid, wide), BF),),
        [VMEM] * 7,
        [
            pltpu.VMEM((frames + 6, 3 * chans, wide), BF),
            pltpu.VMEM((frames + 4, 3 * hid, wide), BF),
        ],
        cost=5_000_000_000,
    )(own, below, above, m1, m2, c1, c2)[0]


def spread_side(dst, f, v):
    chans = v.shape[0]
    for half in range(2):
        w = v[:, tile(half)]
        dst[f, 0:chans, tile(half)] = turn(w, 1)
        dst[f, chans : 2 * chans, tile(half)] = w
        dst[f, 2 * chans : 3 * chans, tile(half)] = turn(w, -1)


def three_rows(up, mid, down):
    lane = lanes(mid.shape)
    up = jnp.where(lane >= PITCH, turn(up, PITCH), 0.0)
    down = jnp.where(lane < LANES - PITCH, turn(down, -PITCH), 0.0)
    return mid + up + down


def over_rows(acc, at, outs):
    halves = []
    for half in range(2):
        up, mid, down = (acc[at + d * outs : at + (d + 1) * outs, tile(half)] for d in range(3))
        halves.append(three_rows(up, mid, down))
    return jnp.concatenate(halves, axis=1)


def patched(v, west, east, y):
    col = lanes(v.shape)
    v = jnp.where(col < DEPTH, turn(west, -(y * PITCH + DEPTH)), v)
    return jnp.where(col >= LANES - DEPTH, turn(east, DEPTH - (y + 1) * PITCH), v)


def side_kernel(
    wide_ref, west_ref, east_ref, first_ref, second_ref, s1_ref, s2_ref, head_ref, c1_ref, c2_ref, c3_ref,
    state_ref, day_ref, t3, part_ref, t1, t2, own, ends,
):
    frames, fields, rows, _ = state_ref.shape
    chans, hid = west_ref.shape[1], c1_ref.shape[0]
    place = lanes((chans, LANES)) % PITCH
    even = is_even("space")
    me, last = lax.axis_index("space"), lax.axis_size("space") - 1
    none = jnp.zeros((chans, LANES), BF)
    for f in range(frames + 2 * DEPTH):
        a, b = first_ref[f], second_ref[f]
        a, b = jnp.where(even, b, a), jnp.where(even, a, b)
        a, b = jnp.where(me > 0, a, none), jnp.where(me < last, b, none)
        west = jnp.where(place < DEPTH, turn(a, 2 * DEPTH - PITCH), west_ref[f])
        east = jnp.where(place >= PITCH - DEPTH, turn(b, PITCH - 2 * DEPTH), east_ref[f])
        spread_side(t1, f, jnp.concatenate([west, east], axis=1))

    pair = lanes((1, 2 * LANES))
    place = pair % PITCH
    outside = ((pair < LANES) & (place < DEPTH) & (me == 0)) | (
        (pair >= LANES) & (place >= PITCH - DEPTH) & (me == last)
    )

    def layer(src, dst, m_ref, bias, count, first):
        for f in range(0, count, 2):
            z = jnp.concatenate([src[f + j] for j in range(4)], axis=0)
            acc = jnp.dot(m_ref[...], z, preferred_element_type=F32)
            for p in range(2):
                h = silu(over_rows(acc, p * 3 * hid, hid) + bias)
                keep = in_trajectory(f + p + first, frames) & ~outside
                spread_side(dst, f + p, jnp.where(keep, h, 0.0).astype(BF))

    layer(t1, t2, s1_ref, c1_ref[...], frames + 4, -2)
    layer(t2, t3, s2_ref, c2_ref[...], frames + 2, -1)
    own[0] = jnp.zeros(own.shape[1:], F32)
    own[rows + 1] = jnp.zeros(own.shape[1:], F32)
    for y in range(0, rows, 2):
        z = jnp.concatenate([wide_ref[j, :, (y + 1) * LANES : (y + 3) * LANES] for j in range(frames + 2)], axis=0)
        acc = jnp.dot(head_ref[...], z, preferred_element_type=F32)
        own[y + 1], own[y + 2] = acc[:, tile(0)], acc[:, tile(1)]
    z = jnp.concatenate([t3[j] for j in range(frames + 2)], axis=0)
    acc = jnp.dot(head_ref[...], z, preferred_element_type=F32)
    ends[0], ends[1] = acc[:, tile(0)], acc[:, tile(1)]
    offsets = [pl.ds(dy, frames, stride=3) for dy in range(3)]
    west, east = (three_rows(*(ends[half, at] for at in offsets)) for half in range(2))
    days = part_ref.shape[0]
    day = day_ref[...]
    for y in range(rows):
        v = patched(sum(own[y + dy, offsets[dy]] for dy in range(3)), west, east, y)
        for d in range(days):
            part_ref[d, y : y + 1, :] = jnp.sum(jnp.where(day == d, v, 0.0), axis=0, keepdims=True)
    base = c3_ref[0:1, 0:1]
    for d in range(days):
        total = 0.5 * part_ref[d]
        for f in range(frames):
            total = total + jnp.where(day[f : f + 1] == d, state_ref[f, 0].astype(F32) + 0.5 * base, 0.0)
        part_ref[d] = total


def make_side(wide, west, east, first, second, s1, s2, head, c1, c2, c3, state, day, days):
    frames, fields, rows, _ = state.shape
    chans, hid = west.shape[1], c1.shape[0]
    return call(
        side_kernel,
        "side",
        (shape_of((frames + 2, 3 * hid, 2 * LANES), BF), shape_of((days, rows, LANES), F32)),
        [VMEM] * 13,
        [
            pltpu.VMEM((frames + 6, 3 * chans, 2 * LANES), BF),
            pltpu.VMEM((frames + 4, 3 * hid, 2 * LANES), BF),
            pltpu.VMEM((rows + 2, head.shape[0], LANES), F32),
            pltpu.VMEM((2, head.shape[0], LANES), F32),
        ],
    )(wide, west, east, first, second, s1, s2, head, c1, c2, c3, state, day)


def own_score(wide_ref, m3_ref, frames, y):
    acc = jnp.dot(m3_ref[...], window(wide_ref, 0, frames + 2, y), preferred_element_type=F32)
    return acc[:, tile(0)], acc[:, tile(1)]


def early_kernel(wide_ref, t3, m3_ref, s3_ref, score_ref, side_ref):
    frames = t3.shape[0] - 2
    fields = m3_ref.shape[0] // frames
    for y in range(0, score_ref.shape[0], 2):
        score_ref[y], score_ref[y + 1] = own_score(wide_ref, m3_ref, frames, y)
    z = jnp.concatenate([t3[j] for j in range(frames + 2)], axis=0)
    acc = jnp.dot(s3_ref[...], z, preferred_element_type=F32)
    for f in range(frames):
        both = over_rows(acc, f * 3 * fields, fields)
        for half in range(2):
            side_ref[half, f * fields : (f + 1) * fields] = both[:, tile(half)]


def make_early(wide, t3, m3, s3, count):
    return call(
        early_kernel,
        "early",
        (shape_of((count, m3.shape[0], LANES), F32), shape_of((2, m3.shape[0], LANES), F32)),
        [VMEM] * 4,
        cost=1_000_000_000,
    )(wide, t3, m3, s3)


def update_kernel(wide_ref, m3_ref, score_ref, side_ref, c3_ref, state_ref, noise_ref, out_ref, head_ref, rest, scr):
    frames, fields, rows, _ = state_ref.shape
    done = score_ref.shape[0]
    for y in range(done, rows, 2):
        rest[y - done], rest[y - done + 1] = own_score(wide_ref, m3_ref, frames, y)
    bias = c3_ref[...]
    for f in range(frames):
        at = slice(f * fields, (f + 1) * fields)
        west, east = side_ref[0, at], side_ref[1, at]
        for y in range(rows):
            v = score_ref[y, at] if y < done else rest[y - done, at]
            scr[f, pl.ds(y, fields, stride=rows), :] = patched(v, west, east, y) + bias
        score = scr[f].reshape(fields, rows, LANES)
        moved = state_ref[f].astype(F32) + 0.8 * score + 0.5 * noise_ref[f].astype(F32)
        out_ref[f] = moved.astype(BF)
        head_ref[f] = moved[0]


def make_update(wide, m3, score, side, c3, state, noise):
    frames, fields, rows, _ = state.shape
    return call(
        update_kernel,
        "update",
        (shape_of(state.shape, BF), shape_of((frames, rows, LANES), F32)),
        [VMEM] * 7,
        [
            pltpu.VMEM((rows - score.shape[0], frames * fields, LANES), F32),
            pltpu.VMEM((frames, fields * rows, LANES), F32),
        ],
        cost=2_000_000_000,
    )(wide, m3, score, side, c3, state, noise)


def correct_kernel(mine_ref, theirs_ref, observed_ref, mask_ref, head_ref, day_ref, _, out_ref, buf, sem):
    frames = head_ref.shape[0]
    days = observed_ref.shape[0]
    mask = mask_ref[...].astype(F32)
    misfit = [0.15 * (mask * (mine_ref[d] + theirs_ref[d] - observed_ref[d])) for d in range(days)]
    for f in range(frames):
        v = head_ref[f]
        for d in range(days):
            v = v - jnp.where(day_ref[f : f + 1] == d, misfit[d], 0.0)
        buf[f, 0] = v.astype(BF)
    copy = pltpu.make_async_copy(buf, out_ref.at[:, 0:1], sem)
    copy.start()
    copy.wait()


def make_correct(mine, theirs, observed, mask, head, day, out):
    frames, rows, _ = head.shape
    return call(
        correct_kernel,
        "correct",
        (shape_of(out.shape, BF),),
        [VMEM] * 6 + [ANYWHERE],
        [pltpu.VMEM((frames, 1, rows, LANES), BF), pltpu.SemaphoreType.DMA],
        alias={6: 0},
        out_specs=(ANYWHERE,),
    )(mine, theirs, observed, mask, head, day, out)[0]


def shifted(value, axis, steps):
    count = lax.axis_size(axis)
    return lax.ppermute(value, axis, [(i, (i + steps) % count) for i in range(count)])


def swapped(value, start):
    blocks, strips = lax.axis_size("tm"), lax.axis_size("space")
    pairs = []
    for t in range(blocks):
        for i in range(strips):
            other = i + 1 if i % 2 == start else i - 1
            if 0 <= other < strips:
                pairs.append((t * strips + i, t * strips + other))
            elif t ^ 1 < blocks:
                pairs.append((t * strips + i, (t ^ 1) * strips + i))
    return lax.ppermute(value, ("tm", "space"), pairs)


def body(
    state, noise, conv_one, bias_one, conv_two, bias_two, conv_three, bias_three, day_of_frame, observed, obs_mask
):
    state, noise = state[:, :, 0], noise[:, :, 0]
    hid, chans = conv_one.shape[:2]
    fields = conv_three.shape[0]
    w1 = conv_one.transpose(2, 3, 4, 1, 0).reshape(27 * chans, hid)
    w2 = conv_two.transpose(2, 3, 4, 0, 1).reshape(27, hid, hid)
    w3 = conv_three.transpose(2, 3, 4, 0, 1).reshape(27, fields, hid)
    own, low, high = make_rows(state)
    below, above = shifted(high, "tm", 1), shifted(low, "tm", -1)
    small = jnp.concatenate([bias_one, bias_two, bias_three, day_of_frame.astype(F32)])[None]
    m1, m2, m3, s1, s2, s3, c1, c2, c3, days, head = make_weights(w1, w2, w3, small, state.shape[0])
    west, east, send1, send2 = make_edges(own, below, above)
    near, far = swapped(send1, 0), swapped(send2, 1)
    wide = make_main(own, below, above, m1, m2, c1, c2)
    t3, mine = make_side(
        wide, west, east, near, far, s1, s2, head, c1, c2, c3, state, days, observed.shape[0]
    )
    score, side = make_early(wide, t3, m3, s3, EARLY)
    out, first = make_update(wide, m3, score, side, c3, state, noise)
    count = lax.axis_size("tm")
    reach = 1
    while True:
        theirs = lax.ppermute(mine, "tm", [(i, i ^ reach) for i in range(count)])
        reach *= 2
        if reach >= count:
            break
        mine = mine + theirs
    out = make_correct(mine, theirs, observed[:, 0], obs_mask[0], first, days, out)
    return out[:, :, None]


def solution(mesh):
    in_specs = (
        P("tm", None, "space", None, None),
        P("tm", None, "space", None, None),
        P(),
        P(),
        P(),
        P(),
        P(),
        P(),
        P("tm"),
        P(None, "space", None, None),
        P("space", None, None),
    )
    out_specs = P("tm", None, "space", None, None)
    return jax.shard_map(body, mesh=mesh, in_specs=in_specs, out_specs=out_specs, check_vma=False)
```

```python
import jax
import jax.numpy as jnp
from jax import lax
from jax.experimental import pallas as pl
from jax.experimental.pallas import tpu as pltpu
from jax.sharding import PartitionSpec as P

BF = jnp.bfloat16
F32 = jnp.float32
LANES = 128
DEPTH = 3
PITCH = 16
VMEM = pl.BlockSpec(memory_space=pltpu.VMEM)
ANYWHERE = pl.BlockSpec(memory_space=pltpu.HBM)
EARLY = 2
LIMIT = 24 * 1024 * 1024


def shape_of(dims, kind):
    return jax.ShapeDtypeStruct(dims, kind)


def call(kernel, name, outs, specs, scratch=(), cost=None, alias=None, out_specs=None):
    return pl.pallas_call(
        kernel,
        out_shape=outs,
        in_specs=specs,
        out_specs=out_specs or (VMEM,) * len(outs),
        scratch_shapes=list(scratch),
        input_output_aliases=alias or {},
        compiler_params=pltpu.CompilerParams(vmem_limit_bytes=LIMIT),
        cost_estimate=cost and pl.CostEstimate(flops=cost, bytes_accessed=1_000_000, transcendentals=0),
        name=name,
    )


def silu(v):
    half = 0.5 * v
    return half + half * jnp.tanh(half)


def lanes(shape):
    return lax.broadcasted_iota(jnp.int32, shape, len(shape) - 1)


def turn(v, steps):
    steps = steps % LANES
    return pltpu.roll(v, steps, 1) if steps else v


def tile(i):
    return slice(i * LANES, (i + 1) * LANES)


def is_even(axis):
    return lax.axis_index(axis) % 2 == 0


def rows_kernel(state_ref, own_ref, low_ref, high_ref, scr):
    frames, chans, rows, _ = state_ref.shape
    for f in range(frames):
        scr[f] = state_ref[f].astype(F32).reshape(chans * rows, LANES)
        for y in range(rows):
            v = scr[f, pl.ds(y, chans, stride=rows), :].astype(BF)
            own_ref[f, :, tile(y)] = v
            if f < DEPTH:
                low_ref[f, :, tile(y)] = v
            if f >= frames - DEPTH:
                high_ref[f - (frames - DEPTH), :, tile(y)] = v


def make_rows(state):
    frames, chans, rows, _ = state.shape
    slab = shape_of((DEPTH, chans, rows * LANES), BF)
    return call(
        rows_kernel,
        "rows",
        (shape_of((frames, chans, rows * LANES), BF), slab, slab),
        [VMEM],
        [pltpu.VMEM((frames, chans * rows, LANES), F32)],
        cost=4_000_000_000,
    )(state)


def weights_kernel(
    w1_ref, w2_ref, w3_ref, small_ref,
    m1_ref, m2_ref, m3_ref, s1_ref, s2_ref, s3_ref, c1_ref, c2_ref, c3_ref, days_ref, head_ref, f2, f3,
):
    small = jnp.broadcast_to(small_ref[...], (8, small_ref.shape[1])).T[:, 0:1]
    at = 0
    for ref in (c1_ref, c2_ref, c3_ref, days_ref):
        ref[...] = jnp.broadcast_to(small[at : at + ref.shape[0]], ref.shape)
        at += ref.shape[0]
    for ref in (m1_ref, m2_ref, m3_ref, s1_ref, s2_ref, s3_ref):
        ref[...] = jnp.zeros_like(ref)
    hid, fields, chans = w2_ref.shape[1], w3_ref.shape[1], w1_ref.shape[0] // 27
    frames = days_ref.shape[0]
    flat = w1_ref[...].astype(F32).T.astype(BF)
    for p in range(2):
        m1_ref[p * hid : (p + 1) * hid, p * 9 * chans : (p + 3) * 9 * chans] = flat
        for dt in range(3):
            for dy in range(3):
                at = (dt * 3 + dy) * 3 * chans
                s1_ref[(p * 3 + dy) * hid : (p * 3 + dy + 1) * hid, (dt + p) * 3 * chans : (dt + p + 1) * 3 * chans] = (
                    flat[:, at : at + 3 * chans]
                )

    def place(raw, flat, main, side, count, outs):
        half = LANES // 2
        for t in range(27):
            for k in range(2):
                flat[k, :, t * hid + k * half : (t + 1) * hid + k * half] = raw[t]
        for p in range(count):
            rows, at = slice(p * outs, (p + 1) * outs), p * 9 * hid
            k = at % LANES // half
            main[rows, at : at + 27 * hid] = flat[k, :, k * half : k * half + 27 * hid]
            for dt in range(3):
                for dy in range(3):
                    rows = slice((p * 3 + dy) * outs, (p * 3 + dy + 1) * outs)
                    at, src = (dt + p) * 3 * hid, (dt * 3 + dy) * 3 * hid
                    k = (at - src) % LANES // half
                    side[rows, at : at + 3 * hid] = flat[k, :, src + k * half : src + k * half + 3 * hid]

    place(w2_ref, f2, m2_ref, s2_ref, 2, hid)
    place(w3_ref, f3, m3_ref, s3_ref, frames, fields)
    shape = (head_ref.shape[0], s3_ref.shape[0])
    pick = lanes(shape) == fields * lax.broadcasted_iota(jnp.int32, shape, 0)
    head_ref[...] = jnp.dot(pick.astype(F32).astype(BF), s3_ref[...], preferred_element_type=F32).astype(BF)


def make_weights(w1, w2, w3, small, frames):
    hid, fields, chans = w2.shape[1], w3.shape[1], w1.shape[0] // 27
    return call(
        weights_kernel,
        "weights",
        (
            shape_of((2 * hid, 4 * 9 * chans), BF),
            shape_of((2 * hid, 4 * 9 * hid), BF),
            shape_of((frames * fields, (frames + 2) * 9 * hid), BF),
            shape_of((6 * hid, 4 * 3 * chans), BF),
            shape_of((6 * hid, 4 * 3 * hid), BF),
            shape_of((frames * 3 * fields, (frames + 2) * 3 * hid), BF),
            shape_of((hid, 1), F32),
            shape_of((hid, 1), F32),
            shape_of((fields, 1), F32),
            shape_of((frames, LANES), F32),
            shape_of((-(-3 * frames // 16) * 16, (frames + 2) * 3 * hid), BF),
        ),
        [VMEM] * 4,
        [pltpu.VMEM((2, w.shape[1], 27 * hid + LANES // 2), BF) for w in (w2, w3)],
        cost=1_000_000_000,
    )(w1, w2, w3, small)


def beside(below_ref, above_ref):
    step, last = lax.axis_index("tm"), lax.axis_size("tm") - 1
    for part, src, inside in ((0, below_ref, step > 0), (1, above_ref, step < last)):
        for f in range(DEPTH):
            for y in range(src.shape[2] // LANES):
                v = src[f, :, tile(y)]
                yield part * DEPTH + f, y, jnp.where(inside, v, jnp.zeros_like(v))


def strips(rows_of_frames, count):
    for f, y, v in rows_of_frames:
        lane = lanes(v.shape)
        group, place = lane // PITCH, lane % PITCH
        if y == 0:
            west, east = jnp.zeros_like(v), jnp.zeros_like(v)
        here = group == y
        west = jnp.where(here & (place >= DEPTH), turn(v, y * PITCH + DEPTH), west)
        east = jnp.where(here & (place < PITCH - DEPTH), turn(v, y * PITCH + PITCH - DEPTH), east)
        if y == count - 1:
            yield f, west, east


def edges_kernel(own_west_ref, own_east_ref, below_ref, above_ref, west_ref, east_ref, send1_ref, send2_ref):
    frames = own_west_ref.shape[0]
    even = is_even("space")

    def put(f, west, east):
        west_ref[f], east_ref[f] = west, east
        send1_ref[f], send2_ref[f] = jnp.where(even, east, west), jnp.where(even, west, east)

    for f in range(frames):
        put(DEPTH + f, own_west_ref[f], own_east_ref[f])
    for f, west, east in strips(beside(below_ref, above_ref), below_ref.shape[2] // LANES):
        put(f if f < DEPTH else f + frames, west, east)


def make_edges(own_west, own_east, below, above):
    frames, chans, _ = own_west.shape
    strip = shape_of((frames + 2 * DEPTH, chans, LANES), BF)
    return call(edges_kernel, "edges", (strip,) * 4, [VMEM] * 4)(own_west, own_east, below, above)


def spread(dst, f, y, v):
    chans = v.shape[0]
    at = tile(y + 1)
    dst[f, 0:chans, at] = turn(v, 1)
    dst[f, chans : 2 * chans, at] = v
    dst[f, 2 * chans : 3 * chans, at] = turn(v, -1)


def window(src, frames, y):
    parts = []
    for f in frames:
        ref, at = src(f)
        for dy in range(3):
            parts.append(ref[at, :, (y + dy) * LANES : (y + dy + 2) * LANES])
    return jnp.concatenate(parts, axis=0)


def plain(ref):
    return lambda f: (ref, f)


def in_trajectory(local, frames):
    step = lax.axis_index("tm") * frames + local
    return (step >= 0) & (step < frames * lax.axis_size("tm"))


def blank_ends(*refs):
    for s in refs:
        s[:, :, tile(0)] = jnp.zeros(s.shape[:2] + (LANES,), BF)
        last = s.shape[2] // LANES - 1
        s[:, :, tile(last)] = jnp.zeros(s.shape[:2] + (LANES,), BF)


def layer(src, dst, m_ref, c_ref, groups, rows, keep):
    hid = c_ref.shape[0]
    for f, count in groups:
        weights = m_ref[...] if count == 2 else m_ref[0:hid, 0 : m_ref.shape[1] // 4 * 3]
        for y in range(0, rows, 2):
            acc = jnp.dot(weights, window(src, range(f, f + count + 2), y), preferred_element_type=F32)
            for p in range(count):
                h = silu(acc[p * hid : (p + 1) * hid] + c_ref[...]).astype(BF)
                inside = keep(f + p)
                h = h if inside is None else jnp.where(inside, h, jnp.zeros_like(h))
                ref, at = dst(f + p)
                spread(ref, at, y, h[:, tile(0)])
                spread(ref, at, y + 1, h[:, tile(1)])


def pairs_of(frames):
    groups = [(f, 2) for f in range(frames[0], frames[-1], 2)]
    return groups + [(frames[-1], 1)] * (len(frames) % 2)


def inner_kernel(own_ref, m1_ref, c1_ref, s1, s2, west_ref, east_ref):
    frames = own_ref.shape[0]
    rows = own_ref.shape[2] // LANES
    each = [(f, y, own_ref[f, :, tile(y)]) for f in range(frames) for y in range(rows)]
    blank_ends(s1, s2)
    for f, y, v in each:
        spread(s1, f, y, v)
    for f, west, east in strips(each, rows):
        west_ref[f], east_ref[f] = west, east
    layer(plain(s1), plain(s2), m1_ref, c1_ref, pairs_of(range(frames - 2)), rows, lambda f: None)


def make_inner(own, m1, c1):
    frames, chans, width = own.shape
    hid, wide = c1.shape[0], width + 2 * LANES
    strip = shape_of((frames, chans, LANES), BF)
    return call(
        inner_kernel,
        "inner",
        (shape_of((frames, 3 * chans, wide), BF), shape_of((frames - 2, 3 * hid, wide), BF), strip, strip),
        [VMEM] * 3,
        cost=1_000_000_000,
    )(own, m1, c1)


def main_kernel(own1, own2, below_ref, above_ref, m1_ref, m2_ref, c1_ref, c2_ref, s3, far1, far2):
    frames = own1.shape[0]
    rows = below_ref.shape[2] // LANES
    blank_ends(far1, far2, s3)
    for f, y, v in beside(below_ref, above_ref):
        spread(far1, f, y, v)

    def split(own, far, edge):
        count = own.shape[0]
        return lambda f: (own, f - edge) if edge <= f < edge + count else (far, f if f < edge else f - count)

    one, two = split(own1, far1, DEPTH), split(own2, far2, DEPTH)
    groups = pairs_of(range(DEPTH)) + pairs_of(range(frames + 1, frames + 4))
    layer(one, two, m1_ref, c1_ref, groups, rows, lambda f: in_trajectory(f - 2, frames))
    layer(two, plain(s3), m2_ref, c2_ref, pairs_of(range(frames + 2)), rows, lambda f: in_trajectory(f - 1, frames))


def make_main(own1, own2, below, above, m1, m2, c1, c2):
    frames, rows1, wide = own1.shape
    rows2 = own2.shape[1]
    return call(
        main_kernel,
        "main",
        (shape_of((frames + 2, rows2, wide), BF),),
        [VMEM] * 8,
        [pltpu.VMEM((2 * DEPTH, rows1, wide), BF), pltpu.VMEM((2 * DEPTH, rows2, wide), BF)],
        cost=5_000_000_000,
    )(own1, own2, below, above, m1, m2, c1, c2)[0]


def spread_side(dst, f, v):
    chans = v.shape[0]
    for half in range(2):
        w = v[:, tile(half)]
        dst[f, 0:chans, tile(half)] = turn(w, 1)
        dst[f, chans : 2 * chans, tile(half)] = w
        dst[f, 2 * chans : 3 * chans, tile(half)] = turn(w, -1)


def three_rows(up, mid, down):
    lane = lanes(mid.shape)
    up = jnp.where(lane >= PITCH, turn(up, PITCH), 0.0)
    down = jnp.where(lane < LANES - PITCH, turn(down, -PITCH), 0.0)
    return mid + up + down


def over_rows(acc, at, outs):
    halves = []
    for half in range(2):
        up, mid, down = (acc[at + d * outs : at + (d + 1) * outs, tile(half)] for d in range(3))
        halves.append(three_rows(up, mid, down))
    return jnp.concatenate(halves, axis=1)


def patched(v, west, east, y):
    col = lanes(v.shape)
    v = jnp.where(col < DEPTH, turn(west, -(y * PITCH + DEPTH)), v)
    return jnp.where(col >= LANES - DEPTH, turn(east, DEPTH - (y + 1) * PITCH), v)


def side_kernel(
    wide_ref, west_ref, east_ref, first_ref, second_ref, s1_ref, s2_ref, head_ref, c1_ref, c2_ref, c3_ref,
    state_ref, day_ref, t3, part_ref, t1, t2, own, ends,
):
    frames, fields, rows, _ = state_ref.shape
    chans, hid = west_ref.shape[1], c1_ref.shape[0]
    place = lanes((chans, LANES)) % PITCH
    even = is_even("space")
    me, last = lax.axis_index("space"), lax.axis_size("space") - 1
    none = jnp.zeros((chans, LANES), BF)
    for f in range(frames + 2 * DEPTH):
        a, b = first_ref[f], second_ref[f]
        a, b = jnp.where(even, b, a), jnp.where(even, a, b)
        a, b = jnp.where(me > 0, a, none), jnp.where(me < last, b, none)
        west = jnp.where(place < DEPTH, turn(a, 2 * DEPTH - PITCH), west_ref[f])
        east = jnp.where(place >= PITCH - DEPTH, turn(b, PITCH - 2 * DEPTH), east_ref[f])
        spread_side(t1, f, jnp.concatenate([west, east], axis=1))

    pair = lanes((1, 2 * LANES))
    place = pair % PITCH
    outside = ((pair < LANES) & (place < DEPTH) & (me == 0)) | (
        (pair >= LANES) & (place >= PITCH - DEPTH) & (me == last)
    )

    def layer(src, dst, m_ref, bias, count, first):
        for f in range(0, count, 2):
            z = jnp.concatenate([src[f + j] for j in range(4)], axis=0)
            for p in range(2):
                acc = jnp.dot(m_ref[p * 3 * hid : (p + 1) * 3 * hid], z, preferred_element_type=F32)
                h = silu(over_rows(acc, 0, hid) + bias)
                keep = in_trajectory(f + p + first, frames) & ~outside
                spread_side(dst, f + p, jnp.where(keep, h, 0.0).astype(BF))

    layer(t1, t2, s1_ref, c1_ref[...], frames + 4, -2)
    layer(t2, t3, s2_ref, c2_ref[...], frames + 2, -1)
    own[0] = jnp.zeros(own.shape[1:], F32)
    own[rows + 1] = jnp.zeros(own.shape[1:], F32)
    for y in range(0, rows, 2):
        z = jnp.concatenate([wide_ref[j, :, (y + 1) * LANES : (y + 3) * LANES] for j in range(frames + 2)], axis=0)
        acc = jnp.dot(head_ref[...], z, preferred_element_type=F32)
        own[y + 1], own[y + 2] = acc[:, tile(0)], acc[:, tile(1)]
    z = jnp.concatenate([t3[j] for j in range(frames + 2)], axis=0)
    acc = jnp.dot(head_ref[...], z, preferred_element_type=F32)
    ends[0], ends[1] = acc[:, tile(0)], acc[:, tile(1)]
    offsets = [pl.ds(dy, frames, stride=3) for dy in range(3)]
    west, east = (three_rows(*(ends[half, at] for at in offsets)) for half in range(2))
    days = part_ref.shape[0]
    day = day_ref[...]
    for y in range(rows):
        v = patched(sum(own[y + dy, offsets[dy]] for dy in range(3)), west, east, y)
        for d in range(days):
            part_ref[d, y : y + 1, :] = jnp.sum(jnp.where(day == d, v, 0.0), axis=0, keepdims=True)
    base = c3_ref[0:1, 0:1]
    for d in range(days):
        total = 0.5 * part_ref[d]
        for f in range(frames):
            total = total + jnp.where(day[f : f + 1] == d, state_ref[f, 0].astype(F32) + 0.5 * base, 0.0)
        part_ref[d] = total


def make_side(wide, west, east, first, second, s1, s2, head, c1, c2, c3, state, day, days):
    frames, fields, rows, _ = state.shape
    chans, hid = west.shape[1], c1.shape[0]
    return call(
        side_kernel,
        "side",
        (shape_of((frames + 2, 3 * hid, 2 * LANES), BF), shape_of((days, rows, LANES), F32)),
        [VMEM] * 13,
        [
            pltpu.VMEM((frames + 6, 3 * chans, 2 * LANES), BF),
            pltpu.VMEM((frames + 4, 3 * hid, 2 * LANES), BF),
            pltpu.VMEM((rows + 2, head.shape[0], LANES), F32),
            pltpu.VMEM((2, head.shape[0], LANES), F32),
        ],
    )(wide, west, east, first, second, s1, s2, head, c1, c2, c3, state, day)


def own_score(wide_ref, m3_ref, frames, y):
    acc = jnp.dot(m3_ref[...], window(plain(wide_ref), range(frames + 2), y), preferred_element_type=F32)
    return acc[:, tile(0)], acc[:, tile(1)]


def early_kernel(wide_ref, t3, m3_ref, s3_ref, score_ref, side_ref):
    frames = t3.shape[0] - 2
    fields = m3_ref.shape[0] // frames
    for y in range(0, score_ref.shape[0], 2):
        score_ref[y], score_ref[y + 1] = own_score(wide_ref, m3_ref, frames, y)
    z = jnp.concatenate([t3[j] for j in range(frames + 2)], axis=0)
    acc = jnp.dot(s3_ref[...], z, preferred_element_type=F32)
    for f in range(frames):
        both = over_rows(acc, f * 3 * fields, fields)
        for half in range(2):
            side_ref[half, f * fields : (f + 1) * fields] = both[:, tile(half)]


def make_early(wide, t3, m3, s3, count):
    return call(
        early_kernel,
        "early",
        (shape_of((count, m3.shape[0], LANES), F32), shape_of((2, m3.shape[0], LANES), F32)),
        [VMEM] * 4,
        cost=1_000_000_000,
    )(wide, t3, m3, s3)


def update_kernel(wide_ref, m3_ref, score_ref, side_ref, c3_ref, state_ref, noise_ref, out_ref, head_ref, rest, scr):
    frames, fields, rows, _ = state_ref.shape
    done = score_ref.shape[0]
    for y in range(done, rows, 2):
        rest[y - done], rest[y - done + 1] = own_score(wide_ref, m3_ref, frames, y)
    bias = c3_ref[...]
    for f in range(frames):
        at = slice(f * fields, (f + 1) * fields)
        west, east = side_ref[0, at], side_ref[1, at]
        for y in range(rows):
            v = score_ref[y, at] if y < done else rest[y - done, at]
            scr[f, pl.ds(y, fields, stride=rows), :] = patched(v, west, east, y) + bias
        score = scr[f].reshape(fields, rows, LANES)
        moved = state_ref[f].astype(F32) + 0.8 * score + 0.5 * noise_ref[f].astype(F32)
        out_ref[f] = moved.astype(BF)
        head_ref[f] = moved[0]


def make_update(wide, m3, score, side, c3, state, noise):
    frames, fields, rows, _ = state.shape
    return call(
        update_kernel,
        "update",
        (shape_of(state.shape, BF), shape_of((frames, rows, LANES), F32)),
        [VMEM] * 7,
        [
            pltpu.VMEM((rows - score.shape[0], frames * fields, LANES), F32),
            pltpu.VMEM((frames, fields * rows, LANES), F32),
        ],
        cost=2_000_000_000,
    )(wide, m3, score, side, c3, state, noise)


def correct_kernel(mine_ref, theirs_ref, observed_ref, mask_ref, head_ref, day_ref, _, out_ref, buf, sem):
    frames = head_ref.shape[0]
    days = observed_ref.shape[0]
    mask = mask_ref[...].astype(F32)
    misfit = [0.15 * (mask * (mine_ref[d] + theirs_ref[d] - observed_ref[d])) for d in range(days)]
    for f in range(frames):
        v = head_ref[f]
        for d in range(days):
            v = v - jnp.where(day_ref[f : f + 1] == d, misfit[d], 0.0)
        buf[f, 0] = v.astype(BF)
    copy = pltpu.make_async_copy(buf, out_ref.at[:, 0:1], sem)
    copy.start()
    copy.wait()


def make_correct(mine, theirs, observed, mask, head, day, out):
    frames, rows, _ = head.shape
    return call(
        correct_kernel,
        "correct",
        (shape_of(out.shape, BF),),
        [VMEM] * 6 + [ANYWHERE],
        [pltpu.VMEM((frames, 1, rows, LANES), BF), pltpu.SemaphoreType.DMA],
        alias={6: 0},
        out_specs=(ANYWHERE,),
    )(mine, theirs, observed, mask, head, day, out)[0]


def shifted(value, axis, steps):
    count = lax.axis_size(axis)
    return lax.ppermute(value, axis, [(i, (i + steps) % count) for i in range(count)])


def swapped(value, start):
    blocks, strips = lax.axis_size("tm"), lax.axis_size("space")
    pairs = []
    for t in range(blocks):
        for i in range(strips):
            other = i + 1 if i % 2 == start else i - 1
            if 0 <= other < strips:
                pairs.append((t * strips + i, t * strips + other))
            elif t ^ 1 < blocks:
                pairs.append((t * strips + i, (t ^ 1) * strips + i))
    return lax.ppermute(value, ("tm", "space"), pairs)


def body(
    state, noise, conv_one, bias_one, conv_two, bias_two, conv_three, bias_three, day_of_frame, observed, obs_mask
):
    state, noise = state[:, :, 0], noise[:, :, 0]
    hid, chans = conv_one.shape[:2]
    fields = conv_three.shape[0]
    w1 = conv_one.transpose(2, 3, 4, 1, 0).reshape(27 * chans, hid)
    w2 = conv_two.transpose(2, 3, 4, 0, 1).reshape(27, hid, hid)
    w3 = conv_three.transpose(2, 3, 4, 0, 1).reshape(27, fields, hid)
    own, low, high = make_rows(state)
    below, above = shifted(high, "tm", 1), shifted(low, "tm", -1)
    small = jnp.concatenate([bias_one, bias_two, bias_three, day_of_frame.astype(F32)])[None]
    m1, m2, m3, s1, s2, s3, c1, c2, c3, days, head = make_weights(w1, w2, w3, small, state.shape[0])
    own1, own2, west, east = make_inner(own, m1, c1)
    west, east, send1, send2 = make_edges(west, east, below, above)
    near, far = swapped(send1, 0), swapped(send2, 1)
    wide = make_main(own1, own2, below, above, m1, m2, c1, c2)
    t3, mine = make_side(
        wide, west, east, near, far, s1, s2, head, c1, c2, c3, state, days, observed.shape[0]
    )
    score, side = make_early(wide, t3, m3, s3, EARLY)
    out, first = make_update(wide, m3, score, side, c3, state, noise)
    count = lax.axis_size("tm")
    reach = 1
    while True:
        theirs = lax.ppermute(mine, "tm", [(i, i ^ reach) for i in range(count)])
        reach *= 2
        if reach >= count:
            break
        mine = mine + theirs
    out = make_correct(mine, theirs, observed[:, 0], obs_mask[0], first, days, out)
    return out[:, :, None]


def solution(mesh):
    in_specs = (
        P("tm", None, "space", None, None),
        P("tm", None, "space", None, None),
        P(),
        P(),
        P(),
        P(),
        P(),
        P(),
        P("tm"),
        P(None, "space", None, None),
        P("space", None, None),
    )
    out_specs = P("tm", None, "space", None, None)
    return jax.shard_map(body, mesh=mesh, in_specs=in_specs, out_specs=out_specs, check_vma=False)
```

```python
import jax
import jax.numpy as jnp
from jax import lax
from jax.experimental import pallas as pl
from jax.experimental.pallas import tpu as pltpu
from jax.sharding import PartitionSpec as P

BF = jnp.bfloat16
F32 = jnp.float32
LANES = 128
DEPTH = 3
PITCH = 16
VMEM = pl.BlockSpec(memory_space=pltpu.VMEM)
ANYWHERE = pl.BlockSpec(memory_space=pltpu.HBM)
EARLY = 2
LIMIT = 24 * 1024 * 1024


def shape_of(dims, kind):
    return jax.ShapeDtypeStruct(dims, kind)


def call(kernel, name, outs, specs, scratch=(), cost=None, alias=None, out_specs=None):
    return pl.pallas_call(
        kernel,
        out_shape=outs,
        in_specs=specs,
        out_specs=out_specs or (VMEM,) * len(outs),
        scratch_shapes=list(scratch),
        input_output_aliases=alias or {},
        compiler_params=pltpu.CompilerParams(vmem_limit_bytes=LIMIT),
        cost_estimate=cost and pl.CostEstimate(flops=cost, bytes_accessed=1_000_000, transcendentals=0),
        name=name,
    )


def silu(v):
    half = 0.5 * v
    return half + half * jnp.tanh(half)


def lanes(shape):
    return lax.broadcasted_iota(jnp.int32, shape, len(shape) - 1)


def turn(v, steps):
    steps = steps % LANES
    return pltpu.roll(v, steps, 1) if steps else v


def tile(i):
    return slice(i * LANES, (i + 1) * LANES)


def is_even(axis):
    return lax.axis_index(axis) % 2 == 0


def rows_kernel(state_ref, own_ref, far_ref, near_ref, scr):
    frames, chans, rows, _ = state_ref.shape
    for f in range(frames):
        scr[f] = state_ref[f].astype(F32).reshape(chans * rows, LANES)
        for y in range(rows):
            v = scr[f, pl.ds(y, chans, stride=rows), :].astype(BF)
            own_ref[f, :, tile(y)] = v
    even = is_even("tm")
    for f in range(DEPTH):
        low, high = own_ref[f], own_ref[frames - DEPTH + f]
        near_ref[f], far_ref[f] = jnp.where(even, high, low), jnp.where(even, low, high)


def make_rows(state):
    frames, chans, rows, _ = state.shape
    slab = shape_of((DEPTH, chans, rows * LANES), BF)
    return call(
        rows_kernel,
        "rows",
        (shape_of((frames, chans, rows * LANES), BF), slab, slab),
        [VMEM],
        [pltpu.VMEM((frames, chans * rows, LANES), F32)],
        cost=4_000_000_000,
    )(state)


def weights_kernel(
    w1_ref, w2_ref, w3_ref, small_ref,
    m1_ref, m2_ref, m3_ref, s1_ref, s2_ref, s3_ref, c1_ref, c2_ref, c3_ref, days_ref, head_ref, f2, f3,
):
    small = jnp.broadcast_to(small_ref[...], (8, small_ref.shape[1])).T[:, 0:1]
    at = 0
    for ref in (c1_ref, c2_ref, c3_ref, days_ref):
        ref[...] = jnp.broadcast_to(small[at : at + ref.shape[0]], ref.shape)
        at += ref.shape[0]
    for ref in (m1_ref, m2_ref, m3_ref, s1_ref, s2_ref, s3_ref):
        ref[...] = jnp.zeros_like(ref)
    hid, fields, chans = w2_ref.shape[1], w3_ref.shape[1], w1_ref.shape[0] // 27
    frames = days_ref.shape[0]
    flat = w1_ref[...].astype(F32).T.astype(BF)
    for p in range(2):
        m1_ref[p * hid : (p + 1) * hid, p * 9 * chans : (p + 3) * 9 * chans] = flat
        for dt in range(3):
            for dy in range(3):
                at = (dt * 3 + dy) * 3 * chans
                s1_ref[(p * 3 + dy) * hid : (p * 3 + dy + 1) * hid, (dt + p) * 3 * chans : (dt + p + 1) * 3 * chans] = (
                    flat[:, at : at + 3 * chans]
                )

    def place(raw, flat, main, side, count, outs):
        half = LANES // 2
        for t in range(27):
            for k in range(2):
                flat[k, :, t * hid + k * half : (t + 1) * hid + k * half] = raw[t]
        for p in range(count):
            rows, at = slice(p * outs, (p + 1) * outs), p * 9 * hid
            k = at % LANES // half
            main[rows, at : at + 27 * hid] = flat[k, :, k * half : k * half + 27 * hid]
            for dt in range(3):
                for dy in range(3):
                    rows = slice((p * 3 + dy) * outs, (p * 3 + dy + 1) * outs)
                    at, src = (dt + p) * 3 * hid, (dt * 3 + dy) * 3 * hid
                    k = (at - src) % LANES // half
                    side[rows, at : at + 3 * hid] = flat[k, :, src + k * half : src + k * half + 3 * hid]

    place(w2_ref, f2, m2_ref, s2_ref, 2, hid)
    place(w3_ref, f3, m3_ref, s3_ref, frames, fields)
    shape = (head_ref.shape[0], s3_ref.shape[0])
    pick = lanes(shape) == fields * lax.broadcasted_iota(jnp.int32, shape, 0)
    head_ref[...] = jnp.dot(pick.astype(F32).astype(BF), s3_ref[...], preferred_element_type=F32).astype(BF)


def make_weights(w1, w2, w3, small, frames):
    hid, fields, chans = w2.shape[1], w3.shape[1], w1.shape[0] // 27
    return call(
        weights_kernel,
        "weights",
        (
            shape_of((2 * hid, 4 * 9 * chans), BF),
            shape_of((2 * hid, 4 * 9 * hid), BF),
            shape_of((frames * fields, (frames + 2) * 9 * hid), BF),
            shape_of((6 * hid, 4 * 3 * chans), BF),
            shape_of((6 * hid, 4 * 3 * hid), BF),
            shape_of((frames * 3 * fields, (frames + 2) * 3 * hid), BF),
            shape_of((hid, 1), F32),
            shape_of((hid, 1), F32),
            shape_of((fields, 1), F32),
            shape_of((frames, LANES), F32),
            shape_of((-(-3 * frames // 16) * 16, (frames + 2) * 3 * hid), BF),
        ),
        [VMEM] * 4,
        [pltpu.VMEM((2, w.shape[1], 27 * hid + LANES // 2), BF) for w in (w2, w3)],
        cost=1_000_000_000,
    )(w1, w2, w3, small)


def beside(near_ref, far_ref):
    step, last = lax.axis_index("tm"), lax.axis_size("tm") - 1
    even = is_even("tm")
    for f in range(DEPTH):
        for y in range(near_ref.shape[2] // LANES):
            a, b = near_ref[f, :, tile(y)], far_ref[f, :, tile(y)]
            none = jnp.zeros_like(a)
            yield f, y, jnp.where(step > 0, jnp.where(even, b, a), none)
            yield DEPTH + f, y, jnp.where(step < last, jnp.where(even, a, b), none)


def strips(rows_of_frames, count):
    begun = {}
    for f, y, v in rows_of_frames:
        lane = lanes(v.shape)
        group, place = lane // PITCH, lane % PITCH
        west, east = begun.pop(f, (jnp.zeros_like(v), jnp.zeros_like(v)))
        here = group == y
        west = jnp.where(here & (place >= DEPTH), turn(v, y * PITCH + DEPTH), west)
        east = jnp.where(here & (place < PITCH - DEPTH), turn(v, y * PITCH + PITCH - DEPTH), east)
        if y == count - 1:
            yield f, west, east
        else:
            begun[f] = west, east


def edges_kernel(own_west_ref, own_east_ref, far_ref, near_ref, west_ref, east_ref, send1_ref, send2_ref):
    frames = own_west_ref.shape[0]
    even = is_even("space")

    def put(f, west, east):
        west_ref[f], east_ref[f] = west, east
        send1_ref[f], send2_ref[f] = jnp.where(even, east, west), jnp.where(even, west, east)

    for f in range(frames):
        put(DEPTH + f, own_west_ref[f], own_east_ref[f])
    for f, west, east in strips(beside(near_ref, far_ref), near_ref.shape[2] // LANES):
        put(f if f < DEPTH else f + frames, west, east)


def make_edges(own_west, own_east, near, far):
    frames, chans, _ = own_west.shape
    strip = shape_of((frames + 2 * DEPTH, chans, LANES), BF)
    return call(edges_kernel, "edges", (strip,) * 4, [VMEM] * 4)(own_west, own_east, far, near)


def spread(dst, f, y, v):
    chans = v.shape[0]
    at = tile(y + 1)
    dst[f, 0:chans, at] = turn(v, 1)
    dst[f, chans : 2 * chans, at] = v
    dst[f, 2 * chans : 3 * chans, at] = turn(v, -1)


def window(src, frames, y):
    parts = []
    for f in frames:
        ref, at = src(f)
        for dy in range(3):
            parts.append(ref[at, :, (y + dy) * LANES : (y + dy + 2) * LANES])
    return jnp.concatenate(parts, axis=0)


def plain(ref):
    return lambda f: (ref, f)


def in_trajectory(local, frames):
    step = lax.axis_index("tm") * frames + local
    return (step >= 0) & (step < frames * lax.axis_size("tm"))


def blank_ends(*refs):
    for s in refs:
        s[:, :, tile(0)] = jnp.zeros(s.shape[:2] + (LANES,), BF)
        last = s.shape[2] // LANES - 1
        s[:, :, tile(last)] = jnp.zeros(s.shape[:2] + (LANES,), BF)


def layer(src, dst, m_ref, c_ref, groups, rows, keep):
    hid = c_ref.shape[0]
    for f, count in groups:
        weights = m_ref[...] if count == 2 else m_ref[0:hid, 0 : m_ref.shape[1] // 4 * 3]
        for y in range(0, rows, 2):
            acc = jnp.dot(weights, window(src, range(f, f + count + 2), y), preferred_element_type=F32)
            for p in range(count):
                h = silu(acc[p * hid : (p + 1) * hid] + c_ref[...]).astype(BF)
                inside = keep(f + p)
                h = h if inside is None else jnp.where(inside, h, jnp.zeros_like(h))
                ref, at = dst(f + p)
                spread(ref, at, y, h[:, tile(0)])
                spread(ref, at, y + 1, h[:, tile(1)])


def pairs_of(frames):
    groups = [(f, 2) for f in range(frames[0], frames[-1], 2)]
    return groups + [(frames[-1], 1)] * (len(frames) % 2)


def inner_kernel(own_ref, m1_ref, c1_ref, s1, s2, west_ref, east_ref):
    frames = own_ref.shape[0]
    rows = own_ref.shape[2] // LANES
    each = [(f, y, own_ref[f, :, tile(y)]) for f in range(frames) for y in range(rows)]
    blank_ends(s1, s2)
    for f, y, v in each:
        spread(s1, f, y, v)
    for f, west, east in strips(each, rows):
        west_ref[f], east_ref[f] = west, east
    layer(plain(s1), plain(s2), m1_ref, c1_ref, pairs_of(range(frames - 2)), rows, lambda f: None)


def make_inner(own, m1, c1):
    frames, chans, width = own.shape
    hid, wide = c1.shape[0], width + 2 * LANES
    strip = shape_of((frames, chans, LANES), BF)
    return call(
        inner_kernel,
        "inner",
        (shape_of((frames, 3 * chans, wide), BF), shape_of((frames - 2, 3 * hid, wide), BF), strip, strip),
        [VMEM] * 3,
        cost=1_000_000_000,
    )(own, m1, c1)


def main_kernel(own1, own2, far_ref, near_ref, m1_ref, m2_ref, c1_ref, c2_ref, s3, far1, far2):
    frames = own1.shape[0]
    rows = near_ref.shape[2] // LANES
    blank_ends(far1, far2, s3)
    for f, y, v in beside(near_ref, far_ref):
        spread(far1, f, y, v)

    def split(own, far, edge):
        count = own.shape[0]
        return lambda f: (own, f - edge) if edge <= f < edge + count else (far, f if f < edge else f - count)

    one, two = split(own1, far1, DEPTH), split(own2, far2, DEPTH)
    groups = pairs_of(range(DEPTH)) + pairs_of(range(frames + 1, frames + 4))
    layer(one, two, m1_ref, c1_ref, groups, rows, lambda f: in_trajectory(f - 2, frames))
    layer(two, plain(s3), m2_ref, c2_ref, pairs_of(range(frames + 2)), rows, lambda f: in_trajectory(f - 1, frames))


def make_main(own1, own2, near, far, m1, m2, c1, c2):
    frames, rows1, wide = own1.shape
    rows2 = own2.shape[1]
    return call(
        main_kernel,
        "main",
        (shape_of((frames + 2, rows2, wide), BF),),
        [VMEM] * 8,
        [pltpu.VMEM((2 * DEPTH, rows1, wide), BF), pltpu.VMEM((2 * DEPTH, rows2, wide), BF)],
        cost=5_000_000_000,
    )(own1, own2, far, near, m1, m2, c1, c2)[0]


def spread_side(dst, f, v):
    chans = v.shape[0]
    for half in range(2):
        w = v[:, tile(half)]
        dst[f, 0:chans, tile(half)] = turn(w, 1)
        dst[f, chans : 2 * chans, tile(half)] = w
        dst[f, 2 * chans : 3 * chans, tile(half)] = turn(w, -1)


def three_rows(up, mid, down):
    lane = lanes(mid.shape)
    up = jnp.where(lane >= PITCH, turn(up, PITCH), 0.0)
    down = jnp.where(lane < LANES - PITCH, turn(down, -PITCH), 0.0)
    return mid + up + down


def over_rows(acc, at, outs):
    halves = []
    for half in range(2):
        up, mid, down = (acc[at + d * outs : at + (d + 1) * outs, tile(half)] for d in range(3))
        halves.append(three_rows(up, mid, down))
    return jnp.concatenate(halves, axis=1)


def patched(v, west, east, y):
    col = lanes(v.shape)
    v = jnp.where(col < DEPTH, turn(west, -(y * PITCH + DEPTH)), v)
    return jnp.where(col >= LANES - DEPTH, turn(east, DEPTH - (y + 1) * PITCH), v)


def side_kernel(
    wide_ref, west_ref, east_ref, first_ref, second_ref, s1_ref, s2_ref, head_ref, c1_ref, c2_ref, c3_ref,
    state_ref, day_ref, t3, part_ref, t1, t2, own, ends,
):
    frames, fields, rows, _ = state_ref.shape
    chans, hid = west_ref.shape[1], c1_ref.shape[0]
    place = lanes((chans, LANES)) % PITCH
    even = is_even("space")
    me, last = lax.axis_index("space"), lax.axis_size("space") - 1
    none = jnp.zeros((chans, LANES), BF)
    for f in range(frames + 2 * DEPTH):
        a, b = first_ref[f], second_ref[f]
        a, b = jnp.where(even, b, a), jnp.where(even, a, b)
        a, b = jnp.where(me > 0, a, none), jnp.where(me < last, b, none)
        west = jnp.where(place < DEPTH, turn(a, 2 * DEPTH - PITCH), west_ref[f])
        east = jnp.where(place >= PITCH - DEPTH, turn(b, PITCH - 2 * DEPTH), east_ref[f])
        spread_side(t1, f, jnp.concatenate([west, east], axis=1))

    pair = lanes((1, 2 * LANES))
    place = pair % PITCH
    outside = ((pair < LANES) & (place < DEPTH) & (me == 0)) | (
        (pair >= LANES) & (place >= PITCH - DEPTH) & (me == last)
    )

    def layer(src, dst, m_ref, bias, count, first):
        for f in range(0, count, 2):
            z = jnp.concatenate([src[f + j] for j in range(4)], axis=0)
            for p in range(2):
                acc = jnp.dot(m_ref[p * 3 * hid : (p + 1) * 3 * hid], z, preferred_element_type=F32)
                h = silu(over_rows(acc, 0, hid) + bias)
                keep = in_trajectory(f + p + first, frames) & ~outside
                spread_side(dst, f + p, jnp.where(keep, h, 0.0).astype(BF))

    layer(t1, t2, s1_ref, c1_ref[...], frames + 4, -2)
    layer(t2, t3, s2_ref, c2_ref[...], frames + 2, -1)
    own[0] = jnp.zeros(own.shape[1:], F32)
    own[rows + 1] = jnp.zeros(own.shape[1:], F32)
    for y in range(0, rows, 2):
        z = jnp.concatenate([wide_ref[j, :, (y + 1) * LANES : (y + 3) * LANES] for j in range(frames + 2)], axis=0)
        acc = jnp.dot(head_ref[...], z, preferred_element_type=F32)
        own[y + 1], own[y + 2] = acc[:, tile(0)], acc[:, tile(1)]
    z = jnp.concatenate([t3[j] for j in range(frames + 2)], axis=0)
    acc = jnp.dot(head_ref[...], z, preferred_element_type=F32)
    ends[0], ends[1] = acc[:, tile(0)], acc[:, tile(1)]
    offsets = [pl.ds(dy, frames, stride=3) for dy in range(3)]
    west, east = (three_rows(*(ends[half, at] for at in offsets)) for half in range(2))
    days = part_ref.shape[0]
    day = day_ref[...]
    for y in range(rows):
        v = patched(sum(own[y + dy, offsets[dy]] for dy in range(3)), west, east, y)
        for d in range(days):
            part_ref[d, y : y + 1, :] = jnp.sum(jnp.where(day == d, v, 0.0), axis=0, keepdims=True)
    base = c3_ref[0:1, 0:1]
    for d in range(days):
        total = 0.5 * part_ref[d]
        for f in range(frames):
            total = total + jnp.where(day[f : f + 1] == d, state_ref[f, 0].astype(F32) + 0.5 * base, 0.0)
        part_ref[d] = total


def make_side(wide, west, east, first, second, s1, s2, head, c1, c2, c3, state, day, days):
    frames, fields, rows, _ = state.shape
    chans, hid = west.shape[1], c1.shape[0]
    return call(
        side_kernel,
        "side",
        (shape_of((frames + 2, 3 * hid, 2 * LANES), BF), shape_of((days, rows, LANES), F32)),
        [VMEM] * 13,
        [
            pltpu.VMEM((frames + 6, 3 * chans, 2 * LANES), BF),
            pltpu.VMEM((frames + 4, 3 * hid, 2 * LANES), BF),
            pltpu.VMEM((rows + 2, head.shape[0], LANES), F32),
            pltpu.VMEM((2, head.shape[0], LANES), F32),
        ],
    )(wide, west, east, first, second, s1, s2, head, c1, c2, c3, state, day)


def own_score(wide_ref, m3_ref, frames, y):
    acc = jnp.dot(m3_ref[...], window(plain(wide_ref), range(frames + 2), y), preferred_element_type=F32)
    return acc[:, tile(0)], acc[:, tile(1)]


def early_kernel(wide_ref, t3, m3_ref, s3_ref, score_ref, side_ref):
    frames = t3.shape[0] - 2
    fields = m3_ref.shape[0] // frames
    for y in range(0, score_ref.shape[0], 2):
        score_ref[y], score_ref[y + 1] = own_score(wide_ref, m3_ref, frames, y)
    z = jnp.concatenate([t3[j] for j in range(frames + 2)], axis=0)
    acc = jnp.dot(s3_ref[...], z, preferred_element_type=F32)
    for f in range(frames):
        both = over_rows(acc, f * 3 * fields, fields)
        for half in range(2):
            side_ref[half, f * fields : (f + 1) * fields] = both[:, tile(half)]


def make_early(wide, t3, m3, s3, count):
    return call(
        early_kernel,
        "early",
        (shape_of((count, m3.shape[0], LANES), F32), shape_of((2, m3.shape[0], LANES), F32)),
        [VMEM] * 4,
        cost=1_000_000_000,
    )(wide, t3, m3, s3)


def update_kernel(wide_ref, m3_ref, score_ref, side_ref, c3_ref, state_ref, noise_ref, out_ref, head_ref, rest, scr):
    frames, fields, rows, _ = state_ref.shape
    done = score_ref.shape[0]
    for y in range(done, rows, 2):
        rest[y - done], rest[y - done + 1] = own_score(wide_ref, m3_ref, frames, y)
    bias = c3_ref[...]
    for f in range(frames):
        at = slice(f * fields, (f + 1) * fields)
        west, east = side_ref[0, at], side_ref[1, at]
        for y in range(rows):
            v = score_ref[y, at] if y < done else rest[y - done, at]
            scr[f, pl.ds(y, fields, stride=rows), :] = patched(v, west, east, y) + bias
        score = scr[f].reshape(fields, rows, LANES)
        moved = state_ref[f].astype(F32) + 0.8 * score + 0.5 * noise_ref[f].astype(F32)
        out_ref[f] = moved.astype(BF)
        head_ref[f] = moved[0]


def make_update(wide, m3, score, side, c3, state, noise):
    frames, fields, rows, _ = state.shape
    return call(
        update_kernel,
        "update",
        (shape_of(state.shape, BF), shape_of((frames, rows, LANES), F32)),
        [VMEM] * 7,
        [
            pltpu.VMEM((rows - score.shape[0], frames * fields, LANES), F32),
            pltpu.VMEM((frames, fields * rows, LANES), F32),
        ],
        cost=2_000_000_000,
    )(wide, m3, score, side, c3, state, noise)


def correct_kernel(mine_ref, theirs_ref, observed_ref, mask_ref, head_ref, day_ref, _, out_ref, buf, sem):
    frames = head_ref.shape[0]
    days = observed_ref.shape[0]
    mask = mask_ref[...].astype(F32)
    misfit = [0.15 * (mask * (mine_ref[d] + theirs_ref[d] - observed_ref[d])) for d in range(days)]
    for f in range(frames):
        v = head_ref[f]
        for d in range(days):
            v = v - jnp.where(day_ref[f : f + 1] == d, misfit[d], 0.0)
        buf[f, 0] = v.astype(BF)
    copy = pltpu.make_async_copy(buf, out_ref.at[:, 0:1], sem)
    copy.start()
    copy.wait()


def make_correct(mine, theirs, observed, mask, head, day, out):
    frames, rows, _ = head.shape
    return call(
        correct_kernel,
        "correct",
        (shape_of(out.shape, BF),),
        [VMEM] * 6 + [ANYWHERE],
        [pltpu.VMEM((frames, 1, rows, LANES), BF), pltpu.SemaphoreType.DMA],
        alias={6: 0},
        out_specs=(ANYWHERE,),
    )(mine, theirs, observed, mask, head, day, out)[0]


def swapped(value, axis, start):
    sizes = {name: lax.axis_size(name) for name in ("tm", "space")}
    other = "space" if axis == "tm" else "tm"
    pairs = []
    for t in range(sizes["tm"]):
        for s in range(sizes["space"]):
            to = {"tm": t, "space": s}
            to[axis] += 1 if to[axis] % 2 == start else -1
            if not 0 <= to[axis] < sizes[axis]:
                to = {"tm": t, "space": s}
                to[other] ^= 1
            pairs.append((t * sizes["space"] + s, to["tm"] * sizes["space"] + to["space"]))
    return lax.ppermute(value, ("tm", "space"), pairs)


def body(
    state, noise, conv_one, bias_one, conv_two, bias_two, conv_three, bias_three, day_of_frame, observed, obs_mask
):
    state, noise = state[:, :, 0], noise[:, :, 0]
    hid, chans = conv_one.shape[:2]
    fields = conv_three.shape[0]
    w1 = conv_one.transpose(2, 3, 4, 1, 0).reshape(27 * chans, hid)
    w2 = conv_two.transpose(2, 3, 4, 0, 1).reshape(27, hid, hid)
    w3 = conv_three.transpose(2, 3, 4, 0, 1).reshape(27, fields, hid)
    own, send2, send1 = make_rows(state)
    far = swapped(send2, "tm", 1)
    near = swapped(send1, "tm", 0)
    small = jnp.concatenate([bias_one, bias_two, bias_three, day_of_frame.astype(F32)])[None]
    m1, m2, m3, s1, s2, s3, c1, c2, c3, days, head = make_weights(w1, w2, w3, small, state.shape[0])
    own1, own2, west, east = make_inner(own, m1, c1)
    west, east, send1, send2 = make_edges(west, east, near, far)
    first, second = swapped(send1, "space", 0), swapped(send2, "space", 1)
    wide = make_main(own1, own2, near, far, m1, m2, c1, c2)
    t3, mine = make_side(
        wide, west, east, first, second, s1, s2, head, c1, c2, c3, state, days, observed.shape[0]
    )
    score, side = make_early(wide, t3, m3, s3, EARLY)
    out, first = make_update(wide, m3, score, side, c3, state, noise)
    count = lax.axis_size("tm")
    reach = 1
    while True:
        theirs = lax.ppermute(mine, "tm", [(i, i ^ reach) for i in range(count)])
        reach *= 2
        if reach >= count:
            break
        mine = mine + theirs
    out = make_correct(mine, theirs, observed[:, 0], obs_mask[0], first, days, out)
    return out[:, :, None]


def solution(mesh):
    in_specs = (
        P("tm", None, "space", None, None),
        P("tm", None, "space", None, None),
        P(),
        P(),
        P(),
        P(),
        P(),
        P(),
        P("tm"),
        P(None, "space", None, None),
        P("space", None, None),
    )
    out_specs = P("tm", None, "space", None, None)
    return jax.shard_map(body, mesh=mesh, in_specs=in_specs, out_specs=out_specs, check_vma=False)
```

```python
import jax
import jax.numpy as jnp
from jax import lax
from jax.experimental import pallas as pl
from jax.experimental.pallas import tpu as pltpu
from jax.sharding import PartitionSpec as P

BF = jnp.bfloat16
F32 = jnp.float32
LANES = 128
DEPTH = 3
PITCH = 16
VMEM = pl.BlockSpec(memory_space=pltpu.VMEM)
ANYWHERE = pl.BlockSpec(memory_space=pltpu.HBM)
EARLY = 2
LIMIT = 24 * 1024 * 1024


def shape_of(dims, kind):
    return jax.ShapeDtypeStruct(dims, kind)


def call(kernel, name, outs, specs, scratch=(), cost=None, alias=None, out_specs=None):
    return pl.pallas_call(
        kernel,
        out_shape=outs,
        in_specs=specs,
        out_specs=out_specs or (VMEM,) * len(outs),
        scratch_shapes=list(scratch),
        input_output_aliases=alias or {},
        compiler_params=pltpu.CompilerParams(vmem_limit_bytes=LIMIT),
        cost_estimate=cost and pl.CostEstimate(flops=cost, bytes_accessed=1_000_000, transcendentals=0),
        name=name,
    )


def silu(v):
    half = 0.5 * v
    return half + half * jnp.tanh(half)


def lanes(shape):
    return lax.broadcasted_iota(jnp.int32, shape, len(shape) - 1)


def turn(v, steps):
    steps = steps % LANES
    return pltpu.roll(v, steps, 1) if steps else v


def tile(i):
    return slice(i * LANES, (i + 1) * LANES)


def is_even(axis):
    return lax.axis_index(axis) % 2 == 0


def rows_kernel(state_ref, own_ref, far_ref, near_ref, scr):
    frames, chans, rows, _ = state_ref.shape
    for f in range(frames):
        scr[f] = state_ref[f].astype(F32).reshape(chans * rows, LANES)
        for y in range(rows):
            v = scr[f, pl.ds(y, chans, stride=rows), :].astype(BF)
            own_ref[f, :, tile(y)] = v
    even = is_even("tm")
    for f in range(DEPTH):
        low, high = own_ref[f], own_ref[frames - DEPTH + f]
        near_ref[f], far_ref[f] = jnp.where(even, high, low), jnp.where(even, low, high)


def make_rows(state):
    frames, chans, rows, _ = state.shape
    slab = shape_of((DEPTH, chans, rows * LANES), BF)
    return call(
        rows_kernel,
        "rows",
        (shape_of((frames, chans, rows * LANES), BF), slab, slab),
        [VMEM],
        [pltpu.VMEM((frames, chans * rows, LANES), F32)],
        cost=4_000_000_000,
    )(state)


def weights_kernel(
    w1_ref, w2_ref, w3_ref, small_ref,
    m1_ref, m2_ref, m3_ref, s1_ref, s2_ref, s3_ref, c1_ref, c2_ref, c3_ref, days_ref, head_ref, f2, f3,
):
    small = jnp.broadcast_to(small_ref[...], (8, small_ref.shape[1])).T[:, 0:1]
    at = 0
    for ref in (c1_ref, c2_ref, c3_ref, days_ref):
        ref[...] = jnp.broadcast_to(small[at : at + ref.shape[0]], ref.shape)
        at += ref.shape[0]
    for ref in (m1_ref, m2_ref, m3_ref, s1_ref, s2_ref, s3_ref):
        ref[...] = jnp.zeros_like(ref)
    hid, fields, chans = w2_ref.shape[1], w3_ref.shape[1], w1_ref.shape[0] // 27
    frames = days_ref.shape[0]
    flat = w1_ref[...].astype(F32).T.astype(BF)
    for p in range(2):
        m1_ref[p * hid : (p + 1) * hid, p * 9 * chans : (p + 3) * 9 * chans] = flat
        for dt in range(3):
            for dy in range(3):
                at = (dt * 3 + dy) * 3 * chans
                s1_ref[(p * 3 + dy) * hid : (p * 3 + dy + 1) * hid, (dt + p) * 3 * chans : (dt + p + 1) * 3 * chans] = (
                    flat[:, at : at + 3 * chans]
                )

    def place(raw, flat, main, side, count, outs):
        half = LANES // 2
        for t in range(27):
            for k in range(2):
                flat[k, :, t * hid + k * half : (t + 1) * hid + k * half] = raw[t]
        for p in range(count):
            rows, at = slice(p * outs, (p + 1) * outs), p * 9 * hid
            k = at % LANES // half
            main[rows, at : at + 27 * hid] = flat[k, :, k * half : k * half + 27 * hid]
            for dt in range(3):
                for dy in range(3):
                    rows = slice((p * 3 + dy) * outs, (p * 3 + dy + 1) * outs)
                    at, src = (dt + p) * 3 * hid, (dt * 3 + dy) * 3 * hid
                    k = (at - src) % LANES // half
                    side[rows, at : at + 3 * hid] = flat[k, :, src + k * half : src + k * half + 3 * hid]

    place(w2_ref, f2, m2_ref, s2_ref, 2, hid)
    place(w3_ref, f3, m3_ref, s3_ref, frames, fields)
    shape = (head_ref.shape[0], s3_ref.shape[0])
    pick = lanes(shape) == fields * lax.broadcasted_iota(jnp.int32, shape, 0)
    head_ref[...] = jnp.dot(pick.astype(F32).astype(BF), s3_ref[...], preferred_element_type=F32).astype(BF)


def make_weights(w1, w2, w3, small, frames):
    hid, fields, chans = w2.shape[1], w3.shape[1], w1.shape[0] // 27
    return call(
        weights_kernel,
        "weights",
        (
            shape_of((2 * hid, 4 * 9 * chans), BF),
            shape_of((2 * hid, 4 * 9 * hid), BF),
            shape_of((frames * fields, (frames + 2) * 9 * hid), BF),
            shape_of((6 * hid, 4 * 3 * chans), BF),
            shape_of((6 * hid, 4 * 3 * hid), BF),
            shape_of((frames * 3 * fields, (frames + 2) * 3 * hid), BF),
            shape_of((hid, 1), F32),
            shape_of((hid, 1), F32),
            shape_of((fields, 1), F32),
            shape_of((frames, LANES), F32),
            shape_of((-(-3 * frames // 16) * 16, (frames + 2) * 3 * hid), BF),
        ),
        [VMEM] * 4,
        [pltpu.VMEM((2, w.shape[1], 27 * hid + LANES // 2), BF) for w in (w2, w3)],
        cost=1_000_000_000,
    )(w1, w2, w3, small)


def beside(near_ref, far_ref):
    step, last = lax.axis_index("tm"), lax.axis_size("tm") - 1
    even = is_even("tm")
    for f in range(DEPTH):
        for y in range(near_ref.shape[2] // LANES):
            a, b = near_ref[f, :, tile(y)], far_ref[f, :, tile(y)]
            none = jnp.zeros_like(a)
            yield f, y, jnp.where(step > 0, jnp.where(even, b, a), none)
            yield DEPTH + f, y, jnp.where(step < last, jnp.where(even, a, b), none)


def strips(rows_of_frames, count):
    begun = {}
    for f, y, v in rows_of_frames:
        lane = lanes(v.shape)
        group, place = lane // PITCH, lane % PITCH
        west, east = begun.pop(f, (jnp.zeros_like(v), jnp.zeros_like(v)))
        here = group == y
        west = jnp.where(here & (place >= DEPTH), turn(v, y * PITCH + DEPTH), west)
        east = jnp.where(here & (place < PITCH - DEPTH), turn(v, y * PITCH + PITCH - DEPTH), east)
        if y == count - 1:
            yield f, west, east
        else:
            begun[f] = west, east


def edges_kernel(own_west_ref, own_east_ref, far_ref, near_ref, west_ref, east_ref, send2_ref, send1_ref):
    frames = own_west_ref.shape[0]
    even = is_even("space")

    def put(f, west, east):
        west_ref[f], east_ref[f] = west, east
        send1_ref[f], send2_ref[f] = jnp.where(even, east, west), jnp.where(even, west, east)

    for f in range(frames):
        put(DEPTH + f, own_west_ref[f], own_east_ref[f])
    for f, west, east in strips(beside(near_ref, far_ref), near_ref.shape[2] // LANES):
        put(f if f < DEPTH else f + frames, west, east)


def make_edges(own_west, own_east, near, far):
    frames, chans, _ = own_west.shape
    strip = shape_of((frames + 2 * DEPTH, chans, LANES), BF)
    return call(edges_kernel, "edges", (strip,) * 4, [VMEM] * 4)(own_west, own_east, far, near)


def spread(dst, f, y, v):
    chans = v.shape[0]
    at = tile(y + 1)
    dst[f, 0:chans, at] = turn(v, 1)
    dst[f, chans : 2 * chans, at] = v
    dst[f, 2 * chans : 3 * chans, at] = turn(v, -1)


def window(src, frames, y):
    parts = []
    for f in frames:
        ref, at = src(f)
        for dy in range(3):
            parts.append(ref[at, :, (y + dy) * LANES : (y + dy + 2) * LANES])
    return jnp.concatenate(parts, axis=0)


def plain(ref):
    return lambda f: (ref, f)


def split(own, far, count=None):
    count = own.shape[0] if count is None else count
    return lambda f: (own, f - DEPTH) if DEPTH <= f < DEPTH + count else (far, f if f < DEPTH else f - count)


def in_trajectory(local, frames):
    step = lax.axis_index("tm") * frames + local
    return (step >= 0) & (step < frames * lax.axis_size("tm"))


def blank_ends(*refs):
    for s in refs:
        s[:, :, tile(0)] = jnp.zeros(s.shape[:2] + (LANES,), BF)
        last = s.shape[2] // LANES - 1
        s[:, :, tile(last)] = jnp.zeros(s.shape[:2] + (LANES,), BF)


def layer(src, dst, m_ref, c_ref, groups, rows, keep):
    hid = c_ref.shape[0]
    for f, count in groups:
        weights = m_ref[...] if count == 2 else m_ref[0:hid, 0 : m_ref.shape[1] // 4 * 3]
        for y in range(0, rows, 2):
            acc = jnp.dot(weights, window(src, range(f, f + count + 2), y), preferred_element_type=F32)
            for p in range(count):
                h = silu(acc[p * hid : (p + 1) * hid] + c_ref[...]).astype(BF)
                inside = keep(f + p)
                h = h if inside is None else jnp.where(inside, h, jnp.zeros_like(h))
                ref, at = dst(f + p)
                spread(ref, at, y, h[:, tile(0)])
                spread(ref, at, y + 1, h[:, tile(1)])


def pairs_of(frames):
    groups = [(f, 2) for f in range(frames[0], frames[-1], 2)]
    return groups + [(frames[-1], 1)] * (len(frames) % 2)


def inner_kernel(own_ref, m1_ref, m2_ref, c1_ref, c2_ref, s1, s2, s3, west_ref, east_ref):
    frames = own_ref.shape[0]
    rows = own_ref.shape[2] // LANES
    each = [(f, y, own_ref[f, :, tile(y)]) for f in range(frames) for y in range(rows)]
    blank_ends(s1, s2, s3)
    for f, y, v in each:
        spread(s1, f, y, v)
    for f, west, east in strips(each, rows):
        west_ref[f], east_ref[f] = west, east
    layer(plain(s1), plain(s2), m1_ref, c1_ref, pairs_of(range(frames - 2)), rows, lambda f: None)
    layer(plain(s2), plain(s3), m2_ref, c2_ref, pairs_of(range(frames - 4)), rows, lambda f: None)


def make_inner(own, m1, m2, c1, c2):
    frames, chans, width = own.shape
    hid, wide = c1.shape[0], width + 2 * LANES
    strip = shape_of((frames, chans, LANES), BF)
    return call(
        inner_kernel,
        "inner",
        (
            shape_of((frames, 3 * chans, wide), BF),
            shape_of((frames - 2, 3 * hid, wide), BF),
            shape_of((frames - 4, 3 * hid, wide), BF),
            strip,
            strip,
        ),
        [VMEM] * 5,
        cost=1_500_000_000,
    )(own, m1, m2, c1, c2)


def main_kernel(own1, own2, far_ref, near_ref, m1_ref, m2_ref, c1_ref, c2_ref, s3, far1, far2):
    frames = own1.shape[0]
    rows = near_ref.shape[2] // LANES
    blank_ends(far1, far2, s3)
    for f, y, v in beside(near_ref, far_ref):
        spread(far1, f, y, v)

    one, two, three = split(own1, far1), split(own2, far2), split(None, s3, frames - 4)
    groups = pairs_of(range(DEPTH)) + pairs_of(range(frames + 1, frames + 4))
    layer(one, two, m1_ref, c1_ref, groups, rows, lambda f: in_trajectory(f - 2, frames))
    groups = pairs_of(range(DEPTH)) + pairs_of(range(frames - 1, frames + 2))
    layer(two, three, m2_ref, c2_ref, groups, rows, lambda f: in_trajectory(f - 1, frames))


def make_main(own1, own2, near, far, m1, m2, c1, c2):
    frames, rows1, wide = own1.shape
    rows2 = own2.shape[1]
    return call(
        main_kernel,
        "main",
        (shape_of((2 * DEPTH, rows2, wide), BF),),
        [VMEM] * 8,
        [pltpu.VMEM((2 * DEPTH, rows1, wide), BF), pltpu.VMEM((2 * DEPTH, rows2, wide), BF)],
        cost=5_000_000_000,
    )(own1, own2, far, near, m1, m2, c1, c2)[0]


def spread_side(dst, f, v):
    chans = v.shape[0]
    for half in range(2):
        w = v[:, tile(half)]
        dst[f, 0:chans, tile(half)] = turn(w, 1)
        dst[f, chans : 2 * chans, tile(half)] = w
        dst[f, 2 * chans : 3 * chans, tile(half)] = turn(w, -1)


def three_rows(up, mid, down):
    lane = lanes(mid.shape)
    up = jnp.where(lane >= PITCH, turn(up, PITCH), 0.0)
    down = jnp.where(lane < LANES - PITCH, turn(down, -PITCH), 0.0)
    return mid + up + down


def over_rows(acc, at, outs):
    halves = []
    for half in range(2):
        up, mid, down = (acc[at + d * outs : at + (d + 1) * outs, tile(half)] for d in range(3))
        halves.append(three_rows(up, mid, down))
    return jnp.concatenate(halves, axis=1)


def patched(v, west, east, y):
    col = lanes(v.shape)
    v = jnp.where(col < DEPTH, turn(west, -(y * PITCH + DEPTH)), v)
    return jnp.where(col >= LANES - DEPTH, turn(east, DEPTH - (y + 1) * PITCH), v)


def side_kernel(
    own3, far3, west_ref, east_ref, second_ref, first_ref, s1_ref, s2_ref, head_ref, c1_ref, c2_ref, c3_ref,
    state_ref, day_ref, t3, part_ref, t1, t2, own, ends,
):
    frames, fields, rows, _ = state_ref.shape
    chans, hid = west_ref.shape[1], c1_ref.shape[0]
    place = lanes((chans, LANES)) % PITCH
    even = is_even("space")
    me, last = lax.axis_index("space"), lax.axis_size("space") - 1
    none = jnp.zeros((chans, LANES), BF)
    for f in range(frames + 2 * DEPTH):
        a, b = first_ref[f], second_ref[f]
        a, b = jnp.where(even, b, a), jnp.where(even, a, b)
        a, b = jnp.where(me > 0, a, none), jnp.where(me < last, b, none)
        west = jnp.where(place < DEPTH, turn(a, 2 * DEPTH - PITCH), west_ref[f])
        east = jnp.where(place >= PITCH - DEPTH, turn(b, PITCH - 2 * DEPTH), east_ref[f])
        spread_side(t1, f, jnp.concatenate([west, east], axis=1))

    pair = lanes((1, 2 * LANES))
    place = pair % PITCH
    outside = ((pair < LANES) & (place < DEPTH) & (me == 0)) | (
        (pair >= LANES) & (place >= PITCH - DEPTH) & (me == last)
    )

    def layer(src, dst, m_ref, bias, count, first):
        for f in range(0, count, 2):
            z = jnp.concatenate([src[f + j] for j in range(4)], axis=0)
            for p in range(2):
                acc = jnp.dot(m_ref[p * 3 * hid : (p + 1) * 3 * hid], z, preferred_element_type=F32)
                h = silu(over_rows(acc, 0, hid) + bias)
                keep = in_trajectory(f + p + first, frames) & ~outside
                spread_side(dst, f + p, jnp.where(keep, h, 0.0).astype(BF))

    layer(t1, t2, s1_ref, c1_ref[...], frames + 4, -2)
    layer(t2, t3, s2_ref, c2_ref[...], frames + 2, -1)
    own[0] = jnp.zeros(own.shape[1:], F32)
    own[rows + 1] = jnp.zeros(own.shape[1:], F32)
    for y in range(0, rows, 2):
        places = [split(own3, far3)(j) for j in range(frames + 2)]
        z = jnp.concatenate([ref[at, :, (y + 1) * LANES : (y + 3) * LANES] for ref, at in places], axis=0)
        acc = jnp.dot(head_ref[...], z, preferred_element_type=F32)
        own[y + 1], own[y + 2] = acc[:, tile(0)], acc[:, tile(1)]
    z = jnp.concatenate([t3[j] for j in range(frames + 2)], axis=0)
    acc = jnp.dot(head_ref[...], z, preferred_element_type=F32)
    ends[0], ends[1] = acc[:, tile(0)], acc[:, tile(1)]
    offsets = [pl.ds(dy, frames, stride=3) for dy in range(3)]
    west, east = (three_rows(*(ends[half, at] for at in offsets)) for half in range(2))
    days = part_ref.shape[0]
    day = day_ref[...]
    for y in range(rows):
        v = patched(sum(own[y + dy, offsets[dy]] for dy in range(3)), west, east, y)
        for d in range(days):
            part_ref[d, y : y + 1, :] = jnp.sum(jnp.where(day == d, v, 0.0), axis=0, keepdims=True)
    base = c3_ref[0:1, 0:1]
    for d in range(days):
        total = 0.5 * part_ref[d]
        for f in range(frames):
            total = total + jnp.where(day[f : f + 1] == d, state_ref[f, 0].astype(F32) + 0.5 * base, 0.0)
        part_ref[d] = total


def make_side(own3, far3, west, east, first, second, s1, s2, head, c1, c2, c3, state, day, days):
    frames, fields, rows, _ = state.shape
    chans, hid = west.shape[1], c1.shape[0]
    return call(
        side_kernel,
        "side",
        (shape_of((frames + 2, 3 * hid, 2 * LANES), BF), shape_of((days, rows, LANES), F32)),
        [VMEM] * 14,
        [
            pltpu.VMEM((frames + 6, 3 * chans, 2 * LANES), BF),
            pltpu.VMEM((frames + 4, 3 * hid, 2 * LANES), BF),
            pltpu.VMEM((rows + 2, head.shape[0], LANES), F32),
            pltpu.VMEM((2, head.shape[0], LANES), F32),
        ],
    )(own3, far3, west, east, second, first, s1, s2, head, c1, c2, c3, state, day)


def own_score(own3, far3, m3_ref, frames, y):
    acc = jnp.dot(m3_ref[...], window(split(own3, far3), range(frames + 2), y), preferred_element_type=F32)
    return acc[:, tile(0)], acc[:, tile(1)]


def early_kernel(own3, far3, t3, m3_ref, s3_ref, score_ref, side_ref):
    frames = t3.shape[0] - 2
    fields = m3_ref.shape[0] // frames
    for y in range(0, score_ref.shape[0], 2):
        score_ref[y], score_ref[y + 1] = own_score(own3, far3, m3_ref, frames, y)
    z = jnp.concatenate([t3[j] for j in range(frames + 2)], axis=0)
    acc = jnp.dot(s3_ref[...], z, preferred_element_type=F32)
    for f in range(frames):
        both = over_rows(acc, f * 3 * fields, fields)
        for half in range(2):
            side_ref[half, f * fields : (f + 1) * fields] = both[:, tile(half)]


def make_early(own3, far3, t3, m3, s3, count):
    return call(
        early_kernel,
        "early",
        (shape_of((count, m3.shape[0], LANES), F32), shape_of((2, m3.shape[0], LANES), F32)),
        [VMEM] * 5,
        cost=1_000_000_000,
    )(own3, far3, t3, m3, s3)


def update_kernel(own3, far3, m3_ref, score_ref, side_ref, c3_ref, state_ref, noise_ref, out_ref, head_ref, rest, scr):
    frames, fields, rows, _ = state_ref.shape
    done = score_ref.shape[0]
    for y in range(done, rows, 2):
        rest[y - done], rest[y - done + 1] = own_score(own3, far3, m3_ref, frames, y)
    bias = c3_ref[...]
    for f in range(frames):
        at = slice(f * fields, (f + 1) * fields)
        west, east = side_ref[0, at], side_ref[1, at]
        for y in range(rows):
            v = score_ref[y, at] if y < done else rest[y - done, at]
            scr[f, pl.ds(y, fields, stride=rows), :] = patched(v, west, east, y) + bias
        score = scr[f].reshape(fields, rows, LANES)
        moved = state_ref[f].astype(F32) + 0.8 * score + 0.5 * noise_ref[f].astype(F32)
        out_ref[f] = moved.astype(BF)
        head_ref[f] = moved[0]


def make_update(own3, far3, m3, score, side, c3, state, noise):
    frames, fields, rows, _ = state.shape
    return call(
        update_kernel,
        "update",
        (shape_of(state.shape, BF), shape_of((frames, rows, LANES), F32)),
        [VMEM] * 8,
        [
            pltpu.VMEM((rows - score.shape[0], frames * fields, LANES), F32),
            pltpu.VMEM((frames, fields * rows, LANES), F32),
        ],
        cost=2_000_000_000,
    )(own3, far3, m3, score, side, c3, state, noise)


def correct_kernel(mine_ref, theirs_ref, observed_ref, mask_ref, head_ref, day_ref, _, out_ref, buf, sem):
    frames = head_ref.shape[0]
    days = observed_ref.shape[0]
    mask = mask_ref[...].astype(F32)
    misfit = [0.15 * (mask * (mine_ref[d] + theirs_ref[d] - observed_ref[d])) for d in range(days)]
    for f in range(frames):
        v = head_ref[f]
        for d in range(days):
            v = v - jnp.where(day_ref[f : f + 1] == d, misfit[d], 0.0)
        buf[f, 0] = v.astype(BF)
    copy = pltpu.make_async_copy(buf, out_ref.at[:, 0:1], sem)
    copy.start()
    copy.wait()


def make_correct(mine, theirs, observed, mask, head, day, out):
    frames, rows, _ = head.shape
    return call(
        correct_kernel,
        "correct",
        (shape_of(out.shape, BF),),
        [VMEM] * 6 + [ANYWHERE],
        [pltpu.VMEM((frames, 1, rows, LANES), BF), pltpu.SemaphoreType.DMA],
        alias={6: 0},
        out_specs=(ANYWHERE,),
    )(mine, theirs, observed, mask, head, day, out)[0]


def swapped(value, axis, start):
    sizes = {name: lax.axis_size(name) for name in ("tm", "space")}
    other = "space" if axis == "tm" else "tm"
    pairs = []
    for t in range(sizes["tm"]):
        for s in range(sizes["space"]):
            to = {"tm": t, "space": s}
            to[axis] += 1 if to[axis] % 2 == start else -1
            if not 0 <= to[axis] < sizes[axis]:
                to = {"tm": t, "space": s}
                to[other] ^= 1
            pairs.append((t * sizes["space"] + s, to["tm"] * sizes["space"] + to["space"]))
    return lax.ppermute(value, ("tm", "space"), pairs)


def body(
    state, noise, conv_one, bias_one, conv_two, bias_two, conv_three, bias_three, day_of_frame, observed, obs_mask
):
    state, noise = state[:, :, 0], noise[:, :, 0]
    hid, chans = conv_one.shape[:2]
    fields = conv_three.shape[0]
    w1 = conv_one.transpose(2, 3, 4, 1, 0).reshape(27 * chans, hid)
    w2 = conv_two.transpose(2, 3, 4, 0, 1).reshape(27, hid, hid)
    w3 = conv_three.transpose(2, 3, 4, 0, 1).reshape(27, fields, hid)
    own, send2, send1 = make_rows(state)
    far = swapped(send2, "tm", 1)
    near = swapped(send1, "tm", 0)
    small = jnp.concatenate([bias_one, bias_two, bias_three, day_of_frame.astype(F32)])[None]
    m1, m2, m3, s1, s2, s3, c1, c2, c3, days, head = make_weights(w1, w2, w3, small, state.shape[0])
    own1, own2, own3, west, east = make_inner(own, m1, m2, c1, c2)
    west, east, send2, send1 = make_edges(west, east, near, far)
    second = swapped(send2, "space", 1)
    first = swapped(send1, "space", 0)
    far3 = make_main(own1, own2, near, far, m1, m2, c1, c2)
    t3, mine = make_side(
        own3, far3, west, east, first, second, s1, s2, head, c1, c2, c3, state, days, observed.shape[0]
    )
    score, side = make_early(own3, far3, t3, m3, s3, EARLY)
    out, first = make_update(own3, far3, m3, score, side, c3, state, noise)
    count = lax.axis_size("tm")
    reach = 1
    while True:
        theirs = lax.ppermute(mine, "tm", [(i, i ^ reach) for i in range(count)])
        reach *= 2
        if reach >= count:
            break
        mine = mine + theirs
    out = make_correct(mine, theirs, observed[:, 0], obs_mask[0], first, days, out)
    return out[:, :, None]


def solution(mesh):
    in_specs = (
        P("tm", None, "space", None, None),
        P("tm", None, "space", None, None),
        P(),
        P(),
        P(),
        P(),
        P(),
        P(),
        P("tm"),
        P(None, "space", None, None),
        P("space", None, None),
    )
    out_specs = P("tm", None, "space", None, None)
    return jax.shard_map(body, mesh=mesh, in_specs=in_specs, out_specs=out_specs, check_vma=False)
```

```python
import functools

import jax
import jax.numpy as jnp
from jax import lax
from jax.experimental import pallas as pl
from jax.experimental.pallas import tpu as pltpu
from jax.sharding import PartitionSpec as P

BF = jnp.bfloat16
F32 = jnp.float32
LANES = 128
DEPTH = 3
PITCH = 16
VMEM = pl.BlockSpec(memory_space=pltpu.VMEM)
ANYWHERE = pl.BlockSpec(memory_space=pltpu.HBM)
LIMIT = 24 * 1024 * 1024


def shape_of(dims, kind):
    return jax.ShapeDtypeStruct(dims, kind)


def call(kernel, name, outs, specs, scratch=(), cost=None, alias=None, out_specs=None):
    return pl.pallas_call(
        kernel,
        out_shape=outs,
        in_specs=specs,
        out_specs=out_specs or (VMEM,) * len(outs),
        scratch_shapes=list(scratch),
        input_output_aliases=alias or {},
        compiler_params=pltpu.CompilerParams(vmem_limit_bytes=LIMIT),
        cost_estimate=cost and pl.CostEstimate(flops=cost, bytes_accessed=1_000_000, transcendentals=0),
        name=name,
    )


def silu(v):
    half = 0.5 * v
    return half + half * jnp.tanh(half)


def lanes(shape):
    return lax.broadcasted_iota(jnp.int32, shape, len(shape) - 1)


def turn(v, steps):
    steps = steps % LANES
    return pltpu.roll(v, steps, 1) if steps else v


def tile(i):
    return slice(i * LANES, (i + 1) * LANES)


def is_even(axis):
    return lax.axis_index(axis) % 2 == 0


def rows_kernel(state_ref, own_ref, far_ref, near_ref, scr):
    frames, chans, rows, _ = state_ref.shape
    for f in range(frames):
        scr[f] = state_ref[f].astype(F32).reshape(chans * rows, LANES)
        for y in range(rows):
            v = scr[f, pl.ds(y, chans, stride=rows), :].astype(BF)
            own_ref[f, :, tile(y)] = v
    even = is_even("tm")
    for f in range(DEPTH):
        low, high = own_ref[f], own_ref[frames - DEPTH + f]
        near_ref[f], far_ref[f] = jnp.where(even, high, low), jnp.where(even, low, high)


def make_rows(state):
    frames, chans, rows, _ = state.shape
    slab = shape_of((DEPTH, chans, rows * LANES), BF)
    return call(
        rows_kernel,
        "rows",
        (shape_of((frames, chans, rows * LANES), BF), slab, slab),
        [VMEM],
        [pltpu.VMEM((frames, chans * rows, LANES), F32)],
        cost=4_000_000_000,
    )(state)


def weights_kernel(
    w1_ref, w2_ref, w3_ref, small_ref,
    m1_ref, m2_ref, m3_ref, s1_ref, s2_ref, s3_ref, c1_ref, c2_ref, c3_ref, days_ref, head_ref, f2, f3,
):
    small = jnp.broadcast_to(small_ref[...], (8, small_ref.shape[1])).T[:, 0:1]
    at = 0
    for ref in (c1_ref, c2_ref, c3_ref, days_ref):
        ref[...] = jnp.broadcast_to(small[at : at + ref.shape[0]], ref.shape)
        at += ref.shape[0]
    for ref in (m1_ref, m2_ref, m3_ref, s1_ref, s2_ref, s3_ref):
        ref[...] = jnp.zeros_like(ref)
    hid, fields, chans = w2_ref.shape[1], w3_ref.shape[1], w1_ref.shape[0] // 27
    frames = days_ref.shape[0]
    flat = w1_ref[...].astype(F32).T.astype(BF)
    for p in range(2):
        m1_ref[p * hid : (p + 1) * hid, p * 9 * chans : (p + 3) * 9 * chans] = flat
        for dt in range(3):
            for dy in range(3):
                at = (dt * 3 + dy) * 3 * chans
                s1_ref[(p * 3 + dy) * hid : (p * 3 + dy + 1) * hid, (dt + p) * 3 * chans : (dt + p + 1) * 3 * chans] = (
                    flat[:, at : at + 3 * chans]
                )

    def place(raw, flat, main, side, count, outs):
        half = LANES // 2
        for t in range(27):
            for k in range(2):
                flat[k, :, t * hid + k * half : (t + 1) * hid + k * half] = raw[t]
        for p in range(count):
            rows, at = slice(p * outs, (p + 1) * outs), p * 9 * hid
            k = at % LANES // half
            main[rows, at : at + 27 * hid] = flat[k, :, k * half : k * half + 27 * hid]
            for dt in range(3):
                for dy in range(3):
                    rows = slice((p * 3 + dy) * outs, (p * 3 + dy + 1) * outs)
                    at, src = (dt + p) * 3 * hid, (dt * 3 + dy) * 3 * hid
                    k = (at - src) % LANES // half
                    side[rows, at : at + 3 * hid] = flat[k, :, src + k * half : src + k * half + 3 * hid]

    place(w2_ref, f2, m2_ref, s2_ref, 2, hid)
    place(w3_ref, f3, m3_ref, s3_ref, frames, fields)
    shape = (head_ref.shape[0], s3_ref.shape[0])
    pick = lanes(shape) == fields * lax.broadcasted_iota(jnp.int32, shape, 0)
    head_ref[...] = jnp.dot(pick.astype(F32).astype(BF), s3_ref[...], preferred_element_type=F32).astype(BF)


def make_weights(w1, w2, w3, small, frames):
    hid, fields, chans = w2.shape[1], w3.shape[1], w1.shape[0] // 27
    return call(
        weights_kernel,
        "weights",
        (
            shape_of((2 * hid, 4 * 9 * chans), BF),
            shape_of((2 * hid, 4 * 9 * hid), BF),
            shape_of((frames * fields, (frames + 2) * 9 * hid), BF),
            shape_of((6 * hid, 4 * 3 * chans), BF),
            shape_of((6 * hid, 4 * 3 * hid), BF),
            shape_of((frames * 3 * fields, (frames + 2) * 3 * hid), BF),
            shape_of((hid, 1), F32),
            shape_of((hid, 1), F32),
            shape_of((fields, 1), F32),
            shape_of((frames, LANES), F32),
            shape_of((-(-3 * frames // 16) * 16, (frames + 2) * 3 * hid), BF),
        ),
        [VMEM] * 4,
        [pltpu.VMEM((2, w.shape[1], 27 * hid + LANES // 2), BF) for w in (w2, w3)],
        cost=1_000_000_000,
    )(w1, w2, w3, small)


def beside(near_ref, far_ref):
    step, last = lax.axis_index("tm"), lax.axis_size("tm") - 1
    even = is_even("tm")
    for f in range(DEPTH):
        for y in range(near_ref.shape[2] // LANES):
            a, b = near_ref[f, :, tile(y)], far_ref[f, :, tile(y)]
            none = jnp.zeros_like(a)
            yield f, y, jnp.where(step > 0, jnp.where(even, b, a), none)
            yield DEPTH + f, y, jnp.where(step < last, jnp.where(even, a, b), none)


def strips(rows_of_frames, count):
    begun = {}
    for f, y, v in rows_of_frames:
        lane = lanes(v.shape)
        group, place = lane // PITCH, lane % PITCH
        west, east = begun.pop(f, (jnp.zeros_like(v), jnp.zeros_like(v)))
        here = group == y
        west = jnp.where(here & (place >= DEPTH), turn(v, y * PITCH + DEPTH), west)
        east = jnp.where(here & (place < PITCH - DEPTH), turn(v, y * PITCH + PITCH - DEPTH), east)
        if y == count - 1:
            yield f, west, east
        else:
            begun[f] = west, east


def edges_kernel(own_west_ref, own_east_ref, far_ref, near_ref, west_ref, east_ref, send1_ref, send2_ref):
    frames = own_west_ref.shape[0]
    even = is_even("space")

    def put(f, west, east):
        west_ref[f], east_ref[f] = west, east
        send1_ref[f], send2_ref[f] = jnp.where(even, east, west), jnp.where(even, west, east)

    for f in range(frames):
        put(DEPTH + f, own_west_ref[f], own_east_ref[f])
    for f, west, east in strips(beside(near_ref, far_ref), near_ref.shape[2] // LANES):
        put(f if f < DEPTH else f + frames, west, east)


def make_edges(own_west, own_east, near, far):
    frames, chans, _ = own_west.shape
    strip = shape_of((frames + 2 * DEPTH, chans, LANES), BF)
    return call(edges_kernel, "edges", (strip,) * 4, [VMEM] * 4)(own_west, own_east, far, near)


def spread(dst, f, y, v):
    chans = v.shape[0]
    at = tile(y + 1)
    dst[f, 0:chans, at] = turn(v, 1)
    dst[f, chans : 2 * chans, at] = v
    dst[f, 2 * chans : 3 * chans, at] = turn(v, -1)


def window(src, frames, y):
    parts = []
    for f in frames:
        ref, at = src(f)
        for dy in range(3):
            parts.append(ref[at, :, (y + dy) * LANES : (y + dy + 2) * LANES])
    return jnp.concatenate(parts, axis=0)


def plain(ref):
    return lambda f: (ref, f)


def in_trajectory(local, frames):
    step = lax.axis_index("tm") * frames + local
    return (step >= 0) & (step < frames * lax.axis_size("tm"))


def blank_ends(*refs):
    for s in refs:
        s[:, :, tile(0)] = jnp.zeros(s.shape[:2] + (LANES,), BF)
        last = s.shape[2] // LANES - 1
        s[:, :, tile(last)] = jnp.zeros(s.shape[:2] + (LANES,), BF)


def layer(src, dst, m_ref, c_ref, groups, rows, keep):
    hid = c_ref.shape[0]
    for f, count in groups:
        weights = m_ref[...] if count == 2 else m_ref[0:hid, 0 : m_ref.shape[1] // 4 * 3]
        for y in range(0, rows, 2):
            acc = jnp.dot(weights, window(src, range(f, f + count + 2), y), preferred_element_type=F32)
            for p in range(count):
                h = silu(acc[p * hid : (p + 1) * hid] + c_ref[...]).astype(BF)
                inside = keep(f + p)
                h = h if inside is None else jnp.where(inside, h, jnp.zeros_like(h))
                ref, at = dst(f + p)
                spread(ref, at, y, h[:, tile(0)])
                spread(ref, at, y + 1, h[:, tile(1)])


def pairs_of(frames):
    groups = [(f, 2) for f in range(frames[0], frames[-1], 2)]
    return groups + [(frames[-1], 1)] * (len(frames) % 2)


def inner_kernel(own_ref, m1_ref, c1_ref, s1, s2, west_ref, east_ref):
    frames = own_ref.shape[0]
    rows = own_ref.shape[2] // LANES
    each = [(f, y, own_ref[f, :, tile(y)]) for f in range(frames) for y in range(rows)]
    blank_ends(s1, s2)
    for f, y, v in each:
        spread(s1, f, y, v)
    for f, west, east in strips(each, rows):
        west_ref[f], east_ref[f] = west, east
    layer(plain(s1), plain(s2), m1_ref, c1_ref, pairs_of(range(frames - 2)), rows, lambda f: None)


def make_inner(own, m1, c1):
    frames, chans, width = own.shape
    hid, wide = c1.shape[0], width + 2 * LANES
    strip = shape_of((frames, chans, LANES), BF)
    return call(
        inner_kernel,
        "inner",
        (shape_of((frames, 3 * chans, wide), BF), shape_of((frames - 2, 3 * hid, wide), BF), strip, strip),
        [VMEM] * 3,
        cost=1_000_000_000,
    )(own, m1, c1)


def main_kernel(own1, own2, far_ref, near_ref, m1_ref, m2_ref, c1_ref, c2_ref, s3, far1, far2):
    frames = own1.shape[0]
    rows = near_ref.shape[2] // LANES
    blank_ends(far1, far2, s3)
    for f, y, v in beside(near_ref, far_ref):
        spread(far1, f, y, v)

    def split(own, far, edge):
        count = own.shape[0]
        return lambda f: (own, f - edge) if edge <= f < edge + count else (far, f if f < edge else f - count)

    one, two = split(own1, far1, DEPTH), split(own2, far2, DEPTH)
    groups = pairs_of(range(DEPTH)) + pairs_of(range(frames + 1, frames + 4))
    layer(one, two, m1_ref, c1_ref, groups, rows, lambda f: in_trajectory(f - 2, frames))
    layer(two, plain(s3), m2_ref, c2_ref, pairs_of(range(frames + 2)), rows, lambda f: in_trajectory(f - 1, frames))


def make_main(own1, own2, near, far, m1, m2, c1, c2):
    frames, rows1, wide = own1.shape
    rows2 = own2.shape[1]
    return call(
        main_kernel,
        "main",
        (shape_of((frames + 2, rows2, wide), BF),),
        [VMEM] * 8,
        [pltpu.VMEM((2 * DEPTH, rows1, wide), BF), pltpu.VMEM((2 * DEPTH, rows2, wide), BF)],
        cost=5_000_000_000,
    )(own1, own2, far, near, m1, m2, c1, c2)[0]


def spread_side(dst, f, v):
    chans = v.shape[0]
    for half in range(2):
        w = v[:, tile(half)]
        dst[f, 0:chans, tile(half)] = turn(w, 1)
        dst[f, chans : 2 * chans, tile(half)] = w
        dst[f, 2 * chans : 3 * chans, tile(half)] = turn(w, -1)


def three_rows(up, mid, down):
    lane = lanes(mid.shape)
    up = jnp.where(lane >= PITCH, turn(up, PITCH), 0.0)
    down = jnp.where(lane < LANES - PITCH, turn(down, -PITCH), 0.0)
    return mid + up + down


def over_rows(acc, at, outs):
    halves = []
    for half in range(2):
        up, mid, down = (acc[at + d * outs : at + (d + 1) * outs, tile(half)] for d in range(3))
        halves.append(three_rows(up, mid, down))
    return jnp.concatenate(halves, axis=1)


def patched(v, west, east, y):
    col = lanes(v.shape)
    v = jnp.where(col < DEPTH, turn(west, -(y * PITCH + DEPTH)), v)
    return jnp.where(col >= LANES - DEPTH, turn(east, DEPTH - (y + 1) * PITCH), v)


def side_kernel(
    wide_ref, west_ref, east_ref, first_ref, second_ref, s1_ref, s2_ref, head_ref, c1_ref, c2_ref, c3_ref,
    state_ref, day_ref, t3, part_ref, t1, t2, own, ends,
):
    frames, fields, rows, _ = state_ref.shape
    chans, hid = west_ref.shape[1], c1_ref.shape[0]
    place = lanes((chans, LANES)) % PITCH
    even = is_even("space")
    me, last = lax.axis_index("space"), lax.axis_size("space") - 1
    none = jnp.zeros((chans, LANES), BF)
    for f in range(frames + 2 * DEPTH):
        a, b = first_ref[f], second_ref[f]
        a, b = jnp.where(even, b, a), jnp.where(even, a, b)
        a, b = jnp.where(me > 0, a, none), jnp.where(me < last, b, none)
        west = jnp.where(place < DEPTH, turn(a, 2 * DEPTH - PITCH), west_ref[f])
        east = jnp.where(place >= PITCH - DEPTH, turn(b, PITCH - 2 * DEPTH), east_ref[f])
        spread_side(t1, f, jnp.concatenate([west, east], axis=1))

    pair = lanes((1, 2 * LANES))
    place = pair % PITCH
    outside = ((pair < LANES) & (place < DEPTH) & (me == 0)) | (
        (pair >= LANES) & (place >= PITCH - DEPTH) & (me == last)
    )

    def layer(src, dst, m_ref, bias, count, first):
        for f in range(0, count, 2):
            z = jnp.concatenate([src[f + j] for j in range(4)], axis=0)
            for p in range(2):
                acc = jnp.dot(m_ref[p * 3 * hid : (p + 1) * 3 * hid], z, preferred_element_type=F32)
                h = silu(over_rows(acc, 0, hid) + bias)
                keep = in_trajectory(f + p + first, frames) & ~outside
                spread_side(dst, f + p, jnp.where(keep, h, 0.0).astype(BF))

    layer(t1, t2, s1_ref, c1_ref[...], frames + 4, -2)
    layer(t2, t3, s2_ref, c2_ref[...], frames + 2, -1)
    own[0] = jnp.zeros(own.shape[1:], F32)
    own[rows + 1] = jnp.zeros(own.shape[1:], F32)
    for y in range(0, rows, 2):
        z = jnp.concatenate([wide_ref[j, :, (y + 1) * LANES : (y + 3) * LANES] for j in range(frames + 2)], axis=0)
        acc = jnp.dot(head_ref[...], z, preferred_element_type=F32)
        own[y + 1], own[y + 2] = acc[:, tile(0)], acc[:, tile(1)]
    z = jnp.concatenate([t3[j] for j in range(frames + 2)], axis=0)
    acc = jnp.dot(head_ref[...], z, preferred_element_type=F32)
    ends[0], ends[1] = acc[:, tile(0)], acc[:, tile(1)]
    offsets = [pl.ds(dy, frames, stride=3) for dy in range(3)]
    west, east = (three_rows(*(ends[half, at] for at in offsets)) for half in range(2))
    days = part_ref.shape[0]
    day = day_ref[...]
    for y in range(rows):
        v = patched(sum(own[y + dy, offsets[dy]] for dy in range(3)), west, east, y)
        for d in range(days):
            part_ref[d, y : y + 1, :] = jnp.sum(jnp.where(day == d, v, 0.0), axis=0, keepdims=True)
    base = c3_ref[0:1, 0:1]
    for d in range(days):
        total = 0.5 * part_ref[d]
        for f in range(frames):
            total = total + jnp.where(day[f : f + 1] == d, state_ref[f, 0].astype(F32) + 0.5 * base, 0.0)
        part_ref[d] = total


def make_side(wide, west, east, first, second, s1, s2, head, c1, c2, c3, state, day, days):
    frames, fields, rows, _ = state.shape
    chans, hid = west.shape[1], c1.shape[0]
    return call(
        side_kernel,
        "side",
        (shape_of((frames + 2, 3 * hid, 2 * LANES), BF), shape_of((days, rows, LANES), F32)),
        [VMEM] * 13,
        [
            pltpu.VMEM((frames + 6, 3 * chans, 2 * LANES), BF),
            pltpu.VMEM((frames + 4, 3 * hid, 2 * LANES), BF),
            pltpu.VMEM((rows + 2, head.shape[0], LANES), F32),
            pltpu.VMEM((2, head.shape[0], LANES), F32),
        ],
    )(wide, west, east, first, second, s1, s2, head, c1, c2, c3, state, day)


def own_score(wide_ref, m3_ref, frames, y):
    acc = jnp.dot(m3_ref[...], window(plain(wide_ref), range(frames + 2), y), preferred_element_type=F32)
    return acc[:, tile(0)], acc[:, tile(1)]


def update_kernel(
    wide_ref, t3, m3_ref, s3_ref, c3_ref, state_ref, noise_ref, out_ref, head_ref, rest, side, scr
):
    frames, fields, rows, _ = state_ref.shape
    z = jnp.concatenate([t3[j] for j in range(frames + 2)], axis=0)
    acc = jnp.dot(s3_ref[...], z, preferred_element_type=F32)
    for f in range(frames):
        both = over_rows(acc, f * 3 * fields, fields)
        for half in range(2):
            side[half, f * fields : (f + 1) * fields] = both[:, tile(half)]
    for y in range(0, rows, 2):
        rest[y], rest[y + 1] = own_score(wide_ref, m3_ref, frames, y)
    bias = c3_ref[...]
    for f in range(frames):
        at = slice(f * fields, (f + 1) * fields)
        west, east = side[0, at], side[1, at]
        for y in range(rows):
            scr[f, pl.ds(y, fields, stride=rows), :] = patched(rest[y, at], west, east, y) + bias
        score = scr[f].reshape(fields, rows, LANES)
        moved = state_ref[f].astype(F32) + 0.8 * score + 0.5 * noise_ref[f].astype(F32)
        out_ref[f] = moved.astype(BF)
        head_ref[f] = moved[0]


def make_update(wide, t3, m3, s3, c3, state, noise):
    frames, fields, rows, _ = state.shape
    return call(
        update_kernel,
        "update",
        (shape_of(state.shape, BF), shape_of((frames, rows, LANES), F32)),
        [VMEM] * 7,
        [
            pltpu.VMEM((rows, frames * fields, LANES), F32),
            pltpu.VMEM((2, frames * fields, LANES), F32),
            pltpu.VMEM((frames, fields * rows, LANES), F32),
        ],
        cost=3_000_000_000,
    )(wide, t3, m3, s3, c3, state, noise)


def correct_kernel(count, *refs):
    parts = refs[:count]
    observed_ref, mask_ref, head_ref, day_ref, _, out_ref, buf, sem = refs[count:]
    frames = head_ref.shape[0]
    days = observed_ref.shape[0]
    mask = mask_ref[...].astype(F32)
    misfit = [0.15 * (mask * (sum(p[d] for p in parts) - observed_ref[d])) for d in range(days)]
    for f in range(frames):
        v = head_ref[f]
        for d in range(days):
            v = v - jnp.where(day_ref[f : f + 1] == d, misfit[d], 0.0)
        buf[f, 0] = v.astype(BF)
    copy = pltpu.make_async_copy(buf, out_ref.at[:, 0:1], sem)
    copy.start()
    copy.wait()


def make_correct(parts, observed, mask, head, day, out):
    frames, rows, _ = head.shape
    return call(
        functools.partial(correct_kernel, len(parts)),
        "correct",
        (shape_of(out.shape, BF),),
        [VMEM] * (len(parts) + 4) + [ANYWHERE],
        [pltpu.VMEM((frames, 1, rows, LANES), BF), pltpu.SemaphoreType.DMA],
        alias={len(parts) + 4: 0},
        out_specs=(ANYWHERE,),
    )(*parts, observed, mask, head, day, out)[0]


def swapped(value, axis, start):
    sizes = {name: lax.axis_size(name) for name in ("tm", "space")}
    other = "space" if axis == "tm" else "tm"
    pairs = []
    for t in range(sizes["tm"]):
        for s in range(sizes["space"]):
            to = {"tm": t, "space": s}
            to[axis] += 1 if to[axis] % 2 == start else -1
            if not 0 <= to[axis] < sizes[axis]:
                to = {"tm": t, "space": s}
                to[other] ^= 1
            pairs.append((t * sizes["space"] + s, to["tm"] * sizes["space"] + to["space"]))
    return lax.ppermute(value, ("tm", "space"), pairs)


def totals_of(mine):
    count = lax.axis_size("tm")

    def partner(value, bits):
        return lax.ppermute(value, "tm", [(i, i ^ bits) for i in range(count)])

    if count & (count - 1):
        return [lax.psum(mine, "tm")]
    far = count // 2
    while far > 2:
        mine = mine + partner(mine, far)
        far //= 2
    return [partner(mine, bits) for bits in (2, 3, 1) if bits < count] + [mine]


def body(
    state, noise, conv_one, bias_one, conv_two, bias_two, conv_three, bias_three, day_of_frame, observed, obs_mask
):
    state, noise = state[:, :, 0], noise[:, :, 0]
    hid, chans = conv_one.shape[:2]
    fields = conv_three.shape[0]
    w1 = conv_one.transpose(2, 3, 4, 1, 0).reshape(27 * chans, hid)
    w2 = conv_two.transpose(2, 3, 4, 0, 1).reshape(27, hid, hid)
    w3 = conv_three.transpose(2, 3, 4, 0, 1).reshape(27, fields, hid)
    own, send2, send1 = make_rows(state)
    far = swapped(send2, "tm", 1)
    near = swapped(send1, "tm", 0)
    small = jnp.concatenate([bias_one, bias_two, bias_three, day_of_frame.astype(F32)])[None]
    m1, m2, m3, s1, s2, s3, c1, c2, c3, days, head = make_weights(w1, w2, w3, small, state.shape[0])
    own1, own2, west, east = make_inner(own, m1, c1)
    west, east, send1, send2 = make_edges(west, east, near, far)
    first, second = swapped(send1, "space", 0), swapped(send2, "space", 1)
    wide = make_main(own1, own2, near, far, m1, m2, c1, c2)
    t3, mine = make_side(
        wide, west, east, first, second, s1, s2, head, c1, c2, c3, state, days, observed.shape[0]
    )
    out, head0 = make_update(wide, t3, m3, s3, c3, state, noise)
    parts = totals_of(mine)
    out = make_correct(parts, observed[:, 0], obs_mask[0], head0, days, out)
    return out[:, :, None]


def solution(mesh):
    in_specs = (
        P("tm", None, "space", None, None),
        P("tm", None, "space", None, None),
        P(),
        P(),
        P(),
        P(),
        P(),
        P(),
        P("tm"),
        P(None, "space", None, None),
        P("space", None, None),
    )
    out_specs = P("tm", None, "space", None, None)
    return jax.shard_map(body, mesh=mesh, in_specs=in_specs, out_specs=out_specs, check_vma=False)
```

```python
import functools

import jax
import jax.numpy as jnp
from jax import lax
from jax.experimental import pallas as pl
from jax.experimental.pallas import tpu as pltpu
from jax.sharding import PartitionSpec as P

BF = jnp.bfloat16
F32 = jnp.float32
LANES = 128
DEPTH = 3
PITCH = 16
VMEM = pl.BlockSpec(memory_space=pltpu.VMEM)
ANYWHERE = pl.BlockSpec(memory_space=pltpu.HBM)
LIMIT = 24 * 1024 * 1024


def shape_of(dims, kind):
    return jax.ShapeDtypeStruct(dims, kind)


def call(kernel, name, outs, specs, scratch=(), cost=None, alias=None, out_specs=None):
    return pl.pallas_call(
        kernel,
        out_shape=outs,
        in_specs=specs,
        out_specs=out_specs or (VMEM,) * len(outs),
        scratch_shapes=list(scratch),
        input_output_aliases=alias or {},
        compiler_params=pltpu.CompilerParams(vmem_limit_bytes=LIMIT),
        cost_estimate=cost and pl.CostEstimate(flops=cost, bytes_accessed=1_000_000, transcendentals=0),
        name=name,
    )


def silu(v):
    half = 0.5 * v
    return half + half * jnp.tanh(half)


def lanes(shape):
    return lax.broadcasted_iota(jnp.int32, shape, len(shape) - 1)


def turn(v, steps):
    steps = steps % LANES
    return pltpu.roll(v, steps, 1) if steps else v


def tile(i):
    return slice(i * LANES, (i + 1) * LANES)


def is_even(axis):
    return lax.axis_index(axis) % 2 == 0


def rows_kernel(state_ref, own_ref, far_ref, near_ref, scr):
    frames, chans, rows, _ = state_ref.shape
    for f in range(frames):
        scr[f] = state_ref[f].astype(F32).reshape(chans * rows, LANES)
        for y in range(rows):
            v = scr[f, pl.ds(y, chans, stride=rows), :].astype(BF)
            own_ref[f, :, tile(y)] = v
    even = is_even("tm")
    for f in range(DEPTH):
        low, high = own_ref[f], own_ref[frames - DEPTH + f]
        near_ref[f], far_ref[f] = jnp.where(even, high, low), jnp.where(even, low, high)


def make_rows(state):
    frames, chans, rows, _ = state.shape
    slab = shape_of((DEPTH, chans, rows * LANES), BF)
    return call(
        rows_kernel,
        "rows",
        (shape_of((frames, chans, rows * LANES), BF), slab, slab),
        [VMEM],
        [pltpu.VMEM((frames, chans * rows, LANES), F32)],
        cost=4_000_000_000,
    )(state)


def weights_kernel(
    w1_ref, w2_ref, w3_ref, small_ref,
    m1_ref, m2_ref, m3_ref, s1_ref, s2_ref, s3_ref, c1_ref, c2_ref, c3_ref, days_ref, head_ref, f2, f3,
):
    small = jnp.broadcast_to(small_ref[...], (8, small_ref.shape[1])).T[:, 0:1]
    at = 0
    for ref in (c1_ref, c2_ref, c3_ref, days_ref):
        ref[...] = jnp.broadcast_to(small[at : at + ref.shape[0]], ref.shape)
        at += ref.shape[0]
    for ref in (m1_ref, m2_ref, m3_ref, s1_ref, s2_ref, s3_ref):
        ref[...] = jnp.zeros_like(ref)
    hid, fields, chans = w2_ref.shape[1], w3_ref.shape[1], w1_ref.shape[0] // 27
    frames = days_ref.shape[0]
    flat = w1_ref[...].astype(F32).T.astype(BF)
    for p in range(2):
        m1_ref[p * hid : (p + 1) * hid, p * 9 * chans : (p + 3) * 9 * chans] = flat
        for dt in range(3):
            for dy in range(3):
                at = (dt * 3 + dy) * 3 * chans
                s1_ref[(p * 3 + dy) * hid : (p * 3 + dy + 1) * hid, (dt + p) * 3 * chans : (dt + p + 1) * 3 * chans] = (
                    flat[:, at : at + 3 * chans]
                )

    def place(raw, flat, main, side, count, outs):
        half = LANES // 2
        for t in range(27):
            for k in range(2):
                flat[k, :, t * hid + k * half : (t + 1) * hid + k * half] = raw[t]
        for p in range(count):
            rows, at = slice(p * outs, (p + 1) * outs), p * 9 * hid
            k = at % LANES // half
            main[rows, at : at + 27 * hid] = flat[k, :, k * half : k * half + 27 * hid]
            for dt in range(3):
                for dy in range(3):
                    rows = slice((p * 3 + dy) * outs, (p * 3 + dy + 1) * outs)
                    at, src = (dt + p) * 3 * hid, (dt * 3 + dy) * 3 * hid
                    k = (at - src) % LANES // half
                    side[rows, at : at + 3 * hid] = flat[k, :, src + k * half : src + k * half + 3 * hid]

    place(w2_ref, f2, m2_ref, s2_ref, 2, hid)
    place(w3_ref, f3, m3_ref, s3_ref, frames, fields)
    shape = (head_ref.shape[0], s3_ref.shape[0])
    pick = lanes(shape) == fields * lax.broadcasted_iota(jnp.int32, shape, 0)
    head_ref[...] = jnp.dot(pick.astype(F32).astype(BF), s3_ref[...], preferred_element_type=F32).astype(BF)


def make_weights(w1, w2, w3, small, frames):
    hid, fields, chans = w2.shape[1], w3.shape[1], w1.shape[0] // 27
    return call(
        weights_kernel,
        "weights",
        (
            shape_of((2 * hid, 4 * 9 * chans), BF),
            shape_of((2 * hid, 4 * 9 * hid), BF),
            shape_of((frames * fields, (frames + 2) * 9 * hid), BF),
            shape_of((6 * hid, 4 * 3 * chans), BF),
            shape_of((6 * hid, 4 * 3 * hid), BF),
            shape_of((frames * 3 * fields, (frames + 2) * 3 * hid), BF),
            shape_of((hid, 1), F32),
            shape_of((hid, 1), F32),
            shape_of((fields, 1), F32),
            shape_of((frames, LANES), F32),
            shape_of((-(-3 * frames // 16) * 16, (frames + 2) * 3 * hid), BF),
        ),
        [VMEM] * 4,
        [pltpu.VMEM((2, w.shape[1], 27 * hid + LANES // 2), BF) for w in (w2, w3)],
        cost=1_000_000_000,
    )(w1, w2, w3, small)


def beside(near_ref, far_ref):
    step, last = lax.axis_index("tm"), lax.axis_size("tm") - 1
    even = is_even("tm")
    for f in range(DEPTH):
        for y in range(near_ref.shape[2] // LANES):
            a, b = near_ref[f, :, tile(y)], far_ref[f, :, tile(y)]
            none = jnp.zeros_like(a)
            yield f, y, jnp.where(step > 0, jnp.where(even, b, a), none)
            yield DEPTH + f, y, jnp.where(step < last, jnp.where(even, a, b), none)


def strips(rows_of_frames, count):
    begun = {}
    for f, y, v in rows_of_frames:
        lane = lanes(v.shape)
        group, place = lane // PITCH, lane % PITCH
        west, east = begun.pop(f, (jnp.zeros_like(v), jnp.zeros_like(v)))
        here = group == y
        west = jnp.where(here & (place >= DEPTH), turn(v, y * PITCH + DEPTH), west)
        east = jnp.where(here & (place < PITCH - DEPTH), turn(v, y * PITCH + PITCH - DEPTH), east)
        if y == count - 1:
            yield f, west, east
        else:
            begun[f] = west, east


def edges_kernel(own_west_ref, own_east_ref, far_ref, near_ref, west_ref, east_ref, send1_ref, send2_ref):
    frames = own_west_ref.shape[0]
    even = is_even("space")

    def put(f, west, east):
        west_ref[f], east_ref[f] = west, east
        send1_ref[f], send2_ref[f] = jnp.where(even, east, west), jnp.where(even, west, east)

    for f in range(frames):
        put(DEPTH + f, own_west_ref[f], own_east_ref[f])
    for f, west, east in strips(beside(near_ref, far_ref), near_ref.shape[2] // LANES):
        put(f if f < DEPTH else f + frames, west, east)


def make_edges(own_west, own_east, near, far):
    frames, chans, _ = own_west.shape
    strip = shape_of((frames + 2 * DEPTH, chans, LANES), BF)
    return call(edges_kernel, "edges", (strip,) * 4, [VMEM] * 4)(own_west, own_east, far, near)


def spread(dst, f, y, v):
    chans = v.shape[0]
    at = tile(y + 1)
    dst[f, 0:chans, at] = turn(v, 1)
    dst[f, chans : 2 * chans, at] = v
    dst[f, 2 * chans : 3 * chans, at] = turn(v, -1)


def window(src, frames, y):
    parts = []
    for f in frames:
        ref, at = src(f)
        for dy in range(3):
            parts.append(ref[at, :, (y + dy) * LANES : (y + dy + 2) * LANES])
    return jnp.concatenate(parts, axis=0)


def plain(ref):
    return lambda f: (ref, f)


def in_trajectory(local, frames):
    step = lax.axis_index("tm") * frames + local
    return (step >= 0) & (step < frames * lax.axis_size("tm"))


def blank_ends(*refs):
    for s in refs:
        s[:, :, tile(0)] = jnp.zeros(s.shape[:2] + (LANES,), BF)
        last = s.shape[2] // LANES - 1
        s[:, :, tile(last)] = jnp.zeros(s.shape[:2] + (LANES,), BF)


def layer(src, dst, m_ref, c_ref, groups, rows, keep):
    hid = c_ref.shape[0]
    for f, count in groups:
        weights = m_ref[...] if count == 2 else m_ref[0:hid, 0 : m_ref.shape[1] // 4 * 3]
        for y in range(0, rows, 2):
            acc = jnp.dot(weights, window(src, range(f, f + count + 2), y), preferred_element_type=F32)
            for p in range(count):
                h = silu(acc[p * hid : (p + 1) * hid] + c_ref[...]).astype(BF)
                inside = keep(f + p)
                h = h if inside is None else jnp.where(inside, h, jnp.zeros_like(h))
                ref, at = dst(f + p)
                spread(ref, at, y, h[:, tile(0)])
                spread(ref, at, y + 1, h[:, tile(1)])


def pairs_of(frames):
    groups = [(f, 2) for f in range(frames[0], frames[-1], 2)]
    return groups + [(frames[-1], 1)] * (len(frames) % 2)


def inner_kernel(own_ref, m1_ref, c1_ref, s1, s2, west_ref, east_ref):
    frames = own_ref.shape[0]
    rows = own_ref.shape[2] // LANES
    each = [(f, y, own_ref[f, :, tile(y)]) for f in range(frames) for y in range(rows)]
    blank_ends(s1, s2)
    for f, y, v in each:
        spread(s1, f, y, v)
    for f, west, east in strips(each, rows):
        west_ref[f], east_ref[f] = west, east
    layer(plain(s1), plain(s2), m1_ref, c1_ref, pairs_of(range(frames - 2)), rows, lambda f: None)


def make_inner(own, m1, c1):
    frames, chans, width = own.shape
    hid, wide = c1.shape[0], width + 2 * LANES
    strip = shape_of((frames, chans, LANES), BF)
    return call(
        inner_kernel,
        "inner",
        (shape_of((frames, 3 * chans, wide), BF), shape_of((frames - 2, 3 * hid, wide), BF), strip, strip),
        [VMEM] * 3,
        cost=1_000_000_000,
    )(own, m1, c1)


def main_kernel(own1, own2, far_ref, near_ref, m1_ref, m2_ref, c1_ref, c2_ref, s3, far1, far2):
    frames = own1.shape[0]
    rows = near_ref.shape[2] // LANES
    blank_ends(far1, far2, s3)
    for f, y, v in beside(near_ref, far_ref):
        spread(far1, f, y, v)

    def split(own, far, edge):
        count = own.shape[0]
        return lambda f: (own, f - edge) if edge <= f < edge + count else (far, f if f < edge else f - count)

    one, two = split(own1, far1, DEPTH), split(own2, far2, DEPTH)
    groups = pairs_of(range(DEPTH)) + pairs_of(range(frames + 1, frames + 4))
    layer(one, two, m1_ref, c1_ref, groups, rows, lambda f: in_trajectory(f - 2, frames))
    layer(two, plain(s3), m2_ref, c2_ref, pairs_of(range(frames + 2)), rows, lambda f: in_trajectory(f - 1, frames))


def make_main(own1, own2, near, far, m1, m2, c1, c2):
    frames, rows1, wide = own1.shape
    rows2 = own2.shape[1]
    return call(
        main_kernel,
        "main",
        (shape_of((frames + 2, rows2, wide), BF),),
        [VMEM] * 8,
        [pltpu.VMEM((2 * DEPTH, rows1, wide), BF), pltpu.VMEM((2 * DEPTH, rows2, wide), BF)],
        cost=5_000_000_000,
    )(own1, own2, far, near, m1, m2, c1, c2)[0]


def spread_side(dst, f, v):
    chans = v.shape[0]
    for half in range(2):
        w = v[:, tile(half)]
        dst[f, 0:chans, tile(half)] = turn(w, 1)
        dst[f, chans : 2 * chans, tile(half)] = w
        dst[f, 2 * chans : 3 * chans, tile(half)] = turn(w, -1)


def three_rows(up, mid, down):
    lane = lanes(mid.shape)
    up = jnp.where(lane >= PITCH, turn(up, PITCH), 0.0)
    down = jnp.where(lane < LANES - PITCH, turn(down, -PITCH), 0.0)
    return mid + up + down


def over_rows(acc, at, outs):
    halves = []
    for half in range(2):
        up, mid, down = (acc[at + d * outs : at + (d + 1) * outs, tile(half)] for d in range(3))
        halves.append(three_rows(up, mid, down))
    return jnp.concatenate(halves, axis=1)


def patched(v, west, east, y):
    col = lanes(v.shape)
    v = jnp.where(col < DEPTH, turn(west, -(y * PITCH + DEPTH)), v)
    return jnp.where(col >= LANES - DEPTH, turn(east, DEPTH - (y + 1) * PITCH), v)


def side_kernel(
    wide_ref, west_ref, east_ref, first_ref, second_ref, s1_ref, s2_ref, head_ref, c1_ref, c2_ref, c3_ref,
    state_ref, day_ref, t3, part_ref, t1, t2, own, ends,
):
    frames, fields, rows, _ = state_ref.shape
    chans, hid = west_ref.shape[1], c1_ref.shape[0]
    place = lanes((chans, LANES)) % PITCH
    even = is_even("space")
    me, last = lax.axis_index("space"), lax.axis_size("space") - 1
    none = jnp.zeros((chans, LANES), BF)
    for f in range(frames + 2 * DEPTH):
        a, b = first_ref[f], second_ref[f]
        a, b = jnp.where(even, b, a), jnp.where(even, a, b)
        a, b = jnp.where(me > 0, a, none), jnp.where(me < last, b, none)
        west = jnp.where(place < DEPTH, turn(a, 2 * DEPTH - PITCH), west_ref[f])
        east = jnp.where(place >= PITCH - DEPTH, turn(b, PITCH - 2 * DEPTH), east_ref[f])
        spread_side(t1, f, jnp.concatenate([west, east], axis=1))

    pair = lanes((1, 2 * LANES))
    place = pair % PITCH
    outside = ((pair < LANES) & (place < DEPTH) & (me == 0)) | (
        (pair >= LANES) & (place >= PITCH - DEPTH) & (me == last)
    )

    def layer(src, dst, m_ref, bias, count, first):
        for f in range(0, count, 2):
            z = jnp.concatenate([src[f + j] for j in range(4)], axis=0)
            for p in range(2):
                acc = jnp.dot(m_ref[p * 3 * hid : (p + 1) * 3 * hid], z, preferred_element_type=F32)
                h = silu(over_rows(acc, 0, hid) + bias)
                keep = in_trajectory(f + p + first, frames) & ~outside
                spread_side(dst, f + p, jnp.where(keep, h, 0.0).astype(BF))

    layer(t1, t2, s1_ref, c1_ref[...], frames + 4, -2)
    layer(t2, t3, s2_ref, c2_ref[...], frames + 2, -1)
    own[0] = jnp.zeros(own.shape[1:], F32)
    own[rows + 1] = jnp.zeros(own.shape[1:], F32)
    for y in range(0, rows, 2):
        z = jnp.concatenate([wide_ref[j, :, (y + 1) * LANES : (y + 3) * LANES] for j in range(frames + 2)], axis=0)
        acc = jnp.dot(head_ref[...], z, preferred_element_type=F32)
        own[y + 1], own[y + 2] = acc[:, tile(0)], acc[:, tile(1)]
    z = jnp.concatenate([t3[j] for j in range(frames + 2)], axis=0)
    acc = jnp.dot(head_ref[...], z, preferred_element_type=F32)
    ends[0], ends[1] = acc[:, tile(0)], acc[:, tile(1)]
    offsets = [pl.ds(dy, frames, stride=3) for dy in range(3)]
    west, east = (three_rows(*(ends[half, at] for at in offsets)) for half in range(2))
    days = part_ref.shape[0]
    day = day_ref[...]
    for y in range(rows):
        v = patched(sum(own[y + dy, offsets[dy]] for dy in range(3)), west, east, y)
        for d in range(days):
            part_ref[d, y : y + 1, :] = jnp.sum(jnp.where(day == d, v, 0.0), axis=0, keepdims=True)
    base = c3_ref[0:1, 0:1]
    for d in range(days):
        total = 0.5 * part_ref[d]
        for f in range(frames):
            total = total + jnp.where(day[f : f + 1] == d, state_ref[f, 0].astype(F32) + 0.5 * base, 0.0)
        part_ref[d] = total


def make_side(wide, west, east, first, second, s1, s2, head, c1, c2, c3, state, day, days):
    frames, fields, rows, _ = state.shape
    chans, hid = west.shape[1], c1.shape[0]
    return call(
        side_kernel,
        "side",
        (shape_of((frames + 2, 3 * hid, 2 * LANES), BF), shape_of((days, rows, LANES), F32)),
        [VMEM] * 13,
        [
            pltpu.VMEM((frames + 6, 3 * chans, 2 * LANES), BF),
            pltpu.VMEM((frames + 4, 3 * hid, 2 * LANES), BF),
            pltpu.VMEM((rows + 2, head.shape[0], LANES), F32),
            pltpu.VMEM((2, head.shape[0], LANES), F32),
        ],
    )(wide, west, east, first, second, s1, s2, head, c1, c2, c3, state, day)


def own_score(wide_ref, m3_ref, frames, y):
    acc = jnp.dot(m3_ref[...], window(plain(wide_ref), range(frames + 2), y), preferred_element_type=F32)
    return acc[:, tile(0)], acc[:, tile(1)]


def update_kernel(
    wide_ref, t3, m3_ref, s3_ref, c3_ref, state_ref, noise_ref, out_ref, head_ref, side, scr
):
    frames, fields, rows, _ = state_ref.shape
    z = jnp.concatenate([t3[j] for j in range(frames + 2)], axis=0)
    acc = jnp.dot(s3_ref[...], z, preferred_element_type=F32)
    for f in range(frames):
        both = over_rows(acc, f * 3 * fields, fields)
        for half in range(2):
            side[half, f * fields : (f + 1) * fields] = both[:, tile(half)]
    bias = c3_ref[...]
    for y in range(0, rows, 2):
        both = own_score(wide_ref, m3_ref, frames, y)
        for f in range(frames):
            at = slice(f * fields, (f + 1) * fields)
            west, east = side[0, at], side[1, at]
            for i in range(2):
                scr[f, pl.ds(y + i, fields, stride=rows), :] = patched(both[i][at], west, east, y + i) + bias
    for f in range(frames):
        score = scr[f].reshape(fields, rows, LANES)
        moved = state_ref[f].astype(F32) + 0.8 * score + 0.5 * noise_ref[f].astype(F32)
        out_ref[f] = moved.astype(BF)
        head_ref[f] = moved[0]


def make_update(wide, t3, m3, s3, c3, state, noise):
    frames, fields, rows, _ = state.shape
    return call(
        update_kernel,
        "update",
        (shape_of(state.shape, BF), shape_of((frames, rows, LANES), F32)),
        [VMEM] * 7,
        [
            pltpu.VMEM((2, frames * fields, LANES), F32),
            pltpu.VMEM((frames, fields * rows, LANES), F32),
        ],
        cost=3_000_000_000,
    )(wide, t3, m3, s3, c3, state, noise)


def correct_kernel(count, *refs):
    parts = refs[:count]
    observed_ref, mask_ref, head_ref, day_ref, body_ref, out_ref, buf, sems = refs[count:]
    frames = head_ref.shape[0]
    others = pltpu.make_async_copy(body_ref.at[:, 1:], out_ref.at[:, 1:], sems.at[0])
    others.start()
    days = observed_ref.shape[0]
    mask = mask_ref[...].astype(F32)
    misfit = [0.15 * (mask * (sum(p[d] for p in parts) - observed_ref[d])) for d in range(days)]
    for f in range(frames):
        v = head_ref[f]
        for d in range(days):
            v = v - jnp.where(day_ref[f : f + 1] == d, misfit[d], 0.0)
        buf[f, 0] = v.astype(BF)
    first = pltpu.make_async_copy(buf, out_ref.at[:, 0:1], sems.at[1])
    first.start()
    others.wait()
    first.wait()


def make_correct(parts, observed, mask, head, day, out):
    frames, rows, _ = head.shape
    return call(
        functools.partial(correct_kernel, len(parts)),
        "correct",
        (shape_of(out.shape, BF),),
        [VMEM] * (len(parts) + 5),
        [pltpu.VMEM((frames, 1, rows, LANES), BF), pltpu.SemaphoreType.DMA((2,))],
        out_specs=(ANYWHERE,),
    )(*parts, observed, mask, head, day, out)[0]


def swapped(value, axis, start):
    sizes = {name: lax.axis_size(name) for name in ("tm", "space")}
    other = "space" if axis == "tm" else "tm"
    pairs = []
    for t in range(sizes["tm"]):
        for s in range(sizes["space"]):
            to = {"tm": t, "space": s}
            to[axis] += 1 if to[axis] % 2 == start else -1
            if not 0 <= to[axis] < sizes[axis]:
                to = {"tm": t, "space": s}
                to[other] ^= 1
            pairs.append((t * sizes["space"] + s, to["tm"] * sizes["space"] + to["space"]))
    return lax.ppermute(value, ("tm", "space"), pairs)


def totals_of(mine):
    count = lax.axis_size("tm")

    def partner(value, bits):
        return lax.ppermute(value, "tm", [(i, i ^ bits) for i in range(count)])

    if count & (count - 1):
        return [lax.psum(mine, "tm")]
    far = count // 2
    while far > 2:
        mine = mine + partner(mine, far)
        far //= 2
    return [partner(mine, bits) for bits in (2, 3, 1) if bits < count] + [mine]


def body(
    state, noise, conv_one, bias_one, conv_two, bias_two, conv_three, bias_three, day_of_frame, observed, obs_mask
):
    state, noise = state[:, :, 0], noise[:, :, 0]
    hid, chans = conv_one.shape[:2]
    fields = conv_three.shape[0]
    w1 = conv_one.transpose(2, 3, 4, 1, 0).reshape(27 * chans, hid)
    w2 = conv_two.transpose(2, 3, 4, 0, 1).reshape(27, hid, hid)
    w3 = conv_three.transpose(2, 3, 4, 0, 1).reshape(27, fields, hid)
    own, send2, send1 = make_rows(state)
    far = swapped(send2, "tm", 1)
    near = swapped(send1, "tm", 0)
    small = jnp.concatenate([bias_one, bias_two, bias_three, day_of_frame.astype(F32)])[None]
    m1, m2, m3, s1, s2, s3, c1, c2, c3, days, head = make_weights(w1, w2, w3, small, state.shape[0])
    own1, own2, west, east = make_inner(own, m1, c1)
    west, east, send1, send2 = make_edges(west, east, near, far)
    first, second = swapped(send1, "space", 0), swapped(send2, "space", 1)
    wide = make_main(own1, own2, near, far, m1, m2, c1, c2)
    t3, mine = make_side(
        wide, west, east, first, second, s1, s2, head, c1, c2, c3, state, days, observed.shape[0]
    )
    out, head0 = make_update(wide, t3, m3, s3, c3, state, noise)
    parts = totals_of(mine)
    out = make_correct(parts, observed[:, 0], obs_mask[0], head0, days, out)
    return out[:, :, None]


def solution(mesh):
    in_specs = (
        P("tm", None, "space", None, None),
        P("tm", None, "space", None, None),
        P(),
        P(),
        P(),
        P(),
        P(),
        P(),
        P("tm"),
        P(None, "space", None, None),
        P("space", None, None),
    )
    out_specs = P("tm", None, "space", None, None)
    return jax.shard_map(body, mesh=mesh, in_specs=in_specs, out_specs=out_specs, check_vma=False)
```

```python
import functools

import jax
import jax.numpy as jnp
from jax import lax
from jax.experimental import pallas as pl
from jax.experimental.pallas import tpu as pltpu
from jax.sharding import PartitionSpec as P

BF = jnp.bfloat16
F32 = jnp.float32
LANES = 128
DEPTH = 3
PITCH = 16
VMEM = pl.BlockSpec(memory_space=pltpu.VMEM)
ANYWHERE = pl.BlockSpec(memory_space=pltpu.HBM)
LIMIT = 24 * 1024 * 1024


def shape_of(dims, kind):
    return jax.ShapeDtypeStruct(dims, kind)


def call(kernel, name, outs, specs, scratch=(), cost=None, alias=None, out_specs=None):
    return pl.pallas_call(
        kernel,
        out_shape=outs,
        in_specs=specs,
        out_specs=out_specs or (VMEM,) * len(outs),
        scratch_shapes=list(scratch),
        input_output_aliases=alias or {},
        compiler_params=pltpu.CompilerParams(vmem_limit_bytes=LIMIT),
        cost_estimate=cost and pl.CostEstimate(flops=cost, bytes_accessed=1_000_000, transcendentals=0),
        name=name,
    )


def silu(v):
    half = 0.5 * v
    return half + half * jnp.tanh(half)


def lanes(shape):
    return lax.broadcasted_iota(jnp.int32, shape, len(shape) - 1)


def turn(v, steps):
    steps = steps % LANES
    return pltpu.roll(v, steps, 1) if steps else v


def tile(i):
    return slice(i * LANES, (i + 1) * LANES)


def is_even(axis):
    return lax.axis_index(axis) % 2 == 0


def rows_kernel(state_ref, own_ref, far_ref, near_ref, scr):
    frames, chans, rows, _ = state_ref.shape
    for f in range(frames):
        scr[f] = state_ref[f].astype(F32).reshape(chans * rows, LANES)
        for y in range(rows):
            v = scr[f, pl.ds(y, chans, stride=rows), :].astype(BF)
            own_ref[f, :, tile(y)] = v
    even = is_even("tm")
    for f in range(DEPTH):
        low, high = own_ref[f], own_ref[frames - DEPTH + f]
        near_ref[f], far_ref[f] = jnp.where(even, high, low), jnp.where(even, low, high)


def make_rows(state):
    frames, chans, rows, _ = state.shape
    slab = shape_of((DEPTH, chans, rows * LANES), BF)
    return call(
        rows_kernel,
        "rows",
        (shape_of((frames, chans, rows * LANES), BF), slab, slab),
        [VMEM],
        [pltpu.VMEM((frames, chans * rows, LANES), F32)],
        cost=4_000_000_000,
    )(state)


def weights_kernel(
    w1_ref, w2_ref, w3_ref, small_ref,
    m1_ref, m2_ref, m3_ref, s1_ref, s2_ref, s3_ref, c1_ref, c2_ref, c3_ref, days_ref, head_ref, f2, f3,
):
    small = jnp.broadcast_to(small_ref[...], (8, small_ref.shape[1])).T[:, 0:1]
    at = 0
    for ref in (c1_ref, c2_ref, c3_ref, days_ref):
        ref[...] = jnp.broadcast_to(small[at : at + ref.shape[0]], ref.shape)
        at += ref.shape[0]
    for ref in (m1_ref, m2_ref, m3_ref, s1_ref, s2_ref, s3_ref):
        ref[...] = jnp.zeros_like(ref)
    hid, fields, chans = w2_ref.shape[1], w3_ref.shape[1], w1_ref.shape[0] // 27
    frames = days_ref.shape[0]
    flat = w1_ref[...].astype(F32).T.astype(BF)
    for p in range(2):
        m1_ref[p * hid : (p + 1) * hid, p * 9 * chans : (p + 3) * 9 * chans] = flat
        for dt in range(3):
            for dy in range(3):
                at = (dt * 3 + dy) * 3 * chans
                s1_ref[(p * 3 + dy) * hid : (p * 3 + dy + 1) * hid, (dt + p) * 3 * chans : (dt + p + 1) * 3 * chans] = (
                    flat[:, at : at + 3 * chans]
                )

    def place(raw, flat, main, side, count, outs):
        half = LANES // 2
        for t in range(27):
            for k in range(2):
                flat[k, :, t * hid + k * half : (t + 1) * hid + k * half] = raw[t]
        for p in range(count):
            rows, at = slice(p * outs, (p + 1) * outs), p * 9 * hid
            k = at % LANES // half
            main[rows, at : at + 27 * hid] = flat[k, :, k * half : k * half + 27 * hid]
            for dt in range(3):
                for dy in range(3):
                    rows = slice((p * 3 + dy) * outs, (p * 3 + dy + 1) * outs)
                    at, src = (dt + p) * 3 * hid, (dt * 3 + dy) * 3 * hid
                    k = (at - src) % LANES // half
                    side[rows, at : at + 3 * hid] = flat[k, :, src + k * half : src + k * half + 3 * hid]

    place(w2_ref, f2, m2_ref, s2_ref, 2, hid)
    place(w3_ref, f3, m3_ref, s3_ref, frames, fields)
    shape = (head_ref.shape[0], s3_ref.shape[0])
    pick = lanes(shape) == fields * lax.broadcasted_iota(jnp.int32, shape, 0)
    head_ref[...] = jnp.dot(pick.astype(F32).astype(BF), s3_ref[...], preferred_element_type=F32).astype(BF)


def make_weights(w1, w2, w3, small, frames):
    hid, fields, chans = w2.shape[1], w3.shape[1], w1.shape[0] // 27
    return call(
        weights_kernel,
        "weights",
        (
            shape_of((2 * hid, 4 * 9 * chans), BF),
            shape_of((2 * hid, 4 * 9 * hid), BF),
            shape_of((frames * fields, (frames + 2) * 9 * hid), BF),
            shape_of((6 * hid, 4 * 3 * chans), BF),
            shape_of((6 * hid, 4 * 3 * hid), BF),
            shape_of((frames * 3 * fields, (frames + 2) * 3 * hid), BF),
            shape_of((hid, 1), F32),
            shape_of((hid, 1), F32),
            shape_of((fields, 1), F32),
            shape_of((frames, LANES), F32),
            shape_of((-(-3 * frames // 16) * 16, (frames + 2) * 3 * hid), BF),
        ),
        [VMEM] * 4,
        [pltpu.VMEM((2, w.shape[1], 27 * hid + LANES // 2), BF) for w in (w2, w3)],
        cost=1_000_000_000,
    )(w1, w2, w3, small)


def beside(near_ref, far_ref):
    step, last = lax.axis_index("tm"), lax.axis_size("tm") - 1
    even = is_even("tm")
    for f in range(DEPTH):
        for y in range(near_ref.shape[2] // LANES):
            a, b = near_ref[f, :, tile(y)], far_ref[f, :, tile(y)]
            none = jnp.zeros_like(a)
            yield f, y, jnp.where(step > 0, jnp.where(even, b, a), none)
            yield DEPTH + f, y, jnp.where(step < last, jnp.where(even, a, b), none)


def strips(rows_of_frames, count):
    begun = {}
    for f, y, v in rows_of_frames:
        lane = lanes(v.shape)
        group, place = lane // PITCH, lane % PITCH
        west, east = begun.pop(f, (jnp.zeros_like(v), jnp.zeros_like(v)))
        here = group == y
        west = jnp.where(here & (place >= DEPTH), turn(v, y * PITCH + DEPTH), west)
        east = jnp.where(here & (place < PITCH - DEPTH), turn(v, y * PITCH + PITCH - DEPTH), east)
        if y == count - 1:
            yield f, west, east
        else:
            begun[f] = west, east


def edges_kernel(own_west_ref, own_east_ref, far_ref, near_ref, west_ref, east_ref, send1_ref, send2_ref):
    frames = own_west_ref.shape[0]
    even = is_even("space")

    def put(f, west, east):
        west_ref[f], east_ref[f] = west, east
        send1_ref[f], send2_ref[f] = jnp.where(even, east, west), jnp.where(even, west, east)

    for f in range(frames):
        put(DEPTH + f, own_west_ref[f], own_east_ref[f])
    for f, west, east in strips(beside(near_ref, far_ref), near_ref.shape[2] // LANES):
        put(f if f < DEPTH else f + frames, west, east)


def make_edges(own_west, own_east, near, far):
    frames, chans, _ = own_west.shape
    strip = shape_of((frames + 2 * DEPTH, chans, LANES), BF)
    return call(edges_kernel, "edges", (strip,) * 4, [VMEM] * 4)(own_west, own_east, far, near)


def spread(dst, f, y, v):
    chans = v.shape[0]
    at = tile(y + 1)
    dst[f, 0:chans, at] = turn(v, 1)
    dst[f, chans : 2 * chans, at] = v
    dst[f, 2 * chans : 3 * chans, at] = turn(v, -1)


def window(src, frames, y):
    parts = []
    for f in frames:
        ref, at = src(f)
        for dy in range(3):
            parts.append(ref[at, :, (y + dy) * LANES : (y + dy + 2) * LANES])
    return jnp.concatenate(parts, axis=0)


def plain(ref):
    return lambda f: (ref, f)


def split(own, far, count=None):
    count = own.shape[0] if count is None else count
    return lambda f: (own, f - DEPTH) if DEPTH <= f < DEPTH + count else (far, f if f < DEPTH else f - count)


def in_trajectory(local, frames):
    step = lax.axis_index("tm") * frames + local
    return (step >= 0) & (step < frames * lax.axis_size("tm"))


def blank_ends(*refs):
    for s in refs:
        s[:, :, tile(0)] = jnp.zeros(s.shape[:2] + (LANES,), BF)
        last = s.shape[2] // LANES - 1
        s[:, :, tile(last)] = jnp.zeros(s.shape[:2] + (LANES,), BF)


def layer(src, dst, m_ref, c_ref, groups, rows, keep):
    hid = c_ref.shape[0]
    for f, count in groups:
        weights = m_ref[...] if count == 2 else m_ref[0:hid, 0 : m_ref.shape[1] // 4 * 3]
        for y in range(0, rows, 2):
            acc = jnp.dot(weights, window(src, range(f, f + count + 2), y), preferred_element_type=F32)
            for p in range(count):
                h = silu(acc[p * hid : (p + 1) * hid] + c_ref[...]).astype(BF)
                inside = keep(f + p)
                h = h if inside is None else jnp.where(inside, h, jnp.zeros_like(h))
                ref, at = dst(f + p)
                spread(ref, at, y, h[:, tile(0)])
                spread(ref, at, y + 1, h[:, tile(1)])


def pairs_of(frames):
    groups = [(f, 2) for f in range(frames[0], frames[-1], 2)]
    return groups + [(frames[-1], 1)] * (len(frames) % 2)


def inner_kernel(own_ref, m1_ref, m2_ref, c1_ref, c2_ref, s1, s2, s3, west_ref, east_ref):
    frames = own_ref.shape[0]
    rows = own_ref.shape[2] // LANES
    each = [(f, y, own_ref[f, :, tile(y)]) for f in range(frames) for y in range(rows)]
    blank_ends(s1, s2, s3)
    for f, y, v in each:
        spread(s1, f, y, v)
    for f, west, east in strips(each, rows):
        west_ref[f], east_ref[f] = west, east
    layer(plain(s1), plain(s2), m1_ref, c1_ref, pairs_of(range(frames - 2)), rows, lambda f: None)
    layer(plain(s2), plain(s3), m2_ref, c2_ref, pairs_of(range(frames - 4)), rows, lambda f: None)


def make_inner(own, m1, m2, c1, c2):
    frames, chans, width = own.shape
    hid, wide = c1.shape[0], width + 2 * LANES
    strip = shape_of((frames, chans, LANES), BF)
    return call(
        inner_kernel,
        "inner",
        (
            shape_of((frames, 3 * chans, wide), BF),
            shape_of((frames - 2, 3 * hid, wide), BF),
            shape_of((frames - 4, 3 * hid, wide), BF),
            strip,
            strip,
        ),
        [VMEM] * 5,
        cost=1_500_000_000,
    )(own, m1, m2, c1, c2)


def main_kernel(own1, own2, far_ref, near_ref, m1_ref, m2_ref, c1_ref, c2_ref, s3, far1, far2):
    frames = own1.shape[0]
    rows = near_ref.shape[2] // LANES
    blank_ends(far1, far2, s3)
    for f, y, v in beside(near_ref, far_ref):
        spread(far1, f, y, v)

    one, two, three = split(own1, far1), split(own2, far2), split(None, s3, frames - 4)
    groups = pairs_of(range(DEPTH)) + pairs_of(range(frames + 1, frames + 4))
    layer(one, two, m1_ref, c1_ref, groups, rows, lambda f: in_trajectory(f - 2, frames))
    groups = pairs_of(range(DEPTH)) + pairs_of(range(frames - 1, frames + 2))
    layer(two, three, m2_ref, c2_ref, groups, rows, lambda f: in_trajectory(f - 1, frames))


def make_main(own1, own2, near, far, m1, m2, c1, c2):
    frames, rows1, wide = own1.shape
    rows2 = own2.shape[1]
    return call(
        main_kernel,
        "main",
        (shape_of((2 * DEPTH, rows2, wide), BF),),
        [VMEM] * 8,
        [pltpu.VMEM((2 * DEPTH, rows1, wide), BF), pltpu.VMEM((2 * DEPTH, rows2, wide), BF)],
        cost=5_000_000_000,
    )(own1, own2, far, near, m1, m2, c1, c2)[0]


def spread_side(dst, f, v):
    chans = v.shape[0]
    for half in range(2):
        w = v[:, tile(half)]
        dst[f, 0:chans, tile(half)] = turn(w, 1)
        dst[f, chans : 2 * chans, tile(half)] = w
        dst[f, 2 * chans : 3 * chans, tile(half)] = turn(w, -1)


def three_rows(up, mid, down):
    lane = lanes(mid.shape)
    up = jnp.where(lane >= PITCH, turn(up, PITCH), 0.0)
    down = jnp.where(lane < LANES - PITCH, turn(down, -PITCH), 0.0)
    return mid + up + down


def over_rows(acc, at, outs):
    halves = []
    for half in range(2):
        up, mid, down = (acc[at + d * outs : at + (d + 1) * outs, tile(half)] for d in range(3))
        halves.append(three_rows(up, mid, down))
    return jnp.concatenate(halves, axis=1)


def patched(v, west, east, y):
    col = lanes(v.shape)
    v = jnp.where(col < DEPTH, turn(west, -(y * PITCH + DEPTH)), v)
    return jnp.where(col >= LANES - DEPTH, turn(east, DEPTH - (y + 1) * PITCH), v)


def side_kernel(
    own3, far3, west_ref, east_ref, first_ref, second_ref, s1_ref, s2_ref, head_ref, c1_ref, c2_ref, c3_ref,
    state_ref, day_ref, t3, part_ref, t1, t2, own, ends,
):
    frames, fields, rows, _ = state_ref.shape
    chans, hid = west_ref.shape[1], c1_ref.shape[0]
    place = lanes((chans, LANES)) % PITCH
    even = is_even("space")
    me, last = lax.axis_index("space"), lax.axis_size("space") - 1
    none = jnp.zeros((chans, LANES), BF)
    for f in range(frames + 2 * DEPTH):
        a, b = first_ref[f], second_ref[f]
        a, b = jnp.where(even, b, a), jnp.where(even, a, b)
        a, b = jnp.where(me > 0, a, none), jnp.where(me < last, b, none)
        west = jnp.where(place < DEPTH, turn(a, 2 * DEPTH - PITCH), west_ref[f])
        east = jnp.where(place >= PITCH - DEPTH, turn(b, PITCH - 2 * DEPTH), east_ref[f])
        spread_side(t1, f, jnp.concatenate([west, east], axis=1))

    pair = lanes((1, 2 * LANES))
    place = pair % PITCH
    outside = ((pair < LANES) & (place < DEPTH) & (me == 0)) | (
        (pair >= LANES) & (place >= PITCH - DEPTH) & (me == last)
    )

    def layer(src, dst, m_ref, bias, count, first):
        for f in range(0, count, 2):
            z = jnp.concatenate([src[f + j] for j in range(4)], axis=0)
            for p in range(2):
                acc = jnp.dot(m_ref[p * 3 * hid : (p + 1) * 3 * hid], z, preferred_element_type=F32)
                h = silu(over_rows(acc, 0, hid) + bias)
                keep = in_trajectory(f + p + first, frames) & ~outside
                spread_side(dst, f + p, jnp.where(keep, h, 0.0).astype(BF))

    layer(t1, t2, s1_ref, c1_ref[...], frames + 4, -2)
    layer(t2, t3, s2_ref, c2_ref[...], frames + 2, -1)
    own[0] = jnp.zeros(own.shape[1:], F32)
    own[rows + 1] = jnp.zeros(own.shape[1:], F32)
    for y in range(0, rows, 2):
        places = [split(own3, far3)(j) for j in range(frames + 2)]
        z = jnp.concatenate([ref[at, :, (y + 1) * LANES : (y + 3) * LANES] for ref, at in places], axis=0)
        acc = jnp.dot(head_ref[...], z, preferred_element_type=F32)
        own[y + 1], own[y + 2] = acc[:, tile(0)], acc[:, tile(1)]
    z = jnp.concatenate([t3[j] for j in range(frames + 2)], axis=0)
    acc = jnp.dot(head_ref[...], z, preferred_element_type=F32)
    ends[0], ends[1] = acc[:, tile(0)], acc[:, tile(1)]
    offsets = [pl.ds(dy, frames, stride=3) for dy in range(3)]
    west, east = (three_rows(*(ends[half, at] for at in offsets)) for half in range(2))
    days = part_ref.shape[0]
    day = day_ref[...]
    for y in range(rows):
        v = patched(sum(own[y + dy, offsets[dy]] for dy in range(3)), west, east, y)
        for d in range(days):
            part_ref[d, y : y + 1, :] = jnp.sum(jnp.where(day == d, v, 0.0), axis=0, keepdims=True)
    base = c3_ref[0:1, 0:1]
    for d in range(days):
        total = 0.5 * part_ref[d]
        for f in range(frames):
            total = total + jnp.where(day[f : f + 1] == d, state_ref[f, 0].astype(F32) + 0.5 * base, 0.0)
        part_ref[d] = total


def make_side(own3, far3, west, east, first, second, s1, s2, head, c1, c2, c3, state, day, days):
    frames, fields, rows, _ = state.shape
    chans, hid = west.shape[1], c1.shape[0]
    return call(
        side_kernel,
        "side",
        (shape_of((frames + 2, 3 * hid, 2 * LANES), BF), shape_of((days, rows, LANES), F32)),
        [VMEM] * 14,
        [
            pltpu.VMEM((frames + 6, 3 * chans, 2 * LANES), BF),
            pltpu.VMEM((frames + 4, 3 * hid, 2 * LANES), BF),
            pltpu.VMEM((rows + 2, head.shape[0], LANES), F32),
            pltpu.VMEM((2, head.shape[0], LANES), F32),
        ],
    )(own3, far3, west, east, first, second, s1, s2, head, c1, c2, c3, state, day)


def own_score(own3, far3, m3_ref, frames, y):
    acc = jnp.dot(m3_ref[...], window(split(own3, far3), range(frames + 2), y), preferred_element_type=F32)
    return acc[:, tile(0)], acc[:, tile(1)]


def update_kernel(
    own3, far3, t3, m3_ref, s3_ref, c3_ref, state_ref, noise_ref, out_ref, head_ref, side, scr
):
    frames, fields, rows, _ = state_ref.shape
    z = jnp.concatenate([t3[j] for j in range(frames + 2)], axis=0)
    acc = jnp.dot(s3_ref[...], z, preferred_element_type=F32)
    for f in range(frames):
        both = over_rows(acc, f * 3 * fields, fields)
        for half in range(2):
            side[half, f * fields : (f + 1) * fields] = both[:, tile(half)]
    bias = c3_ref[...]
    for y in range(0, rows, 2):
        both = own_score(own3, far3, m3_ref, frames, y)
        for f in range(frames):
            at = slice(f * fields, (f + 1) * fields)
            west, east = side[0, at], side[1, at]
            for i in range(2):
                scr[f, pl.ds(y + i, fields, stride=rows), :] = patched(both[i][at], west, east, y + i) + bias
    for f in range(frames):
        score = scr[f].reshape(fields, rows, LANES)
        moved = state_ref[f].astype(F32) + 0.8 * score + 0.5 * noise_ref[f].astype(F32)
        out_ref[f] = moved.astype(BF)
        head_ref[f] = moved[0]


def make_update(own3, far3, t3, m3, s3, c3, state, noise):
    frames, fields, rows, _ = state.shape
    return call(
        update_kernel,
        "update",
        (shape_of(state.shape, BF), shape_of((frames, rows, LANES), F32)),
        [VMEM] * 8,
        [
            pltpu.VMEM((2, frames * fields, LANES), F32),
            pltpu.VMEM((frames, fields * rows, LANES), F32),
        ],
        cost=3_000_000_000,
    )(own3, far3, t3, m3, s3, c3, state, noise)


def correct_kernel(count, *refs):
    parts = refs[:count]
    observed_ref, mask_ref, head_ref, day_ref, body_ref, out_ref, buf, sems = refs[count:]
    frames = head_ref.shape[0]
    others = pltpu.make_async_copy(body_ref.at[:, 1:], out_ref.at[:, 1:], sems.at[0])
    others.start()
    days = observed_ref.shape[0]
    mask = mask_ref[...].astype(F32)
    misfit = [0.15 * (mask * (sum(p[d] for p in parts) - observed_ref[d])) for d in range(days)]
    for f in range(frames):
        v = head_ref[f]
        for d in range(days):
            v = v - jnp.where(day_ref[f : f + 1] == d, misfit[d], 0.0)
        buf[f, 0] = v.astype(BF)
    first = pltpu.make_async_copy(buf, out_ref.at[:, 0:1], sems.at[1])
    first.start()
    others.wait()
    first.wait()


def make_correct(parts, observed, mask, head, day, out):
    frames, rows, _ = head.shape
    return call(
        functools.partial(correct_kernel, len(parts)),
        "correct",
        (shape_of(out.shape, BF),),
        [VMEM] * (len(parts) + 5),
        [pltpu.VMEM((frames, 1, rows, LANES), BF), pltpu.SemaphoreType.DMA((2,))],
        out_specs=(ANYWHERE,),
    )(*parts, observed, mask, head, day, out)[0]


def swapped(value, axis, start):
    sizes = {name: lax.axis_size(name) for name in ("tm", "space")}
    other = "space" if axis == "tm" else "tm"
    pairs = []
    for t in range(sizes["tm"]):
        for s in range(sizes["space"]):
            to = {"tm": t, "space": s}
            to[axis] += 1 if to[axis] % 2 == start else -1
            if not 0 <= to[axis] < sizes[axis]:
                to = {"tm": t, "space": s}
                to[other] ^= 1
            pairs.append((t * sizes["space"] + s, to["tm"] * sizes["space"] + to["space"]))
    return lax.ppermute(value, ("tm", "space"), pairs)


def totals_of(mine):
    count = lax.axis_size("tm")

    def partner(value, bits):
        return lax.ppermute(value, "tm", [(i, i ^ bits) for i in range(count)])

    if count & (count - 1):
        return [lax.psum(mine, "tm")]
    far = count // 2
    while far > 2:
        mine = mine + partner(mine, far)
        far //= 2
    return [partner(mine, bits) for bits in (2, 3, 1) if bits < count] + [mine]


def body(
    state, noise, conv_one, bias_one, conv_two, bias_two, conv_three, bias_three, day_of_frame, observed, obs_mask
):
    state, noise = state[:, :, 0], noise[:, :, 0]
    hid, chans = conv_one.shape[:2]
    fields = conv_three.shape[0]
    w1 = conv_one.transpose(2, 3, 4, 1, 0).reshape(27 * chans, hid)
    w2 = conv_two.transpose(2, 3, 4, 0, 1).reshape(27, hid, hid)
    w3 = conv_three.transpose(2, 3, 4, 0, 1).reshape(27, fields, hid)
    own, send2, send1 = make_rows(state)
    far = swapped(send2, "tm", 1)
    near = swapped(send1, "tm", 0)
    small = jnp.concatenate([bias_one, bias_two, bias_three, day_of_frame.astype(F32)])[None]
    m1, m2, m3, s1, s2, s3, c1, c2, c3, days, head = make_weights(w1, w2, w3, small, state.shape[0])
    own1, own2, own3, west, east = make_inner(own, m1, m2, c1, c2)
    west, east, send1, send2 = make_edges(west, east, near, far)
    first, second = swapped(send1, "space", 0), swapped(send2, "space", 1)
    far3 = make_main(own1, own2, near, far, m1, m2, c1, c2)
    t3, mine = make_side(
        own3, far3, west, east, first, second, s1, s2, head, c1, c2, c3, state, days, observed.shape[0]
    )
    out, head0 = make_update(own3, far3, t3, m3, s3, c3, state, noise)
    parts = totals_of(mine)
    out = make_correct(parts, observed[:, 0], obs_mask[0], head0, days, out)
    return out[:, :, None]


def solution(mesh):
    in_specs = (
        P("tm", None, "space", None, None),
        P("tm", None, "space", None, None),
        P(),
        P(),
        P(),
        P(),
        P(),
        P(),
        P("tm"),
        P(None, "space", None, None),
        P("space", None, None),
    )
    out_specs = P("tm", None, "space", None, None)
    return jax.shard_map(body, mesh=mesh, in_specs=in_specs, out_specs=out_specs, check_vma=False)
```

```python
import functools

import jax
import jax.numpy as jnp
from jax import lax
from jax.experimental import pallas as pl
from jax.experimental.pallas import tpu as pltpu
from jax.sharding import PartitionSpec as P

BF = jnp.bfloat16
F32 = jnp.float32
LANES = 128
DEPTH = 3
PITCH = 16
VMEM = pl.BlockSpec(memory_space=pltpu.VMEM)
ANYWHERE = pl.BlockSpec(memory_space=pltpu.HBM)
LIMIT = 24 * 1024 * 1024


def shape_of(dims, kind):
    return jax.ShapeDtypeStruct(dims, kind)


def call(kernel, name, outs, specs, scratch=(), cost=None, alias=None, out_specs=None):
    return pl.pallas_call(
        kernel,
        out_shape=outs,
        in_specs=specs,
        out_specs=out_specs or (VMEM,) * len(outs),
        scratch_shapes=list(scratch),
        input_output_aliases=alias or {},
        compiler_params=pltpu.CompilerParams(vmem_limit_bytes=LIMIT),
        cost_estimate=cost and pl.CostEstimate(flops=cost, bytes_accessed=1_000_000, transcendentals=0),
        name=name,
    )


def silu(v):
    half = 0.5 * v
    return half + half * jnp.tanh(half)


def lanes(shape):
    return lax.broadcasted_iota(jnp.int32, shape, len(shape) - 1)


def turn(v, steps):
    steps = steps % LANES
    return pltpu.roll(v, steps, 1) if steps else v


def tile(i):
    return slice(i * LANES, (i + 1) * LANES)


def is_even(axis):
    return lax.axis_index(axis) % 2 == 0


def rows_kernel(state_ref, own_ref, far_ref, near_ref, scr):
    frames, chans, rows, _ = state_ref.shape
    for f in range(frames):
        scr[f] = state_ref[f].astype(F32).reshape(chans * rows, LANES)
        for y in range(rows):
            v = scr[f, pl.ds(y, chans, stride=rows), :].astype(BF)
            own_ref[f, :, tile(y)] = v
    even = is_even("tm")
    for f in range(DEPTH):
        low, high = own_ref[f], own_ref[frames - DEPTH + f]
        near_ref[f], far_ref[f] = jnp.where(even, high, low), jnp.where(even, low, high)


def make_rows(state):
    frames, chans, rows, _ = state.shape
    slab = shape_of((DEPTH, chans, rows * LANES), BF)
    return call(
        rows_kernel,
        "rows",
        (shape_of((frames, chans, rows * LANES), BF), slab, slab),
        [VMEM],
        [pltpu.VMEM((frames, chans * rows, LANES), F32)],
        cost=4_000_000_000,
    )(state)


def weights_kernel(
    w1_ref, w2_ref, w3_ref, small_ref,
    m1_ref, m2_ref, m3_ref, s1_ref, s2_ref, s3_ref, c1_ref, c2_ref, c3_ref, days_ref, head_ref, f2, f3,
):
    small = jnp.broadcast_to(small_ref[...], (8, small_ref.shape[1])).T[:, 0:1]
    at = 0
    for ref in (c1_ref, c2_ref, c3_ref, days_ref):
        ref[...] = jnp.broadcast_to(small[at : at + ref.shape[0]], ref.shape)
        at += ref.shape[0]
    for ref in (m1_ref, m2_ref, m3_ref, s1_ref, s2_ref, s3_ref):
        ref[...] = jnp.zeros_like(ref)
    hid, fields, chans = w2_ref.shape[1], w3_ref.shape[1], w1_ref.shape[0] // 27
    frames = days_ref.shape[0]
    flat = w1_ref[...].astype(F32).T.astype(BF)
    for p in range(2):
        m1_ref[p * hid : (p + 1) * hid, p * 9 * chans : (p + 3) * 9 * chans] = flat
        for dt in range(3):
            for dy in range(3):
                at = (dt * 3 + dy) * 3 * chans
                s1_ref[(p * 3 + dy) * hid : (p * 3 + dy + 1) * hid, (dt + p) * 3 * chans : (dt + p + 1) * 3 * chans] = (
                    flat[:, at : at + 3 * chans]
                )

    def place(raw, flat, main, side, count, outs):
        half = LANES // 2
        for t in range(27):
            for k in range(2):
                flat[k, :, t * hid + k * half : (t + 1) * hid + k * half] = raw[t]
        for p in range(count):
            rows, at = slice(p * outs, (p + 1) * outs), p * 9 * hid
            k = at % LANES // half
            main[rows, at : at + 27 * hid] = flat[k, :, k * half : k * half + 27 * hid]
            for dt in range(3):
                for dy in range(3):
                    rows = slice((p * 3 + dy) * outs, (p * 3 + dy + 1) * outs)
                    at, src = (dt + p) * 3 * hid, (dt * 3 + dy) * 3 * hid
                    k = (at - src) % LANES // half
                    side[rows, at : at + 3 * hid] = flat[k, :, src + k * half : src + k * half + 3 * hid]

    place(w2_ref, f2, m2_ref, s2_ref, 2, hid)
    place(w3_ref, f3, m3_ref, s3_ref, frames, fields)
    shape = (head_ref.shape[0], s3_ref.shape[0])
    pick = lanes(shape) == fields * lax.broadcasted_iota(jnp.int32, shape, 0)
    head_ref[...] = jnp.dot(pick.astype(F32).astype(BF), s3_ref[...], preferred_element_type=F32).astype(BF)


def make_weights(w1, w2, w3, small, frames):
    hid, fields, chans = w2.shape[1], w3.shape[1], w1.shape[0] // 27
    return call(
        weights_kernel,
        "weights",
        (
            shape_of((2 * hid, 4 * 9 * chans), BF),
            shape_of((2 * hid, 4 * 9 * hid), BF),
            shape_of((frames * fields, (frames + 2) * 9 * hid), BF),
            shape_of((6 * hid, 4 * 3 * chans), BF),
            shape_of((6 * hid, 4 * 3 * hid), BF),
            shape_of((frames * 3 * fields, (frames + 2) * 3 * hid), BF),
            shape_of((hid, 1), F32),
            shape_of((hid, 1), F32),
            shape_of((fields, 1), F32),
            shape_of((frames, LANES), F32),
            shape_of((-(-3 * frames // 16) * 16, (frames + 2) * 3 * hid), BF),
        ),
        [VMEM] * 4,
        [pltpu.VMEM((2, w.shape[1], 27 * hid + LANES // 2), BF) for w in (w2, w3)],
        cost=1_000_000_000,
    )(w1, w2, w3, small)


def beside(near_ref, far_ref):
    step, last = lax.axis_index("tm"), lax.axis_size("tm") - 1
    even = is_even("tm")
    for f in range(DEPTH):
        for y in range(near_ref.shape[2] // LANES):
            a, b = near_ref[f, :, tile(y)], far_ref[f, :, tile(y)]
            none = jnp.zeros_like(a)
            yield f, y, jnp.where(step > 0, jnp.where(even, b, a), none)
            yield DEPTH + f, y, jnp.where(step < last, jnp.where(even, a, b), none)


def strips(rows_of_frames, count):
    begun = {}
    for f, y, v in rows_of_frames:
        lane = lanes(v.shape)
        group, place = lane // PITCH, lane % PITCH
        west, east = begun.pop(f, (jnp.zeros_like(v), jnp.zeros_like(v)))
        here = group == y
        west = jnp.where(here & (place >= DEPTH), turn(v, y * PITCH + DEPTH), west)
        east = jnp.where(here & (place < PITCH - DEPTH), turn(v, y * PITCH + PITCH - DEPTH), east)
        if y == count - 1:
            yield f, west, east
        else:
            begun[f] = west, east


def edges_kernel(own_west_ref, own_east_ref, far_ref, near_ref, west_ref, east_ref, send1_ref, send2_ref):
    frames = own_west_ref.shape[0]
    even = is_even("space")

    def put(f, west, east):
        west_ref[f], east_ref[f] = west, east
        send1_ref[f], send2_ref[f] = jnp.where(even, east, west), jnp.where(even, west, east)

    for f in range(frames):
        put(DEPTH + f, own_west_ref[f], own_east_ref[f])
    for f, west, east in strips(beside(near_ref, far_ref), near_ref.shape[2] // LANES):
        put(f if f < DEPTH else f + frames, west, east)


def make_edges(own_west, own_east, near, far):
    frames, chans, _ = own_west.shape
    strip = shape_of((frames + 2 * DEPTH, chans, LANES), BF)
    return call(edges_kernel, "edges", (strip,) * 4, [VMEM] * 4)(own_west, own_east, far, near)


def spread(dst, f, y, v):
    chans = v.shape[0]
    at = tile(y + 1)
    dst[f, 0:chans, at] = turn(v, 1)
    dst[f, chans : 2 * chans, at] = v
    dst[f, 2 * chans : 3 * chans, at] = turn(v, -1)


def window(src, frames, y):
    parts = []
    for f in frames:
        ref, at = src(f)
        for dy in range(3):
            parts.append(ref[at, :, (y + dy) * LANES : (y + dy + 2) * LANES])
    return jnp.concatenate(parts, axis=0)


def plain(ref):
    return lambda f: (ref, f)


def split(own, far, count=None):
    count = own.shape[0] if count is None else count
    return lambda f: (own, f - DEPTH) if DEPTH <= f < DEPTH + count else (far, f if f < DEPTH else f - count)


def in_trajectory(local, frames):
    step = lax.axis_index("tm") * frames + local
    return (step >= 0) & (step < frames * lax.axis_size("tm"))


def blank_ends(*refs):
    for s in refs:
        s[:, :, tile(0)] = jnp.zeros(s.shape[:2] + (LANES,), BF)
        last = s.shape[2] // LANES - 1
        s[:, :, tile(last)] = jnp.zeros(s.shape[:2] + (LANES,), BF)


def layer(src, dst, m_ref, c_ref, groups, rows, keep):
    hid = c_ref.shape[0]
    for f, count in groups:
        weights = m_ref[...] if count == 2 else m_ref[0:hid, 0 : m_ref.shape[1] // 4 * 3]
        for y in range(0, rows, 2):
            acc = jnp.dot(weights, window(src, range(f, f + count + 2), y), preferred_element_type=F32)
            for p in range(count):
                h = silu(acc[p * hid : (p + 1) * hid] + c_ref[...]).astype(BF)
                inside = keep(f + p)
                h = h if inside is None else jnp.where(inside, h, jnp.zeros_like(h))
                ref, at = dst(f + p)
                spread(ref, at, y, h[:, tile(0)])
                spread(ref, at, y + 1, h[:, tile(1)])


def pairs_of(frames):
    groups = [(f, 2) for f in range(frames[0], frames[-1], 2)]
    return groups + [(frames[-1], 1)] * (len(frames) % 2)


def inner_kernel(own_ref, m1_ref, m2_ref, c1_ref, c2_ref, s1, s2, s3, west_ref, east_ref):
    frames = own_ref.shape[0]
    rows = own_ref.shape[2] // LANES
    each = [(f, y, own_ref[f, :, tile(y)]) for f in range(frames) for y in range(rows)]
    blank_ends(s1, s2, s3)
    for f, y, v in each:
        spread(s1, f, y, v)
    for f, west, east in strips(each, rows):
        west_ref[f], east_ref[f] = west, east
    layer(plain(s1), plain(s2), m1_ref, c1_ref, pairs_of(range(frames - 2)), rows, lambda f: None)
    layer(plain(s2), plain(s3), m2_ref, c2_ref, pairs_of(range(frames - 4)), rows, lambda f: None)


def make_inner(own, m1, m2, c1, c2):
    frames, chans, width = own.shape
    hid, wide = c1.shape[0], width + 2 * LANES
    strip = shape_of((frames, chans, LANES), BF)
    return call(
        inner_kernel,
        "inner",
        (
            shape_of((frames, 3 * chans, wide), BF),
            shape_of((frames - 2, 3 * hid, wide), BF),
            shape_of((frames - 4, 3 * hid, wide), BF),
            strip,
            strip,
        ),
        [VMEM] * 5,
        cost=1_500_000_000,
    )(own, m1, m2, c1, c2)


def main_kernel(own1, own2, far_ref, near_ref, m1_ref, m2_ref, c1_ref, c2_ref, s3, far1, far2):
    frames = own1.shape[0]
    rows = near_ref.shape[2] // LANES
    blank_ends(far1, far2, s3)
    for f, y, v in beside(near_ref, far_ref):
        spread(far1, f, y, v)

    one, two, three = split(own1, far1), split(own2, far2), split(None, s3, frames - 4)
    groups = pairs_of(range(DEPTH)) + pairs_of(range(frames + 1, frames + 4))
    layer(one, two, m1_ref, c1_ref, groups, rows, lambda f: in_trajectory(f - 2, frames))
    groups = pairs_of(range(DEPTH)) + pairs_of(range(frames - 1, frames + 2))
    layer(two, three, m2_ref, c2_ref, groups, rows, lambda f: in_trajectory(f - 1, frames))


def make_main(own1, own2, near, far, m1, m2, c1, c2):
    frames, rows1, wide = own1.shape
    rows2 = own2.shape[1]
    return call(
        main_kernel,
        "main",
        (shape_of((2 * DEPTH, rows2, wide), BF),),
        [VMEM] * 8,
        [pltpu.VMEM((2 * DEPTH, rows1, wide), BF), pltpu.VMEM((2 * DEPTH, rows2, wide), BF)],
        cost=5_000_000_000,
    )(own1, own2, far, near, m1, m2, c1, c2)[0]


def spread_side(dst, f, v):
    chans = v.shape[0]
    for half in range(2):
        w = v[:, tile(half)]
        dst[f, 0:chans, tile(half)] = turn(w, 1)
        dst[f, chans : 2 * chans, tile(half)] = w
        dst[f, 2 * chans : 3 * chans, tile(half)] = turn(w, -1)


def three_rows(up, mid, down):
    lane = lanes(mid.shape)
    up = jnp.where(lane >= PITCH, turn(up, PITCH), 0.0)
    down = jnp.where(lane < LANES - PITCH, turn(down, -PITCH), 0.0)
    return mid + up + down


def over_rows(acc, at, outs):
    halves = []
    for half in range(2):
        up, mid, down = (acc[at + d * outs : at + (d + 1) * outs, tile(half)] for d in range(3))
        halves.append(three_rows(up, mid, down))
    return jnp.concatenate(halves, axis=1)


def patched(v, west, east, y):
    col = lanes(v.shape)
    v = jnp.where(col < DEPTH, turn(west, -(y * PITCH + DEPTH)), v)
    return jnp.where(col >= LANES - DEPTH, turn(east, DEPTH - (y + 1) * PITCH), v)


def side_kernel(
    own3, far3, west_ref, east_ref, first_ref, second_ref, s1_ref, s2_ref, head_ref, c1_ref, c2_ref, c3_ref,
    state_ref, day_ref, t3, part_ref, t1, t2, own, ends,
):
    frames, fields, rows, _ = state_ref.shape
    chans, hid = west_ref.shape[1], c1_ref.shape[0]
    place = lanes((chans, LANES)) % PITCH
    even = is_even("space")
    me, last = lax.axis_index("space"), lax.axis_size("space") - 1
    none = jnp.zeros((chans, LANES), BF)
    for f in range(frames + 2 * DEPTH):
        a, b = first_ref[f], second_ref[f]
        a, b = jnp.where(even, b, a), jnp.where(even, a, b)
        a, b = jnp.where(me > 0, a, none), jnp.where(me < last, b, none)
        west = jnp.where(place < DEPTH, turn(a, 2 * DEPTH - PITCH), west_ref[f])
        east = jnp.where(place >= PITCH - DEPTH, turn(b, PITCH - 2 * DEPTH), east_ref[f])
        spread_side(t1, f, jnp.concatenate([west, east], axis=1))

    pair = lanes((1, 2 * LANES))
    place = pair % PITCH
    outside = ((pair < LANES) & (place < DEPTH) & (me == 0)) | (
        (pair >= LANES) & (place >= PITCH - DEPTH) & (me == last)
    )

    def layer(src, dst, m_ref, bias, count, first):
        for f in range(0, count, 2):
            z = jnp.concatenate([src[f + j] for j in range(4)], axis=0)
            for p in range(2):
                acc = jnp.dot(m_ref[p * 3 * hid : (p + 1) * 3 * hid], z, preferred_element_type=F32)
                h = silu(over_rows(acc, 0, hid) + bias)
                keep = in_trajectory(f + p + first, frames) & ~outside
                spread_side(dst, f + p, jnp.where(keep, h, 0.0).astype(BF))

    layer(t1, t2, s1_ref, c1_ref[...], frames + 4, -2)
    layer(t2, t3, s2_ref, c2_ref[...], frames + 2, -1)
    own[0] = jnp.zeros(own.shape[1:], F32)
    own[rows + 1] = jnp.zeros(own.shape[1:], F32)
    for y in range(0, rows, 2):
        places = [split(own3, far3)(j) for j in range(frames + 2)]
        z = jnp.concatenate([ref[at, :, (y + 1) * LANES : (y + 3) * LANES] for ref, at in places], axis=0)
        acc = jnp.dot(head_ref[...], z, preferred_element_type=F32)
        own[y + 1], own[y + 2] = acc[:, tile(0)], acc[:, tile(1)]
    z = jnp.concatenate([t3[j] for j in range(frames + 2)], axis=0)
    acc = jnp.dot(head_ref[...], z, preferred_element_type=F32)
    ends[0], ends[1] = acc[:, tile(0)], acc[:, tile(1)]
    offsets = [pl.ds(dy, frames, stride=3) for dy in range(3)]
    west, east = (three_rows(*(ends[half, at] for at in offsets)) for half in range(2))
    days = part_ref.shape[0]
    day = day_ref[...]
    for y in range(rows):
        v = patched(sum(own[y + dy, offsets[dy]] for dy in range(3)), west, east, y)
        for d in range(days):
            part_ref[d, y : y + 1, :] = jnp.sum(jnp.where(day == d, v, 0.0), axis=0, keepdims=True)
    base = c3_ref[0:1, 0:1]
    for d in range(days):
        total = 0.5 * part_ref[d]
        for f in range(frames):
            total = total + jnp.where(day[f : f + 1] == d, state_ref[f, 0].astype(F32) + 0.5 * base, 0.0)
        part_ref[d] = total


def make_side(own3, far3, west, east, first, second, s1, s2, head, c1, c2, c3, state, day, days):
    frames, fields, rows, _ = state.shape
    chans, hid = west.shape[1], c1.shape[0]
    return call(
        side_kernel,
        "side",
        (shape_of((frames + 2, 3 * hid, 2 * LANES), BF), shape_of((days, rows, LANES), F32)),
        [VMEM] * 14,
        [
            pltpu.VMEM((frames + 6, 3 * chans, 2 * LANES), BF),
            pltpu.VMEM((frames + 4, 3 * hid, 2 * LANES), BF),
            pltpu.VMEM((rows + 2, head.shape[0], LANES), F32),
            pltpu.VMEM((2, head.shape[0], LANES), F32),
        ],
    )(own3, far3, west, east, first, second, s1, s2, head, c1, c2, c3, state, day)


def own_score(own3, far3, m3_ref, frames, y):
    acc = jnp.dot(m3_ref[...], window(split(own3, far3), range(frames + 2), y), preferred_element_type=F32)
    return acc[:, tile(0)], acc[:, tile(1)]


def update_kernel(
    own3, far3, t3, m3_ref, s3_ref, c3_ref, state_ref, noise_ref, out_ref, head_ref, side, scr
):
    frames, fields, rows, _ = state_ref.shape
    z = jnp.concatenate([t3[j] for j in range(frames + 2)], axis=0)
    acc = jnp.dot(s3_ref[...], z, preferred_element_type=F32)
    for f in range(frames):
        both = over_rows(acc, f * 3 * fields, fields)
        for half in range(2):
            side[half, f * fields : (f + 1) * fields] = both[:, tile(half)]
    bias = c3_ref[...]
    for y in range(0, rows, 2):
        both = own_score(own3, far3, m3_ref, frames, y)
        for f in range(frames):
            at = slice(f * fields, (f + 1) * fields)
            west, east = side[0, at], side[1, at]
            for i in range(2):
                scr[f, pl.ds(y + i, fields, stride=rows), :] = patched(both[i][at], west, east, y + i) + bias
    for f in range(frames):
        score = scr[f].reshape(fields, rows, LANES)
        moved = state_ref[f].astype(F32) + 0.8 * score + 0.5 * noise_ref[f].astype(F32)
        out_ref[f] = moved.astype(BF)
        head_ref[f] = moved[0]


def make_update(own3, far3, t3, m3, s3, c3, state, noise):
    frames, fields, rows, _ = state.shape
    return call(
        update_kernel,
        "update",
        (shape_of(state.shape, BF), shape_of((frames, rows, LANES), F32)),
        [VMEM] * 8,
        [
            pltpu.VMEM((2, frames * fields, LANES), F32),
            pltpu.VMEM((frames, fields * rows, LANES), F32),
        ],
        cost=3_000_000_000,
    )(own3, far3, t3, m3, s3, c3, state, noise)


def correct_kernel(count, *refs):
    parts = refs[:count]
    observed_ref, mask_ref, head_ref, day_ref, body_ref, out_ref, buf, sems = refs[count:]
    frames = head_ref.shape[0]
    others = pltpu.make_async_copy(body_ref.at[:, 1:], out_ref.at[:, 1:], sems.at[0])
    others.start()
    days = observed_ref.shape[0]
    mask = mask_ref[...].astype(F32)
    misfit = [0.15 * (mask * (sum(p[d] for p in parts) - observed_ref[d])) for d in range(days)]
    for f in range(frames):
        v = head_ref[f]
        for d in range(days):
            v = v - jnp.where(day_ref[f : f + 1] == d, misfit[d], 0.0)
        buf[f, 0] = v.astype(BF)
    first = pltpu.make_async_copy(buf, out_ref.at[:, 0:1], sems.at[1])
    first.start()
    others.wait()
    first.wait()


def make_correct(parts, observed, mask, head, day, out):
    frames, rows, _ = head.shape
    return call(
        functools.partial(correct_kernel, len(parts)),
        "correct",
        (shape_of(out.shape, BF),),
        [VMEM] * (len(parts) + 5),
        [pltpu.VMEM((frames, 1, rows, LANES), BF), pltpu.SemaphoreType.DMA((2,))],
        out_specs=(ANYWHERE,),
    )(*parts, observed, mask, head, day, out)[0]


def swapped(value, axis, start):
    sizes = {name: lax.axis_size(name) for name in ("tm", "space")}
    other = "space" if axis == "tm" else "tm"
    pairs = []
    for t in range(sizes["tm"]):
        for s in range(sizes["space"]):
            to = {"tm": t, "space": s}
            to[axis] += 1 if to[axis] % 2 == start else -1
            if not 0 <= to[axis] < sizes[axis]:
                to = {"tm": t, "space": s}
                to[other] ^= 1
            pairs.append((t * sizes["space"] + s, to["tm"] * sizes["space"] + to["space"]))
    return lax.ppermute(value, ("tm", "space"), pairs)


def totals_of(mine):
    count = lax.axis_size("tm")

    def partner(value, bits):
        return lax.ppermute(value, "tm", [(i, i ^ bits) for i in range(count)])

    if count & (count - 1):
        return [lax.psum(mine, "tm")]
    far = count // 2
    while far > 2:
        mine = mine + partner(mine, far)
        far //= 2
    return [partner(mine, bits) for bits in (1, 3, 2) if bits < count] + [mine]


def body(
    state, noise, conv_one, bias_one, conv_two, bias_two, conv_three, bias_three, day_of_frame, observed, obs_mask
):
    state, noise = state[:, :, 0], noise[:, :, 0]
    hid, chans = conv_one.shape[:2]
    fields = conv_three.shape[0]
    w1 = conv_one.transpose(2, 3, 4, 1, 0).reshape(27 * chans, hid)
    w2 = conv_two.transpose(2, 3, 4, 0, 1).reshape(27, hid, hid)
    w3 = conv_three.transpose(2, 3, 4, 0, 1).reshape(27, fields, hid)
    own, send2, send1 = make_rows(state)
    far = swapped(send2, "tm", 1)
    near = swapped(send1, "tm", 0)
    small = jnp.concatenate([bias_one, bias_two, bias_three, day_of_frame.astype(F32)])[None]
    m1, m2, m3, s1, s2, s3, c1, c2, c3, days, head = make_weights(w1, w2, w3, small, state.shape[0])
    own1, own2, own3, west, east = make_inner(own, m1, m2, c1, c2)
    west, east, send1, send2 = make_edges(west, east, near, far)
    first, second = swapped(send1, "space", 0), swapped(send2, "space", 1)
    far3 = make_main(own1, own2, near, far, m1, m2, c1, c2)
    t3, mine = make_side(
        own3, far3, west, east, first, second, s1, s2, head, c1, c2, c3, state, days, observed.shape[0]
    )
    out, head0 = make_update(own3, far3, t3, m3, s3, c3, state, noise)
    parts = totals_of(mine)
    out = make_correct(parts, observed[:, 0], obs_mask[0], head0, days, out)
    return out[:, :, None]


def solution(mesh):
    in_specs = (
        P("tm", None, "space", None, None),
        P("tm", None, "space", None, None),
        P(),
        P(),
        P(),
        P(),
        P(),
        P(),
        P("tm"),
        P(None, "space", None, None),
        P("space", None, None),
    )
    out_specs = P("tm", None, "space", None, None)
    return jax.shard_map(body, mesh=mesh, in_specs=in_specs, out_specs=out_specs, check_vma=False)
```

```python
import functools

import jax
import jax.numpy as jnp
from jax import lax
from jax.experimental import pallas as pl
from jax.experimental.pallas import tpu as pltpu
from jax.sharding import PartitionSpec as P

BF = jnp.bfloat16
F32 = jnp.float32
LANES = 128
DEPTH = 3
PITCH = 16
VMEM = pl.BlockSpec(memory_space=pltpu.VMEM)
ANYWHERE = pl.BlockSpec(memory_space=pltpu.HBM)
LIMIT = 24 * 1024 * 1024


def shape_of(dims, kind):
    return jax.ShapeDtypeStruct(dims, kind)


def call(kernel, name, outs, specs, scratch=(), cost=None, alias=None, out_specs=None):
    return pl.pallas_call(
        kernel,
        out_shape=outs,
        in_specs=specs,
        out_specs=out_specs or (VMEM,) * len(outs),
        scratch_shapes=list(scratch),
        input_output_aliases=alias or {},
        compiler_params=pltpu.CompilerParams(vmem_limit_bytes=LIMIT),
        cost_estimate=cost and pl.CostEstimate(flops=cost, bytes_accessed=1_000_000, transcendentals=0),
        name=name,
    )


def silu(v):
    half = 0.5 * v
    return half + half * jnp.tanh(half)


def lanes(shape):
    return lax.broadcasted_iota(jnp.int32, shape, len(shape) - 1)


def turn(v, steps):
    steps = steps % LANES
    return pltpu.roll(v, steps, 1) if steps else v


def tile(i):
    return slice(i * LANES, (i + 1) * LANES)


def is_even(axis):
    return lax.axis_index(axis) % 2 == 0


def rows_kernel(state_ref, own_ref, far_ref, near_ref, raw, scr, sems):
    frames, chans, rows, _ = state_ref.shape
    copies = [pltpu.make_async_copy(state_ref.at[f], raw.at[f], sems.at[f]) for f in range(frames)]
    for c in copies:
        c.start()
    for f in range(frames):
        copies[f].wait()
        scr[f] = raw[f].astype(F32).reshape(chans * rows, LANES)
        for y in range(rows):
            v = scr[f, pl.ds(y, chans, stride=rows), :].astype(BF)
            own_ref[f, :, tile(y)] = v
    even = is_even("tm")
    for f in range(DEPTH):
        low, high = own_ref[f], own_ref[frames - DEPTH + f]
        near_ref[f], far_ref[f] = jnp.where(even, high, low), jnp.where(even, low, high)


def make_rows(state):
    frames, chans, rows, _ = state.shape
    slab = shape_of((DEPTH, chans, rows * LANES), BF)
    return call(
        rows_kernel,
        "rows",
        (shape_of((frames, chans, rows * LANES), BF), slab, slab),
        [ANYWHERE],
        [
            pltpu.VMEM(state.shape, BF),
            pltpu.VMEM((frames, chans * rows, LANES), F32),
            pltpu.SemaphoreType.DMA((frames,)),
        ],
        cost=4_000_000_000,
    )(pltpu.with_memory_space_constraint(state, pltpu.HBM))


def weights_kernel(
    w1_ref, w2_ref, w3_ref, small_ref,
    m1_ref, m2_ref, m3_ref, s1_ref, s2_ref, s3_ref, c1_ref, c2_ref, c3_ref, days_ref, head_ref, f2, f3,
):
    small = jnp.broadcast_to(small_ref[...], (8, small_ref.shape[1])).T[:, 0:1]
    at = 0
    for ref in (c1_ref, c2_ref, c3_ref, days_ref):
        ref[...] = jnp.broadcast_to(small[at : at + ref.shape[0]], ref.shape)
        at += ref.shape[0]
    for ref in (m1_ref, m2_ref, m3_ref, s1_ref, s2_ref, s3_ref):
        ref[...] = jnp.zeros_like(ref)
    hid, fields, chans = w2_ref.shape[1], w3_ref.shape[1], w1_ref.shape[0] // 27
    frames = days_ref.shape[0]
    flat = w1_ref[...].astype(F32).T.astype(BF)
    for p in range(2):
        m1_ref[p * hid : (p + 1) * hid, p * 9 * chans : (p + 3) * 9 * chans] = flat
        for dt in range(3):
            for dy in range(3):
                at = (dt * 3 + dy) * 3 * chans
                s1_ref[(p * 3 + dy) * hid : (p * 3 + dy + 1) * hid, (dt + p) * 3 * chans : (dt + p + 1) * 3 * chans] = (
                    flat[:, at : at + 3 * chans]
                )

    def place(raw, flat, main, side, count, outs):
        half = LANES // 2
        for t in range(27):
            for k in range(2):
                flat[k, :, t * hid + k * half : (t + 1) * hid + k * half] = raw[t]
        for p in range(count):
            rows, at = slice(p * outs, (p + 1) * outs), p * 9 * hid
            k = at % LANES // half
            main[rows, at : at + 27 * hid] = flat[k, :, k * half : k * half + 27 * hid]
            for dt in range(3):
                for dy in range(3):
                    rows = slice((p * 3 + dy) * outs, (p * 3 + dy + 1) * outs)
                    at, src = (dt + p) * 3 * hid, (dt * 3 + dy) * 3 * hid
                    k = (at - src) % LANES // half
                    side[rows, at : at + 3 * hid] = flat[k, :, src + k * half : src + k * half + 3 * hid]

    place(w2_ref, f2, m2_ref, s2_ref, 2, hid)
    place(w3_ref, f3, m3_ref, s3_ref, frames, fields)
    shape = (head_ref.shape[0], s3_ref.shape[0])
    pick = lanes(shape) == fields * lax.broadcasted_iota(jnp.int32, shape, 0)
    head_ref[...] = jnp.dot(pick.astype(F32).astype(BF), s3_ref[...], preferred_element_type=F32).astype(BF)


def make_weights(w1, w2, w3, small, frames):
    hid, fields, chans = w2.shape[1], w3.shape[1], w1.shape[0] // 27
    return call(
        weights_kernel,
        "weights",
        (
            shape_of((2 * hid, 4 * 9 * chans), BF),
            shape_of((2 * hid, 4 * 9 * hid), BF),
            shape_of((frames * fields, (frames + 2) * 9 * hid), BF),
            shape_of((6 * hid, 4 * 3 * chans), BF),
            shape_of((6 * hid, 4 * 3 * hid), BF),
            shape_of((frames * 3 * fields, (frames + 2) * 3 * hid), BF),
            shape_of((hid, 1), F32),
            shape_of((hid, 1), F32),
            shape_of((fields, 1), F32),
            shape_of((frames, LANES), F32),
            shape_of((-(-3 * frames // 16) * 16, (frames + 2) * 3 * hid), BF),
        ),
        [VMEM] * 4,
        [pltpu.VMEM((2, w.shape[1], 27 * hid + LANES // 2), BF) for w in (w2, w3)],
        cost=1_000_000_000,
    )(w1, w2, w3, small)


def beside(near_ref, far_ref):
    step, last = lax.axis_index("tm"), lax.axis_size("tm") - 1
    even = is_even("tm")
    for f in range(DEPTH):
        for y in range(near_ref.shape[2] // LANES):
            a, b = near_ref[f, :, tile(y)], far_ref[f, :, tile(y)]
            none = jnp.zeros_like(a)
            yield f, y, jnp.where(step > 0, jnp.where(even, b, a), none)
            yield DEPTH + f, y, jnp.where(step < last, jnp.where(even, a, b), none)


def strips(rows_of_frames, count):
    begun = {}
    for f, y, v in rows_of_frames:
        lane = lanes(v.shape)
        group, place = lane // PITCH, lane % PITCH
        west, east = begun.pop(f, (jnp.zeros_like(v), jnp.zeros_like(v)))
        here = group == y
        west = jnp.where(here & (place >= DEPTH), turn(v, y * PITCH + DEPTH), west)
        east = jnp.where(here & (place < PITCH - DEPTH), turn(v, y * PITCH + PITCH - DEPTH), east)
        if y == count - 1:
            yield f, west, east
        else:
            begun[f] = west, east


def edges_kernel(own_west_ref, own_east_ref, far_ref, near_ref, west_ref, east_ref, send1_ref, send2_ref):
    frames = own_west_ref.shape[0]
    even = is_even("space")

    def put(f, west, east):
        west_ref[f], east_ref[f] = west, east
        send1_ref[f], send2_ref[f] = jnp.where(even, east, west), jnp.where(even, west, east)

    for f in range(frames):
        put(DEPTH + f, own_west_ref[f], own_east_ref[f])
    for f, west, east in strips(beside(near_ref, far_ref), near_ref.shape[2] // LANES):
        put(f if f < DEPTH else f + frames, west, east)


def make_edges(own_west, own_east, near, far):
    frames, chans, _ = own_west.shape
    strip = shape_of((frames + 2 * DEPTH, chans, LANES), BF)
    return call(edges_kernel, "edges", (strip,) * 4, [VMEM] * 4)(own_west, own_east, far, near)


def spread(dst, f, y, v):
    chans = v.shape[0]
    at = tile(y + 1)
    dst[f, 0:chans, at] = turn(v, 1)
    dst[f, chans : 2 * chans, at] = v
    dst[f, 2 * chans : 3 * chans, at] = turn(v, -1)


def window(src, frames, y):
    parts = []
    for f in frames:
        ref, at = src(f)
        for dy in range(3):
            parts.append(ref[at, :, (y + dy) * LANES : (y + dy + 2) * LANES])
    return jnp.concatenate(parts, axis=0)


def plain(ref):
    return lambda f: (ref, f)


def split(own, far, count=None):
    count = own.shape[0] if count is None else count
    return lambda f: (own, f - DEPTH) if DEPTH <= f < DEPTH + count else (far, f if f < DEPTH else f - count)


def in_trajectory(local, frames):
    step = lax.axis_index("tm") * frames + local
    return (step >= 0) & (step < frames * lax.axis_size("tm"))


def blank_ends(*refs):
    for s in refs:
        s[:, :, tile(0)] = jnp.zeros(s.shape[:2] + (LANES,), BF)
        last = s.shape[2] // LANES - 1
        s[:, :, tile(last)] = jnp.zeros(s.shape[:2] + (LANES,), BF)


def layer(src, dst, m_ref, c_ref, groups, rows, keep):
    hid = c_ref.shape[0]
    for f, count in groups:
        weights = m_ref[...] if count == 2 else m_ref[0:hid, 0 : m_ref.shape[1] // 4 * 3]
        for y in range(0, rows, 2):
            acc = jnp.dot(weights, window(src, range(f, f + count + 2), y), preferred_element_type=F32)
            for p in range(count):
                h = silu(acc[p * hid : (p + 1) * hid] + c_ref[...]).astype(BF)
                inside = keep(f + p)
                h = h if inside is None else jnp.where(inside, h, jnp.zeros_like(h))
                ref, at = dst(f + p)
                spread(ref, at, y, h[:, tile(0)])
                spread(ref, at, y + 1, h[:, tile(1)])


def pairs_of(frames):
    groups = [(f, 2) for f in range(frames[0], frames[-1], 2)]
    return groups + [(frames[-1], 1)] * (len(frames) % 2)


def inner_kernel(own_ref, m1_ref, m2_ref, c1_ref, c2_ref, s1, s2, s3, west_ref, east_ref):
    frames = own_ref.shape[0]
    rows = own_ref.shape[2] // LANES
    each = [(f, y, own_ref[f, :, tile(y)]) for f in range(frames) for y in range(rows)]
    blank_ends(s1, s2, s3)
    for f, y, v in each:
        spread(s1, f, y, v)
    for f, west, east in strips(each, rows):
        west_ref[f], east_ref[f] = west, east
    layer(plain(s1), plain(s2), m1_ref, c1_ref, pairs_of(range(frames - 2)), rows, lambda f: None)
    layer(plain(s2), plain(s3), m2_ref, c2_ref, pairs_of(range(frames - 4)), rows, lambda f: None)


def make_inner(own, m1, m2, c1, c2):
    frames, chans, width = own.shape
    hid, wide = c1.shape[0], width + 2 * LANES
    strip = shape_of((frames, chans, LANES), BF)
    return call(
        inner_kernel,
        "inner",
        (
            shape_of((frames, 3 * chans, wide), BF),
            shape_of((frames - 2, 3 * hid, wide), BF),
            shape_of((frames - 4, 3 * hid, wide), BF),
            strip,
            strip,
        ),
        [VMEM] * 5,
        cost=1_500_000_000,
    )(own, m1, m2, c1, c2)


def main_kernel(own1, own2, far_ref, near_ref, m1_ref, m2_ref, c1_ref, c2_ref, s3, far1, far2):
    frames = own1.shape[0]
    rows = near_ref.shape[2] // LANES
    blank_ends(far1, far2, s3)
    for f, y, v in beside(near_ref, far_ref):
        spread(far1, f, y, v)

    one, two, three = split(own1, far1), split(own2, far2), split(None, s3, frames - 4)
    groups = pairs_of(range(DEPTH)) + pairs_of(range(frames + 1, frames + 4))
    layer(one, two, m1_ref, c1_ref, groups, rows, lambda f: in_trajectory(f - 2, frames))
    groups = pairs_of(range(DEPTH)) + pairs_of(range(frames - 1, frames + 2))
    layer(two, three, m2_ref, c2_ref, groups, rows, lambda f: in_trajectory(f - 1, frames))


def make_main(own1, own2, near, far, m1, m2, c1, c2):
    frames, rows1, wide = own1.shape
    rows2 = own2.shape[1]
    return call(
        main_kernel,
        "main",
        (shape_of((2 * DEPTH, rows2, wide), BF),),
        [VMEM] * 8,
        [pltpu.VMEM((2 * DEPTH, rows1, wide), BF), pltpu.VMEM((2 * DEPTH, rows2, wide), BF)],
        cost=5_000_000_000,
    )(own1, own2, far, near, m1, m2, c1, c2)[0]


def spread_side(dst, f, v):
    chans = v.shape[0]
    for half in range(2):
        w = v[:, tile(half)]
        dst[f, 0:chans, tile(half)] = turn(w, 1)
        dst[f, chans : 2 * chans, tile(half)] = w
        dst[f, 2 * chans : 3 * chans, tile(half)] = turn(w, -1)


def three_rows(up, mid, down):
    lane = lanes(mid.shape)
    up = jnp.where(lane >= PITCH, turn(up, PITCH), 0.0)
    down = jnp.where(lane < LANES - PITCH, turn(down, -PITCH), 0.0)
    return mid + up + down


def over_rows(acc, at, outs):
    halves = []
    for half in range(2):
        up, mid, down = (acc[at + d * outs : at + (d + 1) * outs, tile(half)] for d in range(3))
        halves.append(three_rows(up, mid, down))
    return jnp.concatenate(halves, axis=1)


def patched(v, west, east, y):
    col = lanes(v.shape)
    v = jnp.where(col < DEPTH, turn(west, -(y * PITCH + DEPTH)), v)
    return jnp.where(col >= LANES - DEPTH, turn(east, DEPTH - (y + 1) * PITCH), v)


def side_kernel(
    own3, far3, west_ref, east_ref, first_ref, second_ref, s1_ref, s2_ref, head_ref, c1_ref, c2_ref, c3_ref,
    state_ref, day_ref, t3, part_ref, t1, t2, own, ends,
):
    frames, fields, rows, _ = state_ref.shape
    chans, hid = west_ref.shape[1], c1_ref.shape[0]
    place = lanes((chans, LANES)) % PITCH
    even = is_even("space")
    me, last = lax.axis_index("space"), lax.axis_size("space") - 1
    none = jnp.zeros((chans, LANES), BF)
    for f in range(frames + 2 * DEPTH):
        a, b = first_ref[f], second_ref[f]
        a, b = jnp.where(even, b, a), jnp.where(even, a, b)
        a, b = jnp.where(me > 0, a, none), jnp.where(me < last, b, none)
        west = jnp.where(place < DEPTH, turn(a, 2 * DEPTH - PITCH), west_ref[f])
        east = jnp.where(place >= PITCH - DEPTH, turn(b, PITCH - 2 * DEPTH), east_ref[f])
        spread_side(t1, f, jnp.concatenate([west, east], axis=1))

    pair = lanes((1, 2 * LANES))
    place = pair % PITCH
    outside = ((pair < LANES) & (place < DEPTH) & (me == 0)) | (
        (pair >= LANES) & (place >= PITCH - DEPTH) & (me == last)
    )

    def layer(src, dst, m_ref, bias, count, first):
        for f in range(0, count, 2):
            z = jnp.concatenate([src[f + j] for j in range(4)], axis=0)
            for p in range(2):
                acc = jnp.dot(m_ref[p * 3 * hid : (p + 1) * 3 * hid], z, preferred_element_type=F32)
                h = silu(over_rows(acc, 0, hid) + bias)
                keep = in_trajectory(f + p + first, frames) & ~outside
                spread_side(dst, f + p, jnp.where(keep, h, 0.0).astype(BF))

    layer(t1, t2, s1_ref, c1_ref[...], frames + 4, -2)
    layer(t2, t3, s2_ref, c2_ref[...], frames + 2, -1)
    own[0] = jnp.zeros(own.shape[1:], F32)
    own[rows + 1] = jnp.zeros(own.shape[1:], F32)
    for y in range(0, rows, 2):
        places = [split(own3, far3)(j) for j in range(frames + 2)]
        z = jnp.concatenate([ref[at, :, (y + 1) * LANES : (y + 3) * LANES] for ref, at in places], axis=0)
        acc = jnp.dot(head_ref[...], z, preferred_element_type=F32)
        own[y + 1], own[y + 2] = acc[:, tile(0)], acc[:, tile(1)]
    z = jnp.concatenate([t3[j] for j in range(frames + 2)], axis=0)
    acc = jnp.dot(head_ref[...], z, preferred_element_type=F32)
    ends[0], ends[1] = acc[:, tile(0)], acc[:, tile(1)]
    offsets = [pl.ds(dy, frames, stride=3) for dy in range(3)]
    west, east = (three_rows(*(ends[half, at] for at in offsets)) for half in range(2))
    days = part_ref.shape[0]
    day = day_ref[...]
    for y in range(rows):
        v = patched(sum(own[y + dy, offsets[dy]] for dy in range(3)), west, east, y)
        for d in range(days):
            part_ref[d, y : y + 1, :] = jnp.sum(jnp.where(day == d, v, 0.0), axis=0, keepdims=True)
    base = c3_ref[0:1, 0:1]
    for d in range(days):
        total = 0.5 * part_ref[d]
        for f in range(frames):
            total = total + jnp.where(day[f : f + 1] == d, state_ref[f, 0].astype(F32) + 0.5 * base, 0.0)
        part_ref[d] = total


def make_side(own3, far3, west, east, first, second, s1, s2, head, c1, c2, c3, state, day, days):
    frames, fields, rows, _ = state.shape
    chans, hid = west.shape[1], c1.shape[0]
    return call(
        side_kernel,
        "side",
        (shape_of((frames + 2, 3 * hid, 2 * LANES), BF), shape_of((days, rows, LANES), F32)),
        [VMEM] * 14,
        [
            pltpu.VMEM((frames + 6, 3 * chans, 2 * LANES), BF),
            pltpu.VMEM((frames + 4, 3 * hid, 2 * LANES), BF),
            pltpu.VMEM((rows + 2, head.shape[0], LANES), F32),
            pltpu.VMEM((2, head.shape[0], LANES), F32),
        ],
    )(own3, far3, west, east, first, second, s1, s2, head, c1, c2, c3, state, day)


def own_score(own3, far3, m3_ref, frames, y):
    acc = jnp.dot(m3_ref[...], window(split(own3, far3), range(frames + 2), y), preferred_element_type=F32)
    return acc[:, tile(0)], acc[:, tile(1)]


def update_kernel(
    own3, far3, t3, m3_ref, s3_ref, c3_ref, state_ref, noise_ref, out_ref, head_ref, side, scr
):
    frames, fields, rows, _ = state_ref.shape
    z = jnp.concatenate([t3[j] for j in range(frames + 2)], axis=0)
    acc = jnp.dot(s3_ref[...], z, preferred_element_type=F32)
    for f in range(frames):
        both = over_rows(acc, f * 3 * fields, fields)
        for half in range(2):
            side[half, f * fields : (f + 1) * fields] = both[:, tile(half)]
    bias = c3_ref[...]
    for y in range(0, rows, 2):
        both = own_score(own3, far3, m3_ref, frames, y)
        for f in range(frames):
            at = slice(f * fields, (f + 1) * fields)
            west, east = side[0, at], side[1, at]
            for i in range(2):
                scr[f, pl.ds(y + i, fields, stride=rows), :] = patched(both[i][at], west, east, y + i) + bias
    for f in range(frames):
        score = scr[f].reshape(fields, rows, LANES)
        moved = state_ref[f].astype(F32) + 0.8 * score + 0.5 * noise_ref[f].astype(F32)
        out_ref[f] = moved.astype(BF)
        head_ref[f] = moved[0]


def make_update(own3, far3, t3, m3, s3, c3, state, noise):
    frames, fields, rows, _ = state.shape
    return call(
        update_kernel,
        "update",
        (shape_of(state.shape, BF), shape_of((frames, rows, LANES), F32)),
        [VMEM] * 8,
        [
            pltpu.VMEM((2, frames * fields, LANES), F32),
            pltpu.VMEM((frames, fields * rows, LANES), F32),
        ],
        cost=3_000_000_000,
    )(own3, far3, t3, m3, s3, c3, state, noise)


def correct_kernel(count, *refs):
    parts = refs[:count]
    observed_ref, mask_ref, head_ref, day_ref, body_ref, out_ref, buf, sems = refs[count:]
    frames = head_ref.shape[0]
    others = pltpu.make_async_copy(body_ref.at[:, 1:], out_ref.at[:, 1:], sems.at[0])
    others.start()
    days = observed_ref.shape[0]
    mask = mask_ref[...].astype(F32)
    misfit = [0.15 * (mask * (sum(p[d] for p in parts) - observed_ref[d])) for d in range(days)]
    for f in range(frames):
        v = head_ref[f]
        for d in range(days):
            v = v - jnp.where(day_ref[f : f + 1] == d, misfit[d], 0.0)
        buf[f, 0] = v.astype(BF)
    first = pltpu.make_async_copy(buf, out_ref.at[:, 0:1], sems.at[1])
    first.start()
    others.wait()
    first.wait()


def make_correct(parts, observed, mask, head, day, out):
    frames, rows, _ = head.shape
    return call(
        functools.partial(correct_kernel, len(parts)),
        "correct",
        (shape_of(out.shape, BF),),
        [VMEM] * (len(parts) + 5),
        [pltpu.VMEM((frames, 1, rows, LANES), BF), pltpu.SemaphoreType.DMA((2,))],
        out_specs=(ANYWHERE,),
    )(*parts, observed, mask, head, day, out)[0]


def swapped(value, axis, start):
    sizes = {name: lax.axis_size(name) for name in ("tm", "space")}
    other = "space" if axis == "tm" else "tm"
    pairs = []
    for t in range(sizes["tm"]):
        for s in range(sizes["space"]):
            to = {"tm": t, "space": s}
            to[axis] += 1 if to[axis] % 2 == start else -1
            if not 0 <= to[axis] < sizes[axis]:
                to = {"tm": t, "space": s}
                to[other] ^= 1
            pairs.append((t * sizes["space"] + s, to["tm"] * sizes["space"] + to["space"]))
    return lax.ppermute(value, ("tm", "space"), pairs)


def totals_of(mine):
    count = lax.axis_size("tm")

    def partner(value, bits):
        return lax.ppermute(value, "tm", [(i, i ^ bits) for i in range(count)])

    if count & (count - 1):
        return [lax.psum(mine, "tm")]
    far = count // 2
    while far > 2:
        mine = mine + partner(mine, far)
        far //= 2
    return [partner(mine, bits) for bits in (1, 3, 2) if bits < count] + [mine]


def body(
    state, noise, conv_one, bias_one, conv_two, bias_two, conv_three, bias_three, day_of_frame, observed, obs_mask
):
    state, noise = state[:, :, 0], noise[:, :, 0]
    hid, chans = conv_one.shape[:2]
    fields = conv_three.shape[0]
    w1 = conv_one.transpose(2, 3, 4, 1, 0).reshape(27 * chans, hid)
    w2 = conv_two.transpose(2, 3, 4, 0, 1).reshape(27, hid, hid)
    w3 = conv_three.transpose(2, 3, 4, 0, 1).reshape(27, fields, hid)
    own, send2, send1 = make_rows(state)
    far = swapped(send2, "tm", 1)
    near = swapped(send1, "tm", 0)
    small = jnp.concatenate([bias_one, bias_two, bias_three, day_of_frame.astype(F32)])[None]
    m1, m2, m3, s1, s2, s3, c1, c2, c3, days, head = make_weights(w1, w2, w3, small, state.shape[0])
    own1, own2, own3, west, east = make_inner(own, m1, m2, c1, c2)
    west, east, send1, send2 = make_edges(west, east, near, far)
    first, second = swapped(send1, "space", 0), swapped(send2, "space", 1)
    far3 = make_main(own1, own2, near, far, m1, m2, c1, c2)
    t3, mine = make_side(
        own3, far3, west, east, first, second, s1, s2, head, c1, c2, c3, state, days, observed.shape[0]
    )
    out, head0 = make_update(own3, far3, t3, m3, s3, c3, state, noise)
    parts = totals_of(mine)
    out = make_correct(parts, observed[:, 0], obs_mask[0], head0, days, out)
    return out[:, :, None]


def solution(mesh):
    in_specs = (
        P("tm", None, "space", None, None),
        P("tm", None, "space", None, None),
        P(),
        P(),
        P(),
        P(),
        P(),
        P(),
        P("tm"),
        P(None, "space", None, None),
        P("space", None, None),
    )
    out_specs = P("tm", None, "space", None, None)
    return jax.shard_map(body, mesh=mesh, in_specs=in_specs, out_specs=out_specs, check_vma=False)
```
